32 devices in a mesh: bucket: 2 (over core), frame: 8 (over z, y), seq: 2 (over x).
Axes of the slice: x: 2, y: 2, z: 4, core: 2. Of those that a mesh axis runs over, the one named last changes fastest.
Arguments:
- latent: bfloat16 [2, 16, 1024, 1152], P('bucket', 'frame', 'seq'), may hold values from -6 to 6
- condition: bfloat16 [2, 1152], P('bucket'), may hold values from -6 to 6
- text: bfloat16 [2, 128, 4096], P('bucket'), may hold values from -6 to 6
- text_len: int32 [2], P('bucket'), may hold values from 16 to 128, as said below
- clip_ids: int32 [2, 16], P('bucket'), may hold values from 0 to 8, as said below
- video_flag: int32 [2, 16], P('bucket'), may hold values from 0 to 1, as said below
- ada_weight: bfloat16 [1152, 10368], P(None, ('frame', 'seq')), may hold values from -0.1875 to 0.1875
- text_kv_weight: bfloat16 [4096, 2304], P(None, ('frame', 'seq')), may hold values from -0.09375 to 0.09375
- qkv_weight: bfloat16 [1152, 3456], P(('frame', 'seq')), may hold values from -0.1875 to 0.1875
- proj_weight: bfloat16 [1152, 1152], P(('frame', 'seq')), may hold values from -0.75 to 0.75
- cross_q_weight: bfloat16 [1152, 1152], P(('frame', 'seq')), may hold values from -0.125 to 0.125
- cross_proj_weight: bfloat16 [1152, 1152], P(('frame', 'seq')), may hold values from -0.5 to 0.5
- up_weight: bfloat16 [1152, 4608], P(('frame', 'seq')), may hold values from -0.1875 to 0.1875
- down_weight: bfloat16 [4608, 1152], P(('frame', 'seq')), may hold values from -0.09375 to 0.09375
- temporal_qkv_weight: bfloat16 [1152, 3456], P(('frame', 'seq')), may hold values from -0.1875 to 0.1875
- temporal_proj_weight: bfloat16 [1152, 1152], P(('frame', 'seq')), may hold values from -0.25 to 0.25
- cotangent: bfloat16 [2, 16, 1024, 1152], P('bucket', 'frame', 'seq'), may hold values from -6 to 6
Outputs:
- result: bfloat16 [2, 16, 1024, 1152], P('bucket', 'frame', 'seq')
- latent_grad: float32 [2, 16, 1024, 1152], P('bucket', 'frame', 'seq')
- ada_grad: float32 [1152, 10368], P(None, ('frame', 'seq'))
- text_kv_grad: float32 [4096, 2304], P(None, ('frame', 'seq'))
- qkv_grad: float32 [1152, 3456], P(('frame', 'seq'))
- proj_grad: float32 [1152, 1152], P(('frame', 'seq'))
- cross_q_grad: float32 [1152, 1152], P(('frame', 'seq'))
- cross_proj_grad: float32 [1152, 1152], P(('frame', 'seq'))
- up_grad: float32 [1152, 4608], P(('frame', 'seq'))
- down_grad: float32 [4608, 1152], P(('frame', 'seq'))
- temporal_qkv_grad: float32 [1152, 3456], P(('frame', 'seq'))
- temporal_proj_grad: float32 [1152, 1152], P(('frame', 'seq'))
The draws below stay inside these ranges and needn't reach their ends.
Inputs may be any that keep to these rules, and one draw needn't show every extreme that they name: `clip_ids`: in each bucket, clip ids start at 0 and rise by one from clip to clip along the frames; a video is 8 consecutive frames sharing one id, an image is one frame with an id of its own; half of a bucket's frames belong to videos. `video_flag`: 1 exactly on the frames of videos (clips of 8 frames). `text_len`: some bucket uses all 128 caption tokens.
All inputs are finite; a program needn't handle non-finite values.
Results may differ from the reference program's by a relative error of at most 0.025.
Values may be sent and summed in bfloat16 or wider, within the bound.
No kernel may reach another device: no remote copies, remote signals or barrier semaphores. Data moves between devices by JAX's collectives and lax.ppermute only.
A program may use at most 512 MiB of HBM per device.

```python
import math
import jax
import jax.numpy as jnp
from jax import lax

D = 1152
HEADS = 16
FF = 4608
TEXT_W = 4096
TEXT = 128
FRAME_TOK = 1024
CLIP = 8
FR_DEV = 2
HD = 72
BUCKETS = 2
FRAMES = 16


def unit_field(key, shape):
    values = jnp.clip(jax.random.normal(key, shape, jnp.float32), -6.0, 6.0)
    return values.astype(jnp.bfloat16)


def draw_latent(key, part):
    return unit_field(jax.random.fold_in(key, 31), (BUCKETS, FRAMES, FRAME_TOK, D))


def draw_condition(key, part):
    return unit_field(jax.random.fold_in(key, 37), (BUCKETS, D))


def draw_text(key, part):
    return unit_field(jax.random.fold_in(key, 41), (BUCKETS, TEXT, TEXT_W))


def clip_layout(key):
    video_count = FRAMES // (2 * CLIP)
    unit_count = video_count + FRAMES // 2
    base_key = jax.random.fold_in(key, 17)
    clip_rows = []
    flag_rows = []
    for bucket in range(BUCKETS):
        unit_order = jax.random.permutation(jax.random.fold_in(base_key, bucket), unit_count)
        is_video = unit_order < video_count
        repeats = jnp.where(is_video, CLIP, 1)
        clip_rows.append(jnp.repeat(jnp.arange(unit_count, dtype=jnp.int32), repeats, total_repeat_length=FRAMES))
        flag_rows.append(jnp.repeat(is_video.astype(jnp.int32), repeats, total_repeat_length=FRAMES))
    return (jnp.stack(clip_rows), jnp.stack(flag_rows))


def draw_clip_ids(key, part):
    return clip_layout(key)[0]


def draw_video_flag(key, part):
    return clip_layout(key)[1]


def draw_text_len(key, part):
    lengths = jax.random.randint(jax.random.fold_in(key, 3), (BUCKETS,), TEXT // 8, TEXT + 1)
    longest = jax.random.randint(jax.random.fold_in(key, 5), (), 0, BUCKETS)
    return jnp.where(jnp.arange(BUCKETS) == longest, TEXT, lengths).astype(jnp.int32)


def shard_levels(key, dims, shards, least, high):
    factor_of, own = 1.0, jax.random.fold_in(key, 6)
    for axis_at, parts in shards:
        draws = jnp.exp(jax.random.uniform(jax.random.fold_in(own, axis_at), (parts,), jnp.float32, least / len(shards), high / len(shards)))
        factor_of = factor_of * jnp.repeat(draws, dims[axis_at] // parts).reshape([-1 if axis == axis_at else 1 for axis in range(len(dims))])
    return factor_of


def scatter_about(rng, dims, scale, bound, shards=(), kind=jnp.bfloat16):
    factor_of = shard_levels(rng, dims, shards, -0.22, 0.18) if shards else 1.0
    values = jax.random.normal(rng, dims, jnp.float32) * scale * factor_of
    return jnp.minimum(jnp.maximum(values, -bound), bound).astype(kind)


def setup_inputs(seed: int = 0) -> dict:
    arg_keys = jax.random.split(jax.random.key(seed), 18)
    latent = draw_latent(jax.random.fold_in(arg_keys[17], 71), 0)
    condition = draw_condition(jax.random.fold_in(arg_keys[17], 71), 0)
    text = draw_text(jax.random.fold_in(arg_keys[17], 71), 0)
    text_len = draw_text_len(jax.random.fold_in(arg_keys[17], 71), 0)
    clip_ids = draw_clip_ids(jax.random.fold_in(arg_keys[17], 71), 0)
    video_flag = draw_video_flag(jax.random.fold_in(arg_keys[17], 71), 0)
    ada_weight = scatter_about(arg_keys[6], (D, 9 * D), D ** -0.5, 0.1875, ((1, 16),))
    text_kv_weight = scatter_about(arg_keys[7], (TEXT_W, 2 * D), TEXT_W ** -0.5, 0.09375, ((1, 16),))
    qkv_weight = scatter_about(arg_keys[8], (D, 3 * D), D ** -0.5, 0.1875, ((0, 16),))
    proj_weight = scatter_about(arg_keys[9], (D, D), (D // 16) ** -0.5, 0.75, ((0, 16),))
    cross_q_weight = scatter_about(arg_keys[10], (D, D), (2 * D) ** -0.5, 0.125, ((0, 16),))
    cross_proj_weight = scatter_about(arg_keys[11], (D, D), (D // 8) ** -0.5, 0.5, ((0, 16),))
    up_weight = scatter_about(arg_keys[12], (D, FF), D ** -0.5, 0.1875, ((0, 16),))
    down_weight = scatter_about(arg_keys[13], (FF, D), FF ** -0.5, 0.09375, ((0, 16),))
    temporal_qkv_weight = scatter_about(arg_keys[14], (D, 3 * D), D ** -0.5, 0.1875, ((0, 16),))
    temporal_proj_weight = scatter_about(arg_keys[15], (D, D), (D // 2) ** -0.5, 0.25, ((0, 16),))
    cotangent = scatter_about(arg_keys[16], (BUCKETS, FRAMES, FRAME_TOK, D), 1.0, 6.0, ((0, 2), (1, 8), (2, 2)))
    return {"latent": latent, "condition": condition, "text": text, "text_len": text_len, "clip_ids": clip_ids, "video_flag": video_flag, "ada_weight": ada_weight, "text_kv_weight": text_kv_weight, "qkv_weight": qkv_weight, "proj_weight": proj_weight, "cross_q_weight": cross_q_weight, "cross_proj_weight": cross_proj_weight, "up_weight": up_weight, "down_weight": down_weight, "temporal_qkv_weight": temporal_qkv_weight, "temporal_proj_weight": temporal_proj_weight, "cotangent": cotangent}


@jax.custom_vjp
def low(v):
    return lax.optimization_barrier(v.astype(jnp.bfloat16)).astype(jnp.float32)

@jax.custom_vjp
def low_back(v):
    return v

def low_keep(v):
    return (low(v), None)

def low_pass(kept, grad):
    return (grad,)

def back_keep(v):
    return (v, None)

def back_low(kept, grad):
    return (low(grad),)
low.defvjp(low_keep, low_pass)
low_back.defvjp(back_keep, back_low)
highest = lax.Precision.HIGHEST
epsilon = 1e-06
masked_fill = -1e+30

def matmul(left, right):
    return jnp.dot(left, right, precision=highest)

def normalize(values):
    centred = values - lax.optimization_barrier(jnp.mean(values, axis=-1, keepdims=True))
    return centred * lax.rsqrt(lax.optimization_barrier(jnp.mean(centred * centred, axis=-1, keepdims=True)) + epsilon)

def frame_group(group_rows, modulation, key_text, value_text, live_keys, weight_set):
    qkv_full, proj_full, cross_q_full, cross_proj_full, up_full, down_full = weight_set
    frames = group_rows.shape[0]
    score_scale = 1.0 / math.sqrt(HD)
    hidden_a = low(normalize(group_rows) * (1.0 + modulation[1]) + modulation[0])
    qkv_rows = low_back(low(matmul(hidden_a, qkv_full)))
    query_heads = qkv_rows[..., :D].reshape(frames, FRAME_TOK, HEADS, HD)
    key_heads = qkv_rows[..., D:2 * D].reshape(frames, FRAME_TOK, HEADS, HD)
    value_heads = qkv_rows[..., 2 * D:].reshape(frames, FRAME_TOK, HEADS, HD)
    scores = low_back(jnp.einsum('fqhe,fkhe->fqhk', query_heads, key_heads, precision=highest) * score_scale)
    prob_rows = jax.nn.softmax(scores, axis=-1)
    attended = low_back(low(jnp.einsum('fqhk,fkhe->fqhe', low(prob_rows), value_heads, precision=highest).reshape(frames, FRAME_TOK, D)))
    after_a = group_rows + modulation[2] * low_back(matmul(attended, proj_full))
    cross_query = low_back(low(matmul(low(after_a), cross_q_full))).reshape(frames, FRAME_TOK, HEADS, HD)
    cross_scores = low_back(jnp.einsum('fqhe,khe->fqhk', cross_query, key_text, precision=highest) * score_scale)
    cross_scores = jnp.where(live_keys, cross_scores, masked_fill)
    cross_probs = jax.nn.softmax(cross_scores, axis=-1)
    cross_out = low_back(low(jnp.einsum('fqhk,khe->fqhe', low(cross_probs), value_text, precision=highest).reshape(frames, FRAME_TOK, D)))
    after_c = after_a + low_back(matmul(cross_out, cross_proj_full))
    hidden_m = low(normalize(after_c) * (1.0 + modulation[4]) + modulation[3])
    upward = low_back(matmul(hidden_m, up_full))
    activated = low(jax.nn.gelu(upward, approximate=True))
    return after_c + modulation[5] * low_back(matmul(activated, down_full))

def bucket_forward(inputs, silu_cond, text_rows, length, frame_clips, frame_flags, ada_full, text_kv_full, weight_set, temporal_qkv_full, temporal_proj_full):
    modulation = matmul(silu_cond[None], ada_full).reshape(9, D)
    text_kv = low_back(low(matmul(text_rows, text_kv_full)))
    key_text = text_kv[:, :D].reshape(TEXT, HEADS, HD)
    value_text = text_kv[:, D:].reshape(TEXT, HEADS, HD)
    live_keys = jnp.arange(TEXT) < length
    groups = inputs.reshape(FRAMES // FR_DEV, FR_DEV, FRAME_TOK, D)

    def one_group(group_rows):
        return frame_group(group_rows, modulation, key_text, value_text, live_keys, weight_set)
    after_m = lax.map(jax.checkpoint(one_group), groups).reshape(FRAMES, FRAME_TOK, D)
    hidden_t = low(normalize(after_m) * (1.0 + modulation[7]) + modulation[6])
    temporal_rows = low_back(low(matmul(hidden_t, temporal_qkv_full)))
    query_heads = temporal_rows[..., :D].reshape(FRAMES, FRAME_TOK, HEADS, HD)
    key_heads = temporal_rows[..., D:2 * D].reshape(FRAMES, FRAME_TOK, HEADS, HD)
    value_heads = temporal_rows[..., 2 * D:].reshape(FRAMES, FRAME_TOK, HEADS, HD)
    frame_pad = ((1, 1), (0, 0), (0, 0), (0, 0))
    keys_padded = jnp.pad(key_heads, frame_pad)
    values_padded = jnp.pad(value_heads, frame_pad)
    clips_ext = jnp.concatenate([jnp.full((1,), -1, jnp.int32), frame_clips.astype(jnp.int32), jnp.full((1,), -1, jnp.int32)])
    prev_live = clips_ext[:-2] == clips_ext[1:-1]
    next_live = clips_ext[2:] == clips_ext[1:-1]
    score_scale = 1.0 / math.sqrt(HD)
    score_prev = jnp.where(prev_live[:, None, None], lax.optimization_barrier(jnp.sum(query_heads * keys_padded[:-2], axis=-1)) * score_scale, masked_fill)
    score_self = lax.optimization_barrier(jnp.sum(query_heads * key_heads, axis=-1)) * score_scale
    score_next = jnp.where(next_live[:, None, None], lax.optimization_barrier(jnp.sum(query_heads * keys_padded[2:], axis=-1)) * score_scale, masked_fill)
    temporal_probs = jax.nn.softmax(jnp.stack([score_prev, score_self, score_next], axis=-1), axis=-1)
    mixed = temporal_probs[..., 0:1] * values_padded[:-2] + temporal_probs[..., 1:2] * value_heads + temporal_probs[..., 2:3] * values_padded[2:]
    mixed_low = low(mixed.reshape(FRAMES, FRAME_TOK, D))
    branch = low_back(matmul(mixed_low, temporal_proj_full))
    return after_m + frame_flags.astype(inputs.dtype)[:, None, None] * modulation[8] * branch

def reference(latent, condition, text, text_len, clip_ids, video_flag, ada_weight, text_kv_weight, qkv_weight, proj_weight, cross_q_weight, cross_proj_weight, up_weight, down_weight, temporal_qkv_weight, temporal_proj_weight, cotangent):
    inputs = latent.astype(jnp.float32)
    silu_cond = jax.nn.silu(condition.astype(jnp.float32))
    text_rows = text.astype(jnp.float32)

    def forward(inputs, ada_full, text_kv_full, qkv_full, proj_full, cross_q_full, cross_proj_full, up_full, down_full, temporal_qkv_full, temporal_proj_full):
        weight_set = (qkv_full, proj_full, cross_q_full, cross_proj_full, up_full, down_full)
        bucket_outputs = []
        for bucket in range(BUCKETS):
            bucket_outputs.append(jax.checkpoint(bucket_forward)(inputs[bucket], silu_cond[bucket], text_rows[bucket], text_len[bucket], clip_ids[bucket], video_flag[bucket], ada_full, text_kv_full, weight_set, temporal_qkv_full, temporal_proj_full))
        return jnp.stack(bucket_outputs)
    result, pullback = jax.vjp(forward, inputs, ada_weight.astype(jnp.float32), text_kv_weight.astype(jnp.float32), qkv_weight.astype(jnp.float32), proj_weight.astype(jnp.float32), cross_q_weight.astype(jnp.float32), cross_proj_weight.astype(jnp.float32), up_weight.astype(jnp.float32), down_weight.astype(jnp.float32), temporal_qkv_weight.astype(jnp.float32), temporal_proj_weight.astype(jnp.float32))
    grads = pullback(cotangent.astype(jnp.float32))
    return (result.astype(jnp.bfloat16), grads[0], grads[1], grads[2], grads[3], grads[4], grads[5], grads[6], grads[7], grads[8], grads[9], grads[10])
```

```python
import math

import jax
import jax.numpy as jnp
from jax import lax
from jax.sharding import PartitionSpec as P

HEADS = 16


epsilon = 1e-06
highest = lax.Precision.HIGHEST
masked_fill = -1e30


def extended(array, sides, width):
    for axis, dim in sides:
        devices, length = (lax.axis_size(axis), array.shape[dim])
        up = [(i, (i + 1) % devices) for i in range(devices - 1)]
        down = [(j, i) for i, j in up]
        last = lax.slice_in_dim(array, length - width, length, axis=dim)
        initial = lax.slice_in_dim(array, 0, width, axis=dim)
        before = lax.ppermute(last, axis, up)
        after = lax.ppermute(initial, axis, down)
        array = jnp.concatenate([before, array, after], axis=dim)
    return array


def product(left, right):
    return jnp.dot(left, right, preferred_element_type=jnp.float32)


def product_left(left, right):
    return lax.dot_general(
        left, right, (((0,), (0,)), ((), ())), preferred_element_type=jnp.float32
    )


def product_right(left, right):
    return lax.dot_general(
        left, right, (((1,), (1,)), ((), ())), preferred_element_type=jnp.float32
    )


def normalize(values):
    centred = values - jnp.mean(values, axis=-1, keepdims=True)
    reciprocal = lax.rsqrt(jnp.mean(centred * centred, axis=-1, keepdims=True) + epsilon)
    return (centred * reciprocal, reciprocal)


def normalize_back(upstream, normed, reciprocal):
    return reciprocal * (
        upstream
        - jnp.mean(upstream, axis=-1, keepdims=True)
        - normed * jnp.mean(upstream * normed, axis=-1, keepdims=True)
    )


def gather_halves(is_first, lower, upper):
    return lax.all_gather(
        jnp.where(is_first, lower, upper), ("bucket", "frame", "seq"), axis=0, tiled=True
    )


def scatter_halves(lower, upper):
    stacked = jnp.concatenate(
        [
            jnp.concatenate([part.astype(jnp.bfloat16) for part in lower], axis=1),
            jnp.concatenate([part.astype(jnp.bfloat16) for part in upper], axis=1),
        ],
        axis=0,
    )
    return lax.psum_scatter(stacked, ("bucket", "frame", "seq"), scatter_dimension=0, tiled=True)


def whole_halves(is_first, own):
    other = lax.ppermute(own, "bucket", [(0, 1), (1, 0)])
    return (
        jnp.where(is_first, own, other).astype(jnp.float32),
        jnp.where(is_first, other, own).astype(jnp.float32),
    )


def block_width():
    return 256


def gelu_tanh(values):
    return jax.nn.gelu(values, approximate=True)


def spatial_forward(query_heads, key_rows, value_rows):
    frame_count, row_count, head_count, head_size = query_heads.shape
    score_scale = 1.0 / math.sqrt(head_size)
    initial = (
        jnp.full((frame_count, row_count, head_count), masked_fill, jnp.float32),
        jnp.zeros((frame_count, row_count, head_count), jnp.float32),
        jnp.zeros((frame_count, row_count, head_count, head_size), jnp.float32),
        jnp.zeros((frame_count, row_count, head_count, head_size), jnp.float32),
    )

    def absorb(carried, pieces, anchor):
        key_piece, value_piece = pieces
        piece_rows = key_piece.shape[1]
        block_rows = block_width()
        running, normaliser, accumulated, exact_sum = carried
        for offset in range(0, piece_rows, block_rows):
            key_block = key_piece[:, offset : offset + block_rows].reshape(
                frame_count, block_rows, head_count, head_size
            )
            value_block = value_piece[:, offset : offset + block_rows].reshape(
                frame_count, block_rows, head_count, head_size
            )
            scores = (
                jnp.einsum(
                    "fqhe,fkhe->fqhk", query_heads, key_block, preferred_element_type=jnp.float32
                )
                * score_scale
            )
            highest_now = jnp.maximum(running, jnp.max(scores, axis=-1))
            factor = jnp.exp(running - highest_now)
            weights = jnp.exp(scores - highest_now[..., None])
            normaliser = normaliser * factor + jnp.sum(weights, axis=-1)
            accumulated = accumulated * factor[..., None] + jnp.einsum(
                "fqhk,fkhe->fqhe",
                weights.astype(jnp.bfloat16),
                value_block,
                preferred_element_type=jnp.float32,
            )
            exact_sum = exact_sum * factor[..., None] + jnp.einsum(
                "fqhk,fkhe->fqhe", weights, value_block.astype(jnp.float32), precision=highest
            )
            running = highest_now
        return (running, normaliser, accumulated, exact_sum)

    running, normaliser, accumulated, exact_sum = absorb(
        initial,
        (
            lax.all_gather(key_rows, "seq", axis=1, tiled=True),
            lax.all_gather(value_rows, "seq", axis=1, tiled=True),
        ),
        jnp.int32(0),
    )
    return (
        accumulated / normaliser[..., None],
        exact_sum / normaliser[..., None],
        running + jnp.log(normaliser),
    )


def spatial_backward(query_heads, key_rows, value_rows, log_total, grad_heads, delta_rows):
    frame_count, row_count, head_count, head_size = query_heads.shape
    score_scale = 1.0 / math.sqrt(head_size)
    model_width = key_rows.shape[2]
    full_rows = key_rows.shape[1] * lax.axis_size("seq")
    initial = (
        jnp.zeros(query_heads.shape, jnp.float32),
        jnp.zeros((frame_count, full_rows, model_width), jnp.float32),
        jnp.zeros((frame_count, full_rows, model_width), jnp.float32),
    )

    def absorb(carried, pieces, anchor):
        key_piece, value_piece = pieces
        piece_rows = key_piece.shape[1]
        block_rows = block_width()
        query_grad, key_grad, value_grad = carried
        for offset in range(0, piece_rows, block_rows):
            key_block = key_piece[:, offset : offset + block_rows].reshape(
                frame_count, block_rows, head_count, head_size
            )
            value_block = value_piece[:, offset : offset + block_rows].reshape(
                frame_count, block_rows, head_count, head_size
            )
            scores = (
                jnp.einsum(
                    "fqhe,fkhe->fqhk", query_heads, key_block, preferred_element_type=jnp.float32
                )
                * score_scale
            )
            prob_rows = jnp.exp(scores - log_total[..., None])
            value_part = jnp.einsum(
                "fqhk,fqhe->fkhe",
                prob_rows.astype(jnp.bfloat16),
                grad_heads,
                preferred_element_type=jnp.float32,
            )
            prob_grad = jnp.einsum(
                "fqhe,fkhe->fqhk", grad_heads, value_block, preferred_element_type=jnp.float32
            )
            score_grad = (prob_rows * (prob_grad - delta_rows[..., None])).astype(jnp.bfloat16)
            query_grad = (
                query_grad
                + jnp.einsum(
                    "fqhk,fkhe->fqhe", score_grad, key_block, preferred_element_type=jnp.float32
                )
                * score_scale
            )
            key_part = (
                jnp.einsum(
                    "fqhk,fqhe->fkhe", score_grad, query_heads, preferred_element_type=jnp.float32
                )
                * score_scale
            )
            row_start = anchor + offset
            key_grad = lax.dynamic_update_slice_in_dim(
                key_grad,
                lax.dynamic_slice_in_dim(key_grad, row_start, block_rows, 1)
                + key_part.reshape(frame_count, block_rows, model_width),
                row_start,
                1,
            )
            value_grad = lax.dynamic_update_slice_in_dim(
                value_grad,
                lax.dynamic_slice_in_dim(value_grad, row_start, block_rows, 1)
                + value_part.reshape(frame_count, block_rows, model_width),
                row_start,
                1,
            )
        return (query_grad, key_grad, value_grad)

    query_grad, key_grad, value_grad = absorb(
        initial,
        (
            lax.all_gather(key_rows, "seq", axis=1, tiled=True),
            lax.all_gather(value_rows, "seq", axis=1, tiled=True),
        ),
        jnp.int32(0),
    )
    key_grad, value_grad = (
        lax.psum_scatter(
            key_grad.astype(jnp.bfloat16), "seq", scatter_dimension=1, tiled=True
        ).astype(jnp.float32),
        lax.psum_scatter(
            value_grad.astype(jnp.bfloat16), "seq", scatter_dimension=1, tiled=True
        ).astype(jnp.float32),
    )
    return (query_grad, key_grad, value_grad)


def per_device(
    latent,
    condition,
    text,
    text_len,
    clip_ids,
    video_flag,
    ada_weight,
    text_kv_weight,
    qkv_weight,
    proj_weight,
    cross_q_weight,
    cross_proj_weight,
    up_weight,
    down_weight,
    temporal_qkv_weight,
    temporal_proj_weight,
    cotangent,
):
    frame_count, row_count, model_width = (latent.shape[1], latent.shape[2], latent.shape[3])
    head_count = HEADS
    head_size = model_width // head_count
    score_scale = 1.0 / math.sqrt(head_size)
    total_rows = frame_count * row_count
    silu_cond = jax.nn.silu(condition.astype(jnp.float32))
    mod_part = jnp.dot(silu_cond, ada_weight.astype(jnp.float32), precision=highest)
    text_part = product(text[0], text_kv_weight)
    mod_full, text_full = (
        lax.all_gather(mod_part, ("frame", "seq"), axis=1, tiled=True),
        lax.all_gather(text_part, ("frame", "seq"), axis=1, tiled=True),
    )
    modulation = mod_full.reshape(9, model_width)
    text_kv = text_full.astype(jnp.bfloat16)
    text_count = text_kv.shape[0]
    key_text = text_kv[:, :model_width].reshape(text_count, head_count, head_size)
    value_text = text_kv[:, model_width:].reshape(text_count, head_count, head_size)
    is_first = lax.axis_index("bucket") == 0
    ff_width = up_weight.shape[1]
    shard_rows = up_weight.shape[0]
    shards = lax.axis_size(("frame", "seq"))
    ff_blocks = ff_width // model_width
    up_mixed = (
        up_weight.reshape(shard_rows, shards, ff_blocks, shard_rows)
        .transpose(0, 2, 1, 3)
        .reshape(shard_rows, ff_width)
    )
    down_wide = (
        down_weight.reshape(ff_blocks, shard_rows, model_width)
        .transpose(1, 0, 2)
        .reshape(shard_rows, ff_width)
    )
    half_ff = ff_width // 2
    gathered_a = gather_halves(
        is_first,
        qkv_weight,
        jnp.concatenate([proj_weight, cross_q_weight, cross_proj_weight], axis=1),
    )
    gathered_b = gather_halves(
        is_first,
        jnp.concatenate([up_mixed[:, :half_ff], down_wide[:, :half_ff]], axis=1),
        jnp.concatenate([up_mixed[:, half_ff:], down_wide[:, half_ff:]], axis=1),
    )
    gathered_c = gather_halves(
        is_first,
        temporal_qkv_weight[:, : 2 * model_width],
        jnp.concatenate([temporal_qkv_weight[:, 2 * model_width :], temporal_proj_weight], axis=1),
    )
    qkv_full = gathered_a[:model_width]
    proj_full = gathered_a[model_width:, :model_width]
    cross_q_full = gathered_a[model_width:, model_width : 2 * model_width]
    cross_proj_full = gathered_a[model_width:, 2 * model_width :]
    up_halves = (gathered_b[:model_width, :half_ff], gathered_b[model_width:, :half_ff])
    down_parts = [
        gathered_b[
            model_width * (index * 2 // ff_blocks) :, half_ff:
        ][:model_width, model_width * (index % (ff_blocks // 2)) :][:, :model_width]
        for index in range(ff_blocks)
    ]
    tqk_full = gathered_c[:model_width]
    tv_full = gathered_c[model_width:, :model_width]
    tproj_full = gathered_c[model_width:, model_width:]
    inputs = latent[0].reshape(total_rows, model_width).astype(jnp.float32)
    normed_a, recip_a = normalize(inputs)
    hidden_a = (normed_a * (1.0 + modulation[1]) + modulation[0]).astype(jnp.bfloat16)
    qkv_rows = product(hidden_a, qkv_full).astype(jnp.bfloat16)
    query_heads = qkv_rows[:, :model_width].reshape(frame_count, row_count, head_count, head_size)
    key_rows = qkv_rows[:, model_width : 2 * model_width].reshape(
        frame_count, row_count, model_width
    )
    value_rows = qkv_rows[:, 2 * model_width :].reshape(frame_count, row_count, model_width)
    attended, attended_exact, log_total = spatial_forward(query_heads, key_rows, value_rows)
    attended_low = attended.reshape(total_rows, model_width).astype(jnp.bfloat16)
    branch_a = product(attended_low, proj_full)
    after_a = inputs + modulation[2] * branch_a
    after_low = after_a.astype(jnp.bfloat16)
    cross_query = (
        product(after_low, cross_q_full)
        .astype(jnp.bfloat16)
        .reshape(total_rows, head_count, head_size)
    )
    live_keys = jnp.arange(text_count) < text_len[0]
    cross_scores = (
        jnp.einsum("rhe,khe->rhk", cross_query, key_text, preferred_element_type=jnp.float32)
        * score_scale
    )
    cross_probs = jax.nn.softmax(jnp.where(live_keys, cross_scores, masked_fill), axis=-1)
    cross_low = cross_probs.astype(jnp.bfloat16)
    cross_out = (
        jnp.einsum("rhk,khe->rhe", cross_low, value_text, preferred_element_type=jnp.float32)
        .reshape(total_rows, model_width)
        .astype(jnp.bfloat16)
    )
    after_c = after_a + product(cross_out, cross_proj_full)
    normed_m, recip_m = normalize(after_c)
    hidden_m = (normed_m * (1.0 + modulation[4]) + modulation[3]).astype(jnp.bfloat16)
    upward_halves = [product(hidden_m, part) for part in up_halves]
    activated_halves = [gelu_tanh(part).astype(jnp.bfloat16) for part in upward_halves]
    activated_parts = [
        activated_halves[index * 2 // ff_blocks][
            :, model_width * (index % (ff_blocks // 2)) :
        ][:, :model_width]
        for index in range(ff_blocks)
    ]
    branch_m = sum(product(left, right) for left, right in zip(activated_parts, down_parts))
    after_m = after_c + modulation[5] * branch_m
    normed_t, recip_t = normalize(after_m)
    hidden_t = (normed_t * (1.0 + modulation[7]) + modulation[6]).astype(jnp.bfloat16)
    temporal_rows = jnp.concatenate(
        [
            product(hidden_t, tqk_full).astype(jnp.bfloat16),
            product(hidden_t, tv_full).astype(jnp.bfloat16),
        ],
        axis=1,
    )
    temporal_query = (
        temporal_rows[:, :model_width]
        .astype(jnp.float32)
        .reshape(frame_count, row_count, head_count, head_size)
    )
    key_value = temporal_rows[:, model_width:].reshape(frame_count, row_count, 2 * model_width)
    padded = extended(key_value, (("frame", 0),), 1)
    first_frame = lax.axis_index("frame") * frame_count
    clips_ext = jnp.concatenate(
        [jnp.full((1,), -1, jnp.int32), clip_ids[0], jnp.full((1,), -1, jnp.int32)]
    )
    clips_local = lax.dynamic_slice_in_dim(clips_ext, first_frame, frame_count + 2)
    prev_live = clips_local[:-2] == clips_local[1:-1]
    next_live = clips_local[2:] == clips_local[1:-1]
    flag_local = lax.dynamic_slice_in_dim(video_flag[0], first_frame, frame_count).astype(
        jnp.float32
    )
    neighbour_sets = (padded[:-2], padded[1:-1], padded[2:])
    key_sets = [
        member[..., :model_width]
        .astype(jnp.float32)
        .reshape(frame_count, row_count, head_count, head_size)
        for member in neighbour_sets
    ]
    value_sets = [
        member[..., model_width:]
        .astype(jnp.float32)
        .reshape(frame_count, row_count, head_count, head_size)
        for member in neighbour_sets
    ]
    score_prev = jnp.where(
        prev_live[:, None, None],
        jnp.sum(temporal_query * key_sets[0], axis=-1) * score_scale,
        masked_fill,
    )
    score_self = jnp.sum(temporal_query * key_sets[1], axis=-1) * score_scale
    score_next = jnp.where(
        next_live[:, None, None],
        jnp.sum(temporal_query * key_sets[2], axis=-1) * score_scale,
        masked_fill,
    )
    temporal_probs = jax.nn.softmax(
        jnp.stack([score_prev, score_self, score_next], axis=-1), axis=-1
    )
    mixed = (
        temporal_probs[..., 0:1] * value_sets[0]
        + temporal_probs[..., 1:2] * value_sets[1]
        + temporal_probs[..., 2:3] * value_sets[2]
    )
    mixed_low = mixed.reshape(total_rows, model_width).astype(jnp.bfloat16)
    branch_t = product(mixed_low, tproj_full)
    flag_rows = jnp.repeat(flag_local, row_count)[:, None]
    result_rows = after_m + flag_rows * modulation[8] * branch_t
    result = result_rows.astype(jnp.bfloat16).reshape(latent.shape)
    result_grad = cotangent[0].reshape(total_rows, model_width).astype(jnp.float32)
    gate_t_grad = jnp.sum(flag_rows * branch_t * result_grad, axis=0)
    branch_t_grad = (flag_rows * modulation[8] * result_grad).astype(jnp.bfloat16)
    temporal_proj_grad = product_left(mixed_low, branch_t_grad)
    mixed_grad = product_right(branch_t_grad, tproj_full).reshape(
        frame_count, row_count, head_count, head_size
    )
    prob_grads = jnp.stack(
        [
            jnp.sum(mixed_grad * value_sets[0], axis=-1),
            jnp.sum(mixed_grad * value_sets[1], axis=-1),
            jnp.sum(mixed_grad * value_sets[2], axis=-1),
        ],
        axis=-1,
    )
    score_grads = temporal_probs * (
        prob_grads - jnp.sum(temporal_probs * prob_grads, axis=-1, keepdims=True)
    )
    tquery_grad = (
        score_grads[..., 0:1] * key_sets[0]
        + score_grads[..., 1:2] * key_sets[1]
        + score_grads[..., 2:3] * key_sets[2]
    ) * score_scale
    pair_grads = [
        jnp.concatenate(
            [
                (score_grads[..., index : index + 1] * temporal_query * score_scale).reshape(
                    frame_count, row_count, model_width
                ),
                (temporal_probs[..., index : index + 1] * mixed_grad).reshape(
                    frame_count, row_count, model_width
                ),
            ],
            axis=-1,
        )
        for index in range(3)
    ]
    padded_grad = jnp.zeros((frame_count + 2, row_count, 2 * model_width), jnp.float32)
    padded_grad = (
        padded_grad.at[:-2].add(pair_grads[0]).at[1:-1].add(pair_grads[1]).at[2:].add(pair_grads[2])
    )
    outgoing = jnp.stack([padded_grad[0], padded_grad[-1]])
    incoming = extended(outgoing.astype(jnp.bfloat16), (("frame", 0),), 1).astype(outgoing.dtype)
    own_grad = padded_grad[1:-1].at[0].add(incoming[0]).at[-1].add(incoming[3])
    temporal_grad = jnp.concatenate(
        [
            tquery_grad.reshape(total_rows, model_width),
            own_grad.reshape(total_rows, 2 * model_width),
        ],
        axis=1,
    ).astype(jnp.bfloat16)
    tqk_grad = product_left(hidden_t, temporal_grad[:, : 2 * model_width])
    tv_grad = product_left(hidden_t, temporal_grad[:, 2 * model_width :])
    scattered_c = scatter_halves([tqk_grad], [tv_grad, temporal_proj_grad])
    hidden_t_grad = product_right(temporal_grad[:, : 2 * model_width], tqk_full) + product_right(
        temporal_grad[:, 2 * model_width :], tv_full
    )
    grad_m = result_grad + normalize_back(hidden_t_grad * (1.0 + modulation[7]), normed_t, recip_t)
    gate_m_grad = jnp.sum(branch_m * grad_m, axis=0)
    branch_m_grad = (modulation[5] * grad_m).astype(jnp.bfloat16)
    down_grads = [product_left(part, branch_m_grad) for part in activated_parts]
    upward_grads = []
    for index in range(2):
        activated_grad = jnp.concatenate(
            [
                product_right(branch_m_grad, part)
                for part in down_parts[index * ff_blocks // 2 : (index + 1) * ff_blocks // 2]
            ],
            axis=1,
        )
        gelu_back = jax.vjp(gelu_tanh, upward_halves[index])[1]
        upward_grads.append(gelu_back(activated_grad)[0].astype(jnp.bfloat16))
    up_grads = [product_left(hidden_m, part) for part in upward_grads]
    scattered_b = scatter_halves(
        [up_grads[0]] + down_grads[: ff_blocks // 2], [up_grads[1]] + down_grads[ff_blocks // 2 :]
    )
    hidden_m_grad = product_right(upward_grads[0], up_halves[0]) + product_right(
        upward_grads[1], up_halves[1]
    )
    grad_c = grad_m + normalize_back(hidden_m_grad * (1.0 + modulation[4]), normed_m, recip_m)
    cross_branch_grad = grad_c.astype(jnp.bfloat16)
    cross_proj_grad = product_left(cross_out, cross_branch_grad)
    cross_out_grad = (
        product_right(cross_branch_grad, cross_proj_full)
        .astype(jnp.bfloat16)
        .reshape(total_rows, head_count, head_size)
    )
    value_text_grad = jnp.einsum(
        "rhk,rhe->khe", cross_low, cross_out_grad, preferred_element_type=jnp.float32
    )
    cross_prob_grad = jnp.einsum(
        "rhe,khe->rhk", cross_out_grad, value_text, preferred_element_type=jnp.float32
    )
    cross_score_grad = (
        cross_probs
        * (cross_prob_grad - jnp.sum(cross_probs * cross_prob_grad, axis=-1, keepdims=True))
    ).astype(jnp.bfloat16)
    cross_query_grad = (
        (
            jnp.einsum(
                "rhk,khe->rhe", cross_score_grad, key_text, preferred_element_type=jnp.float32
            )
            * score_scale
        )
        .reshape(total_rows, model_width)
        .astype(jnp.bfloat16)
    )
    key_text_grad = (
        jnp.einsum(
            "rhk,rhe->khe", cross_score_grad, cross_query, preferred_element_type=jnp.float32
        )
        * score_scale
    )
    cross_q_grad = product_left(after_low, cross_query_grad)
    grad_a = grad_c + product_right(cross_query_grad, cross_q_full)
    gate_a_grad = jnp.sum(branch_a * grad_a, axis=0)
    branch_a_grad = (modulation[2] * grad_a).astype(jnp.bfloat16)
    proj_grad = product_left(attended_low, branch_a_grad)
    attended_grad = (
        product_right(branch_a_grad, proj_full)
        .astype(jnp.bfloat16)
        .reshape(frame_count, row_count, head_count, head_size)
    )
    delta_rows = jnp.sum(attended_grad.astype(jnp.float32) * attended_exact, axis=-1)
    query_grad, key_grad, value_grad = spatial_backward(
        query_heads, key_rows, value_rows, log_total, attended_grad, delta_rows
    )
    qkv_rows_grad = jnp.concatenate(
        [
            query_grad.reshape(total_rows, model_width),
            key_grad.reshape(total_rows, model_width),
            value_grad.reshape(total_rows, model_width),
        ],
        axis=1,
    ).astype(jnp.bfloat16)
    qkv_grad = product_left(hidden_a, qkv_rows_grad)
    hidden_a_grad = product_right(qkv_rows_grad, qkv_full)
    input_grad = grad_a + normalize_back(hidden_a_grad * (1.0 + modulation[1]), normed_a, recip_a)
    latent_grad = input_grad.reshape(latent.shape)
    mod_grad = jnp.stack(
        [
            jnp.sum(hidden_a_grad, axis=0),
            jnp.sum(hidden_a_grad * normed_a, axis=0),
            gate_a_grad,
            jnp.sum(hidden_m_grad, axis=0),
            jnp.sum(hidden_m_grad * normed_m, axis=0),
            gate_m_grad,
            jnp.sum(hidden_t_grad, axis=0),
            jnp.sum(hidden_t_grad * normed_t, axis=0),
            gate_t_grad,
        ]
    ).reshape(1, 9 * model_width)
    text_grad = jnp.concatenate(
        [
            key_text_grad.reshape(text_count, model_width),
            value_text_grad.reshape(text_count, model_width),
        ],
        axis=1,
    )
    mod_slice, text_slice = (
        lax.psum_scatter(mod_grad, ("frame", "seq"), scatter_dimension=1, tiled=True),
        lax.psum_scatter(text_grad, ("frame", "seq"), scatter_dimension=1, tiled=True),
    )
    swap = [(0, 1), (1, 0)]
    silu_pair = jnp.concatenate([silu_cond, lax.ppermute(silu_cond, "bucket", swap)], axis=0)
    mod_pair = jnp.concatenate([mod_slice, lax.ppermute(mod_slice, "bucket", swap)], axis=0)
    ada_grad = lax.dot_general(
        silu_pair, mod_pair, (((0,), (0,)), ((), ())), precision=highest
    )
    text_low = text_slice.astype(jnp.bfloat16)
    text_pair = jnp.concatenate([text[0], lax.ppermute(text[0], "bucket", swap)], axis=0)
    slice_pair = jnp.concatenate([text_low, lax.ppermute(text_low, "bucket", swap)], axis=0)
    text_kv_grad = product_left(text_pair, slice_pair)
    scattered_a = scatter_halves([qkv_grad], [proj_grad, cross_q_grad, cross_proj_grad])
    lower_a, upper_a = whole_halves(is_first, scattered_a)
    lower_b, upper_b = whole_halves(is_first, scattered_b)
    lower_c, upper_c = whole_halves(is_first, scattered_c)
    up_shard = (
        jnp.concatenate([lower_b[:, :half_ff], upper_b[:, :half_ff]], axis=1)
        .reshape(shard_rows, ff_blocks, shards, shard_rows)
        .transpose(0, 2, 1, 3)
        .reshape(shard_rows, ff_width)
    )
    down_shard = (
        jnp.concatenate([lower_b[:, half_ff:], upper_b[:, half_ff:]], axis=1)
        .reshape(shard_rows, ff_blocks, model_width)
        .transpose(1, 0, 2)
        .reshape(ff_blocks * shard_rows, model_width)
    )
    return (
        result,
        latent_grad,
        ada_grad,
        text_kv_grad,
        lower_a,
        upper_a[:, :model_width],
        upper_a[:, model_width : 2 * model_width],
        upper_a[:, 2 * model_width :],
        up_shard,
        down_shard,
        jnp.concatenate([lower_c, upper_c[:, :model_width]], axis=1),
        upper_c[:, model_width:],
    )


def solution(mesh):
    return jax.shard_map(
        per_device,
        mesh=mesh,
        in_specs=(
            P("bucket", "frame", "seq", None),
            P("bucket", None),
            P("bucket", None, None),
            P("bucket"),
            P("bucket", None),
            P("bucket", None),
            P(None, ("frame", "seq")),
            P(None, ("frame", "seq")),
            P(("frame", "seq"), None),
            P(("frame", "seq"), None),
            P(("frame", "seq"), None),
            P(("frame", "seq"), None),
            P(("frame", "seq"), None),
            P(("frame", "seq"), None),
            P(("frame", "seq"), None),
            P(("frame", "seq"), None),
            P("bucket", "frame", "seq", None),
        ),
        out_specs=(
            P("bucket", "frame", "seq", None),
            P("bucket", "frame", "seq", None),
            P(None, ("frame", "seq")),
            P(None, ("frame", "seq")),
            P(("frame", "seq"), None),
            P(("frame", "seq"), None),
            P(("frame", "seq"), None),
            P(("frame", "seq"), None),
            P(("frame", "seq"), None),
            P(("frame", "seq"), None),
            P(("frame", "seq"), None),
            P(("frame", "seq"), None),
        ),
        check_vma=False,
    )
```

```python
import math

import jax
import jax.numpy as jnp
from jax import lax
from jax.experimental import pallas as pl
from jax.experimental.pallas import tpu as pltpu
from jax.sharding import PartitionSpec as P

HEADS = 16


epsilon = 1e-06
highest = lax.Precision.HIGHEST
masked_fill = -1e30
vmem_limit = 48 * 1024 * 1024


def product(left, right):
    return jnp.dot(left, right, preferred_element_type=jnp.float32)


def contract(left, right, left_dim, right_dim):
    return lax.dot_general(
        left, right, (((left_dim,), (right_dim,)), ((), ())), preferred_element_type=jnp.float32
    )


def call(body, grid, in_specs, out_specs, out_shape, name):
    return pl.pallas_call(
        body,
        grid=grid,
        in_specs=in_specs,
        out_specs=out_specs,
        out_shape=out_shape,
        name=name,
        compiler_params=pltpu.CompilerParams(vmem_limit_bytes=vmem_limit),
    )


def spatial_forward(query, key_value, frame_count):
    model_width, total_rows = query.shape
    head_size = model_width // HEADS
    rows = total_rows // frame_count
    keys = key_value.shape[1] // frame_count
    scale = 1.0 / math.sqrt(head_size)

    def body(q_ref, k_ref, v_ref, out_ref, lse_ref):
        scores = contract(k_ref[...], q_ref[...], 0, 0) * scale
        top = jnp.max(scores, axis=0, keepdims=True)
        weights = jnp.exp(scores - top)
        total = jnp.sum(weights, axis=0, keepdims=True)
        out = product(v_ref[...], weights.astype(jnp.bfloat16))
        out_ref[...] = (out / total).astype(jnp.bfloat16)
        lse_ref[0] = top + jnp.log(total)

    return call(
        body,
        (frame_count, HEADS),
        [
            pl.BlockSpec((head_size, rows), lambda f, h: (h, f)),
            pl.BlockSpec((head_size, keys), lambda f, h: (h, f)),
            pl.BlockSpec((head_size, keys), lambda f, h: (HEADS + h, f)),
        ],
        [
            pl.BlockSpec((head_size, rows), lambda f, h: (h, f)),
            pl.BlockSpec((1, 1, rows), lambda f, h: (f * HEADS + h, 0, 0)),
        ],
        [
            jax.ShapeDtypeStruct(query.shape, jnp.bfloat16),
            jax.ShapeDtypeStruct((frame_count * HEADS, 1, rows), jnp.float32),
        ],
        "spatial_forward",
    )(query, key_value, key_value)


def spatial_backward(query, key_value, log_total, upstream, frame_count, frame):
    model_width, total_rows = query.shape
    head_size = model_width // HEADS
    rows = total_rows // frame_count
    keys = key_value.shape[1] // frame_count
    scale = 1.0 / math.sqrt(head_size)

    def body(q_ref, k_ref, v_ref, lse_ref, up_ref, dq_ref, dkv_ref):
        query_head, key_head, up_head = (q_ref[...], k_ref[...], up_ref[...])
        probs = jnp.exp(contract(key_head, query_head, 0, 0) * scale - lse_ref[0])
        dkv_ref[1] = contract(up_head, probs.astype(jnp.bfloat16), 1, 1).astype(jnp.bfloat16)
        prob_grad = contract(v_ref[...], up_head, 0, 0)
        delta = jnp.sum(probs * prob_grad, axis=0, keepdims=True)
        score_grad = (probs * (prob_grad - delta)).astype(jnp.bfloat16)
        dq_ref[...] = (product(key_head, score_grad) * scale).astype(jnp.bfloat16)
        dkv_ref[0] = (contract(query_head, score_grad, 1, 1) * scale).astype(jnp.bfloat16)

    query_grad, pair_grad = call(
        body,
        (HEADS,),
        [
            pl.BlockSpec((head_size, rows), lambda h: (h, frame)),
            pl.BlockSpec((head_size, keys), lambda h: (h, frame)),
            pl.BlockSpec((head_size, keys), lambda h: (HEADS + h, frame)),
            pl.BlockSpec((1, 1, rows), lambda h: (frame * HEADS + h, 0, 0)),
            pl.BlockSpec((head_size, rows), lambda h: (h, frame)),
        ],
        [
            pl.BlockSpec((head_size, rows), lambda h: (h, 0)),
            pl.BlockSpec((2, head_size, keys), lambda h: (0, h, 0)),
        ],
        [
            jax.ShapeDtypeStruct((model_width, rows), jnp.bfloat16),
            jax.ShapeDtypeStruct((2, model_width, keys), jnp.bfloat16),
        ],
        "spatial_backward",
    )(query, key_value, key_value, log_total, upstream)
    return (query_grad, pair_grad.reshape(2 * model_width, keys))


def cross_probs_of(length_ref, q_ref, k_ref, scale):
    scores = contract(k_ref[...], q_ref[...], 0, 0) * scale
    live = lax.broadcasted_iota(jnp.int32, scores.shape, 0) < length_ref[0]
    scores = jnp.where(live, scores, masked_fill)
    weights = jnp.exp(scores - jnp.max(scores, axis=0, keepdims=True))
    return weights / jnp.sum(weights, axis=0, keepdims=True)


def cross_forward(length, query, text_pair):
    model_width, total_rows = query.shape
    head_size = model_width // HEADS
    keys = text_pair.shape[1]
    scale = 1.0 / math.sqrt(head_size)

    def body(length_ref, q_ref, k_ref, v_ref, out_ref):
        probs = cross_probs_of(length_ref, q_ref, k_ref, scale)
        out_ref[...] = product(v_ref[...], probs.astype(jnp.bfloat16)).astype(jnp.bfloat16)

    return call(
        body,
        (HEADS,),
        [
            pl.BlockSpec(memory_space=pltpu.SMEM),
            pl.BlockSpec((head_size, total_rows), lambda h: (h, 0)),
            pl.BlockSpec((head_size, keys), lambda h: (h, 0)),
            pl.BlockSpec((head_size, keys), lambda h: (HEADS + h, 0)),
        ],
        pl.BlockSpec((head_size, total_rows), lambda h: (h, 0)),
        jax.ShapeDtypeStruct(query.shape, jnp.bfloat16),
        "cross_forward",
    )(length, query, text_pair, text_pair)


def cross_backward(length, query, text_pair, upstream):
    model_width, total_rows = query.shape
    head_size = model_width // HEADS
    keys = text_pair.shape[1]
    scale = 1.0 / math.sqrt(head_size)

    def body(length_ref, q_ref, k_ref, v_ref, up_ref, dq_ref, dkv_ref):
        up_head = up_ref[...]
        probs = cross_probs_of(length_ref, q_ref, k_ref, scale)
        prob_grad = contract(v_ref[...], up_head, 0, 0)
        delta = jnp.sum(probs * prob_grad, axis=0, keepdims=True)
        score_grad = (probs * (prob_grad - delta)).astype(jnp.bfloat16)
        dq_ref[...] = (product(k_ref[...], score_grad) * scale).astype(jnp.bfloat16)
        dkv_ref[0] = contract(q_ref[...], score_grad, 1, 1) * scale
        dkv_ref[1] = contract(up_head, probs.astype(jnp.bfloat16), 1, 1)

    query_grad, pair_grad = call(
        body,
        (HEADS,),
        [
            pl.BlockSpec(memory_space=pltpu.SMEM),
            pl.BlockSpec((head_size, total_rows), lambda h: (h, 0)),
            pl.BlockSpec((head_size, keys), lambda h: (h, 0)),
            pl.BlockSpec((head_size, keys), lambda h: (HEADS + h, 0)),
            pl.BlockSpec((head_size, total_rows), lambda h: (h, 0)),
        ],
        [
            pl.BlockSpec((head_size, total_rows), lambda h: (h, 0)),
            pl.BlockSpec((2, head_size, keys), lambda h: (0, h, 0)),
        ],
        [
            jax.ShapeDtypeStruct(query.shape, jnp.bfloat16),
            jax.ShapeDtypeStruct((2, model_width, keys), jnp.float32),
        ],
        "cross_backward",
    )(length, query, text_pair, text_pair, upstream)
    return (query_grad, pair_grad.reshape(text_pair.shape))


def temporal_probs_of(live_ref, query_frame, key_frames, frame, scale):
    scores = []
    for index in range(3):
        score = jnp.sum(query_frame * key_frames[index], axis=0, keepdims=True) * scale
        if index != 1:
            score = jnp.where(live_ref[frame, index // 2] != 0, score, masked_fill)
        scores.append(score)
    top = jnp.maximum(jnp.maximum(scores[0], scores[1]), scores[2])
    weights = [jnp.exp(score - top) for score in scores]
    inverse = 1.0 / (weights[0] + weights[1] + weights[2])
    return [weight * inverse for weight in weights]


def temporal_forward(live, query, key_value, frame_count):
    model_width, total_rows = query.shape
    head_size = model_width // HEADS
    rows = total_rows // frame_count
    extended_rows = key_value.shape[1]
    scale = 1.0 / math.sqrt(head_size)

    def body(live_ref, q_ref, k_ref, v_ref, out_ref):
        for frame in range(frame_count):
            query_frame = q_ref[:, frame * rows : (frame + 1) * rows].astype(jnp.float32)
            spans = [slice((frame + j) * rows, (frame + j + 1) * rows) for j in range(3)]
            key_frames = [k_ref[:, span].astype(jnp.float32) for span in spans]
            probs = temporal_probs_of(live_ref, query_frame, key_frames, frame, scale)
            mixed = sum(
                prob * v_ref[:, span].astype(jnp.float32) for prob, span in zip(probs, spans)
            )
            out_ref[:, frame * rows : (frame + 1) * rows] = mixed.astype(jnp.bfloat16)

    return call(
        body,
        (HEADS,),
        [
            pl.BlockSpec(memory_space=pltpu.SMEM),
            pl.BlockSpec((head_size, total_rows), lambda h: (h, 0)),
            pl.BlockSpec((head_size, extended_rows), lambda h: (h, 0)),
            pl.BlockSpec((head_size, extended_rows), lambda h: (HEADS + h, 0)),
        ],
        pl.BlockSpec((head_size, total_rows), lambda h: (h, 0)),
        jax.ShapeDtypeStruct(query.shape, jnp.bfloat16),
        "temporal_forward",
    )(live, query, key_value, key_value)


def temporal_backward(live, query, key_value, upstream, frame_count):
    model_width, total_rows = query.shape
    head_size = model_width // HEADS
    rows = total_rows // frame_count
    extended_rows = key_value.shape[1]
    scale = 1.0 / math.sqrt(head_size)

    def body(live_ref, q_ref, k_ref, v_ref, up_ref, dq_ref, dkv_ref):
        key_sums = [None] * (frame_count + 2)
        value_sums = [None] * (frame_count + 2)
        for frame in range(frame_count):
            own = slice(frame * rows, (frame + 1) * rows)
            query_frame = q_ref[:, own].astype(jnp.float32)
            up_frame = up_ref[:, own]
            spans = [slice((frame + j) * rows, (frame + j + 1) * rows) for j in range(3)]
            key_frames = [k_ref[:, span].astype(jnp.float32) for span in spans]
            probs = temporal_probs_of(live_ref, query_frame, key_frames, frame, scale)
            prob_grads = [
                jnp.sum(up_frame * v_ref[:, span].astype(jnp.float32), axis=0, keepdims=True)
                for span in spans
            ]
            delta = sum(prob * grad for prob, grad in zip(probs, prob_grads))
            score_grads = [
                prob * (grad - delta) * scale for prob, grad in zip(probs, prob_grads)
            ]
            dq_ref[:, own] = sum(
                grad * key_frame for grad, key_frame in zip(score_grads, key_frames)
            ).astype(jnp.bfloat16)
            for j in range(3):
                key_part = score_grads[j] * query_frame
                value_part = probs[j] * up_frame
                at = frame + j
                key_sums[at] = key_part if key_sums[at] is None else key_sums[at] + key_part
                value_sums[at] = (
                    value_part if value_sums[at] is None else value_sums[at] + value_part
                )
        for at in range(frame_count + 2):
            dkv_ref[0, :, at * rows : (at + 1) * rows] = key_sums[at].astype(jnp.bfloat16)
            dkv_ref[1, :, at * rows : (at + 1) * rows] = value_sums[at].astype(jnp.bfloat16)

    query_grad, pair_grad = call(
        body,
        (HEADS,),
        [
            pl.BlockSpec(memory_space=pltpu.SMEM),
            pl.BlockSpec((head_size, total_rows), lambda h: (h, 0)),
            pl.BlockSpec((head_size, extended_rows), lambda h: (h, 0)),
            pl.BlockSpec((head_size, extended_rows), lambda h: (HEADS + h, 0)),
            pl.BlockSpec((head_size, total_rows), lambda h: (h, 0)),
        ],
        [
            pl.BlockSpec((head_size, total_rows), lambda h: (h, 0)),
            pl.BlockSpec((2, head_size, extended_rows), lambda h: (0, h, 0)),
        ],
        [
            jax.ShapeDtypeStruct(query.shape, jnp.bfloat16),
            jax.ShapeDtypeStruct((2, model_width, extended_rows), jnp.bfloat16),
        ],
        "temporal_backward",
    )(live, query, key_value, key_value, upstream)
    return (query_grad, pair_grad.reshape(key_value.shape))


def normalize(values):
    centred = values - jnp.mean(values, axis=-1, keepdims=True)
    reciprocal = lax.rsqrt(jnp.mean(centred * centred, axis=-1, keepdims=True) + epsilon)
    return (centred * reciprocal, reciprocal)


def normalize_back(upstream, normed, reciprocal):
    return reciprocal * (
        upstream
        - jnp.mean(upstream, axis=-1, keepdims=True)
        - normed * jnp.mean(upstream * normed, axis=-1, keepdims=True)
    )


def gelu_tanh(values):
    return jax.nn.gelu(values, approximate=True)


def gather_halves(is_first, lower, upper):
    return lax.all_gather(
        jnp.where(is_first, lower, upper), ("bucket", "frame", "seq"), axis=0, tiled=True
    )


def tree_bits():
    return [
        (axis, step)
        for axis in ("frame", "seq")
        for step in reversed(range(lax.axis_size(axis).bit_length() - 1))
    ]


def tree_order(turn):
    bits = tree_bits()
    last = bits[0]
    first = [bit for bit in bits[::-1] if bit != last]
    turn = turn % len(first)
    return first[turn:] + first[:turn] + [last]


def my_bit(bit):
    return (lax.axis_index(bit[0]) >> bit[1]) & 1


def across(value, bit):
    axis, step = bit
    return lax.ppermute(
        value, axis, [(i, i ^ (1 << step)) for i in range(lax.axis_size(axis))]
    )


def gather_tree(value):
    for bit in tree_bits()[::-1]:
        other = across(value, bit)
        mine = my_bit(bit) == 0
        value = jnp.concatenate(
            [jnp.where(mine, value, other), jnp.where(mine, other, value)], axis=0
        )
    return value


class Chain:
    def __init__(self, is_first, pair, turn):
        self.order = tree_order(turn)
        self.dims = tree_bits()
        self.is_first = is_first
        self.received = None
        if len(pair) == 2:
            lower, upper = pair
            self.kept = jnp.where(is_first, lower, upper)
            self.received = swapped(jnp.where(is_first, upper, lower))
        else:
            self.kept = pair[0]

    def advance(self):
        value = self.kept
        if self.received is not None:
            value = (
                value.astype(jnp.float32) + self.received.astype(jnp.float32)
            ).astype(value.dtype)
        if self.dims and value.ndim == 2:
            count = 1 << len(self.dims)
            value = value.reshape(
                (2,) * len(self.dims) + (value.shape[0] // count, value.shape[1])
            )
        if self.order:
            bit = self.order.pop(0)
            dim = self.dims.index(bit)
            self.dims.remove(bit)
            index = my_bit(bit)
            self.received = across(
                lax.dynamic_index_in_dim(value, 1 - index, dim, keepdims=False), bit
            )
            self.kept = lax.dynamic_index_in_dim(value, index, dim, keepdims=False)
        else:
            self.kept = value
            self.received = None

    def finish(self):
        while self.received is not None or self.order:
            self.advance()
        return self.kept


def tick(main, chains):
    main, received = lax.optimization_barrier((main, [chain.received for chain in chains]))
    for chain, value in zip(chains, received):
        chain.received = value
        chain.advance()
    return main


def both_of(chain):
    own = chain.finish()
    other = swapped(own)
    return (
        jnp.where(chain.is_first, own, other).astype(jnp.float32),
        jnp.where(chain.is_first, other, own).astype(jnp.float32),
    )


def low(value):
    return value.astype(jnp.bfloat16)


def swapped(value):
    return lax.ppermute(value, "bucket", [(0, 1), (1, 0)])


def per_device(
    latent,
    condition,
    text,
    text_len,
    clip_ids,
    video_flag,
    ada_weight,
    text_kv_weight,
    qkv_weight,
    proj_weight,
    cross_q_weight,
    cross_proj_weight,
    up_weight,
    down_weight,
    temporal_qkv_weight,
    temporal_proj_weight,
    cotangent,
):
    frame_count, row_count, width = (latent.shape[1], latent.shape[2], latent.shape[3])
    total_rows = frame_count * row_count
    seq_size = lax.axis_size("seq")
    frame_size = lax.axis_size("frame")
    shards = seq_size * frame_size
    is_first = lax.axis_index("bucket") == 0
    ff_width = up_weight.shape[1]
    shard_rows = up_weight.shape[0]
    ff_blocks = ff_width // width
    half_ff = ff_width // 2

    shifts = [
        [((i + s) % seq_size, i) for i in range(seq_size)] for s in range(1, seq_size)
    ]
    latent_rest = [lax.ppermute(latent[0], "seq", shift) for shift in shifts]

    gathered_a = gather_halves(
        is_first,
        qkv_weight,
        jnp.concatenate([proj_weight, cross_q_weight, cross_proj_weight], axis=1),
    )
    up_mixed = (
        up_weight.reshape(shard_rows, shards, ff_blocks, shard_rows)
        .transpose(0, 2, 1, 3)
        .reshape(shard_rows, ff_width)
    )
    down_wide = (
        down_weight.reshape(ff_blocks, shard_rows, width)
        .transpose(1, 0, 2)
        .reshape(shard_rows, ff_width)
    )
    gathered_b = gather_halves(
        is_first,
        jnp.concatenate([up_mixed[:, :half_ff], down_wide[:, :half_ff]], axis=1),
        jnp.concatenate([up_mixed[:, half_ff:], down_wide[:, half_ff:]], axis=1),
    )

    silu_cond = jax.nn.silu(condition.astype(jnp.float32))
    mod_part = jnp.dot(silu_cond, ada_weight.astype(jnp.float32), precision=highest)
    modulation = gather_tree(mod_part).reshape(9, width)
    text_part = contract(text_kv_weight, text[0], 0, 1).astype(jnp.bfloat16)
    text_pair = gather_tree(text_part)

    inputs = latent[0].reshape(total_rows, width).astype(jnp.float32)
    normed_a, recip_a = normalize(inputs)
    hidden_a = (normed_a * (1.0 + modulation[1]) + modulation[0]).astype(jnp.bfloat16)
    normed_rest = [
        normalize(rest.reshape(total_rows, width).astype(jnp.float32))[0] for rest in latent_rest
    ]
    hidden_rest = [
        (normed * (1.0 + modulation[1]) + modulation[0]).astype(jnp.bfloat16)
        for normed in normed_rest
    ]
    hidden_all = jnp.concatenate(
        [part.reshape(frame_count, row_count, width) for part in [hidden_a] + hidden_rest], axis=1
    ).reshape(frame_count * seq_size * row_count, width)
    query_full = gathered_a[:width, :width]
    pair_full = gathered_a[:width, width:]
    proj_full = gathered_a[width:, :width]
    cross_q_full = gathered_a[width:, width : 2 * width]
    cross_proj_full = gathered_a[width:, 2 * width :]
    query = contract(query_full, hidden_a, 0, 1).astype(jnp.bfloat16)
    key_value = contract(pair_full, hidden_all, 0, 1).astype(jnp.bfloat16)
    attended, log_total = spatial_forward(query, key_value, frame_count)
    branch_a = contract(attended, proj_full, 0, 0)
    after_a = inputs + modulation[2] * branch_a
    after_low = after_a.astype(jnp.bfloat16)
    cross_query = contract(cross_q_full, after_low, 0, 1).astype(jnp.bfloat16)
    cross_out = cross_forward(text_len, cross_query, text_pair)
    after_c = after_a + contract(cross_out, cross_proj_full, 0, 0)
    normed_m, recip_m = normalize(after_c)
    hidden_m = (normed_m * (1.0 + modulation[4]) + modulation[3]).astype(jnp.bfloat16)

    temporal_lower, temporal_upper = lax.optimization_barrier(
        (
            jnp.concatenate([temporal_qkv_weight[:, :width], temporal_proj_weight], axis=1),
            temporal_qkv_weight[:, width:],
            query,
        )
    )[:2]
    gathered_c = gather_halves(is_first, temporal_lower, temporal_upper)
    up_halves = (gathered_b[:width, :half_ff], gathered_b[width:, :half_ff])
    per_half = ff_blocks // 2
    down_halves = (gathered_b[:width, half_ff:], gathered_b[width:, half_ff:])
    down_parts = [
        down_halves[index // per_half][
            :, width * (index % per_half) : width * (index % per_half + 1)
        ]
        for index in range(ff_blocks)
    ]
    tquery_full = gathered_c[:width, :width]
    tproj_full = gathered_c[:width, width:]
    tpair_full = gathered_c[width:]

    upward_halves = [product(hidden_m, part) for part in up_halves]
    activated_halves = [gelu_tanh(part).astype(jnp.bfloat16) for part in upward_halves]
    activated_parts = [
        activated_halves[index // per_half][
            :, width * (index % per_half) : width * (index % per_half + 1)
        ]
        for index in range(ff_blocks)
    ]
    branch_m = sum(product(left, right) for left, right in zip(activated_parts, down_parts))
    after_m = after_c + modulation[5] * branch_m
    normed_t, recip_t = normalize(after_m)
    hidden_t = (normed_t * (1.0 + modulation[7]) + modulation[6]).astype(jnp.bfloat16)
    ahead = [(i, i + 1) for i in range(frame_size - 1)]
    back = [(i + 1, i) for i in range(frame_size - 1)]
    hidden_prev = lax.ppermute(hidden_t[total_rows - row_count :], "frame", ahead)
    hidden_next = lax.ppermute(hidden_t[:row_count], "frame", back)
    hidden_ext = jnp.concatenate([hidden_prev, hidden_t, hidden_next], axis=0)
    tquery = contract(tquery_full, hidden_t, 0, 1).astype(jnp.bfloat16)
    tpair = contract(tpair_full, hidden_ext, 0, 1).astype(jnp.bfloat16)
    first_frame = lax.axis_index("frame") * frame_count
    clips_ext = jnp.concatenate(
        [jnp.full((1,), -1, jnp.int32), clip_ids[0], jnp.full((1,), -1, jnp.int32)]
    )
    clips_local = lax.dynamic_slice_in_dim(clips_ext, first_frame, frame_count + 2)
    live = jnp.stack(
        [clips_local[:-2] == clips_local[1:-1], clips_local[2:] == clips_local[1:-1]], axis=1
    ).astype(jnp.int32)
    flag_local = lax.dynamic_slice_in_dim(video_flag[0], first_frame, frame_count).astype(
        jnp.float32
    )
    mixed = temporal_forward(live, tquery, tpair, frame_count)
    branch_t = contract(mixed, tproj_full, 0, 0)
    flag_rows = jnp.repeat(flag_local, row_count)[:, None]
    result_rows = after_m + flag_rows * modulation[8] * branch_t
    result = result_rows.astype(jnp.bfloat16).reshape(latent.shape)

    result_grad = cotangent[0].reshape(total_rows, width).astype(jnp.float32)
    gate_t_grad = jnp.sum(flag_rows * branch_t * result_grad, axis=0)
    branch_t_grad = (flag_rows * modulation[8] * result_grad).astype(jnp.bfloat16)
    mixed_grad = contract(tproj_full, branch_t_grad, 1, 1)
    tquery_grad, tpair_grad = temporal_backward(live, tquery, tpair, mixed_grad, frame_count)
    ext_grad = contract(tpair_grad, tpair_full, 0, 1)
    to_prev = lax.ppermute(low(ext_grad[:row_count]), "frame", back)
    to_next = lax.ppermute(low(ext_grad[-row_count:]), "frame", ahead)
    tpair_weight_grad = low(contract(hidden_ext, tpair_grad, 0, 1))
    tquery_weight_grad = low(contract(hidden_t, tquery_grad, 0, 1))
    tproj_weight_grad = low(contract(mixed, branch_t_grad, 1, 0))
    hidden_t_grad = ext_grad[row_count:-row_count] + contract(tquery_grad, tquery_full, 0, 1)
    hidden_t_grad = jnp.concatenate(
        [
            hidden_t_grad[:row_count] + to_next.astype(jnp.float32),
            hidden_t_grad[row_count : total_rows - row_count],
            hidden_t_grad[total_rows - row_count :] + to_prev.astype(jnp.float32),
        ],
        axis=0,
    )
    hidden_t_grad, tpair_weight_grad, tquery_weight_grad, tproj_weight_grad = (
        lax.optimization_barrier(
            (hidden_t_grad, tpair_weight_grad, tquery_weight_grad, tproj_weight_grad)
        )
    )
    chain_tqk = Chain(is_first, (tquery_weight_grad, tpair_weight_grad[:, :width]), 0)
    chain_tpv = Chain(is_first, (tproj_weight_grad, tpair_weight_grad[:, width:]), 1)
    chains_t = [chain_tqk, chain_tpv]
    grad_m = result_grad + normalize_back(hidden_t_grad * (1.0 + modulation[7]), normed_t, recip_t)
    gate_m_grad = jnp.sum(branch_m * grad_m, axis=0)
    branch_m_grad = low(modulation[5] * grad_m)
    upward_grads = []
    for index in range(2):
        activated_grad = jnp.concatenate(
            [
                contract(branch_m_grad, part, 1, 1)
                for part in down_parts[index * per_half : (index + 1) * per_half]
            ],
            axis=1,
        )
        if index == 0:
            activated_grad = tick(activated_grad, chains_t)
        gelu_back = jax.vjp(gelu_tanh, upward_halves[index])[1]
        upward_grads.append(low(gelu_back(activated_grad)[0]))
    hidden_m_grad = contract(upward_grads[0], up_halves[0], 1, 1) + contract(
        upward_grads[1], up_halves[1], 1, 1
    )
    hidden_m_grad = tick(hidden_m_grad, chains_t)
    up_grads = [low(contract(hidden_m, part, 0, 0)) for part in upward_grads]
    down_grads = [low(contract(part, branch_m_grad, 0, 0)) for part in activated_parts]
    hidden_m_grad, up_grads, down_grads = lax.optimization_barrier(
        (hidden_m_grad, up_grads, down_grads)
    )
    chains_m = [
        Chain(
            is_first,
            (
                up_grads[0][:, width * index : width * (index + 1)],
                up_grads[1][:, width * index : width * (index + 1)],
            ),
            index,
        )
        for index in range(per_half)
    ] + [
        Chain(is_first, (down_grads[index], down_grads[per_half + index]), per_half + index)
        for index in range(per_half)
    ]
    hidden_m_grad = tick(hidden_m_grad, chains_t)
    grad_c = grad_m + normalize_back(hidden_m_grad * (1.0 + modulation[4]), normed_m, recip_m)
    cross_branch_grad = low(grad_c)
    cross_out_grad = low(contract(cross_proj_full, cross_branch_grad, 1, 1))
    cross_out_grad = tick(cross_out_grad, chains_t + chains_m)
    cross_query_grad, text_grad = cross_backward(text_len, cross_query, text_pair, cross_out_grad)
    chain_text = Chain(is_first, (low(text_grad),), 1)
    chain_text.advance()
    grad_a = grad_c + contract(cross_query_grad, cross_q_full, 0, 1)
    gate_a_grad = jnp.sum(branch_a * grad_a, axis=0)
    branch_a_grad = low(modulation[2] * grad_a)
    attended_grad = low(contract(proj_full, branch_a_grad, 1, 1))
    attended_grad = tick(attended_grad, chains_t + [chain_text])
    proj_grad = low(contract(attended, branch_a_grad, 1, 0))
    cross_q_grad = low(contract(after_low, cross_query_grad, 0, 1))
    cross_proj_grad = low(contract(cross_out, cross_branch_grad, 1, 0))
    attended_grad, proj_grad, cross_q_grad, cross_proj_grad = lax.optimization_barrier(
        (attended_grad, proj_grad, cross_q_grad, cross_proj_grad)
    )
    chain_pq = Chain(is_first, (proj_grad, cross_q_grad), 2)
    attended_grad = tick(attended_grad, chains_m + [chain_text])
    query_grads, pair_grads = ([], [])
    for frame in range(frame_count):
        query_grad, pair_grad = spatial_backward(
            query, key_value, log_total, attended_grad, frame_count, frame
        )
        query_grads.append(query_grad)
        pair_grads.append(pair_grad)
        if frame == 0:
            query_grads[0], attended_grad = tick(
                (query_grads[0], attended_grad), chains_m + [chain_pq, chain_text]
            )
    query_grad = jnp.concatenate(query_grads, axis=1)
    pair_grad = jnp.concatenate(pair_grads, axis=1)
    pair_grad = tick(pair_grad, chains_m + [chain_pq, chain_text])
    all_grad = contract(pair_grad, pair_full, 0, 1).reshape(
        frame_count, seq_size, row_count, width
    )
    rest_grad = [
        lax.ppermute(
            low(all_grad[:, s + 1]), "seq", [(j, i) for i, j in shifts[s]]
        )
        for s in range(seq_size - 1)
    ]
    pair_weight_grad = low(contract(hidden_all, pair_grad, 0, 1))
    chain_vp = Chain(is_first, (pair_weight_grad[:, width:], cross_proj_grad), 1)
    query_weight_grad = low(contract(hidden_a, query_grad, 0, 1))
    chain_qk = Chain(is_first, (query_weight_grad, pair_weight_grad[:, :width]), 2)
    own_grad = all_grad[:, 0].reshape(total_rows, width) + contract(query_grad, query_full, 0, 1)
    shift_a_grad = jnp.sum(own_grad, axis=0)
    scale_a_grad = jnp.sum(own_grad * normed_a, axis=0)
    for s in range(seq_size - 1):
        rest_rows = all_grad[:, s + 1].reshape(total_rows, width)
        shift_a_grad = shift_a_grad + jnp.sum(rest_rows, axis=0)
        scale_a_grad = scale_a_grad + jnp.sum(rest_rows * normed_rest[s], axis=0)
    hidden_a_grad = sum([rest.astype(jnp.float32).reshape(total_rows, width) for rest in rest_grad], own_grad)
    input_grad = grad_a + normalize_back(hidden_a_grad * (1.0 + modulation[1]), normed_a, recip_a)
    latent_grad = input_grad.reshape(latent.shape)
    mod_grad = jnp.stack(
        [
            shift_a_grad,
            scale_a_grad,
            gate_a_grad,
            jnp.sum(hidden_m_grad, axis=0),
            jnp.sum(hidden_m_grad * normed_m, axis=0),
            gate_m_grad,
            jnp.sum(hidden_t_grad, axis=0),
            jnp.sum(hidden_t_grad * normed_t, axis=0),
            gate_t_grad,
        ]
    ).reshape(shards, 9 * width // shards)
    mod_slice = Chain(is_first, (mod_grad,), 0).finish()
    text_low = chain_text.finish()
    silu_pair = jnp.concatenate([silu_cond, swapped(silu_cond)], axis=0)
    mod_pair = jnp.concatenate([mod_slice, swapped(mod_slice)], axis=0)
    ada_grad = lax.dot_general(
        silu_pair, mod_pair, (((0,), (0,)), ((), ())), precision=highest
    )
    text_both = jnp.concatenate([text[0], swapped(text[0])], axis=0)
    slice_both = jnp.concatenate([text_low, swapped(text_low)], axis=1)
    text_kv_grad = contract(text_both, slice_both, 0, 1)
    query_shard, key_shard = both_of(chain_qk)
    value_shard, cross_proj_shard = both_of(chain_vp)
    proj_shard, cross_q_shard = both_of(chain_pq)
    tquery_shard, tkey_shard = both_of(chain_tqk)
    tproj_shard, tvalue_shard = both_of(chain_tpv)
    ff_shards = [both_of(chain) for chain in chains_m]
    up_shard = (
        jnp.concatenate(
            [pair[side] for side in range(2) for pair in ff_shards[:per_half]], axis=1
        )
        .reshape(shard_rows, ff_blocks, shards, shard_rows)
        .transpose(0, 2, 1, 3)
        .reshape(shard_rows, ff_width)
    )
    down_shard = jnp.concatenate(
        [pair[side] for side in range(2) for pair in ff_shards[per_half:]], axis=0
    )
    return (
        result,
        latent_grad,
        ada_grad,
        text_kv_grad,
        jnp.concatenate([query_shard, key_shard, value_shard], axis=1),
        proj_shard,
        cross_q_shard,
        cross_proj_shard,
        up_shard,
        down_shard,
        jnp.concatenate([tquery_shard, tkey_shard, tvalue_shard], axis=1),
        tproj_shard,
    )


def solution(mesh):
    return jax.shard_map(
        per_device,
        mesh=mesh,
        in_specs=(
            P("bucket", "frame", "seq", None),
            P("bucket", None),
            P("bucket", None, None),
            P("bucket"),
            P("bucket", None),
            P("bucket", None),
            P(None, ("frame", "seq")),
            P(None, ("frame", "seq")),
            P(("frame", "seq"), None),
            P(("frame", "seq"), None),
            P(("frame", "seq"), None),
            P(("frame", "seq"), None),
            P(("frame", "seq"), None),
            P(("frame", "seq"), None),
            P(("frame", "seq"), None),
            P(("frame", "seq"), None),
            P("bucket", "frame", "seq", None),
        ),
        out_specs=(
            P("bucket", "frame", "seq", None),
            P("bucket", "frame", "seq", None),
            P(None, ("frame", "seq")),
            P(None, ("frame", "seq")),
            P(("frame", "seq"), None),
            P(("frame", "seq"), None),
            P(("frame", "seq"), None),
            P(("frame", "seq"), None),
            P(("frame", "seq"), None),
            P(("frame", "seq"), None),
            P(("frame", "seq"), None),
            P(("frame", "seq"), None),
        ),
        check_vma=False,
    )
```

```python
import math

import jax
import jax.numpy as jnp
from jax import lax
from jax.experimental import pallas as pl
from jax.experimental.pallas import tpu as pltpu
from jax.sharding import PartitionSpec as P

HEADS = 16


epsilon = 1e-06
highest = lax.Precision.HIGHEST
masked_fill = -1e30
vmem_limit = 48 * 1024 * 1024


def product(left, right):
    return jnp.dot(left, right, preferred_element_type=jnp.float32)


def contract(left, right, left_dim, right_dim):
    return lax.dot_general(
        left, right, (((left_dim,), (right_dim,)), ((), ())), preferred_element_type=jnp.float32
    )


def call(body, grid, in_specs, out_specs, out_shape, name):
    return pl.pallas_call(
        body,
        grid=grid,
        in_specs=in_specs,
        out_specs=out_specs,
        out_shape=out_shape,
        name=name,
        compiler_params=pltpu.CompilerParams(vmem_limit_bytes=vmem_limit),
    )


def spatial_forward(query, key_value, frame_count):
    model_width, total_rows = query.shape
    head_size = model_width // HEADS
    rows = total_rows // frame_count
    keys = key_value.shape[1] // frame_count
    scale = 1.0 / math.sqrt(head_size)

    def body(q_ref, k_ref, v_ref, out_ref, lse_ref):
        scores = contract(k_ref[...], q_ref[...], 0, 0) * scale
        top = jnp.max(scores, axis=0, keepdims=True)
        weights = jnp.exp(scores - top)
        total = jnp.sum(weights, axis=0, keepdims=True)
        out = product(v_ref[...], weights.astype(jnp.bfloat16))
        out_ref[...] = (out / total).astype(jnp.bfloat16)
        lse_ref[0] = top + jnp.log(total)

    return call(
        body,
        (frame_count, HEADS),
        [
            pl.BlockSpec((head_size, rows), lambda f, h: (h, f)),
            pl.BlockSpec((head_size, keys), lambda f, h: (h, f)),
            pl.BlockSpec((head_size, keys), lambda f, h: (HEADS + h, f)),
        ],
        [
            pl.BlockSpec((head_size, rows), lambda f, h: (h, f)),
            pl.BlockSpec((1, 1, rows), lambda f, h: (f * HEADS + h, 0, 0)),
        ],
        [
            jax.ShapeDtypeStruct(query.shape, jnp.bfloat16),
            jax.ShapeDtypeStruct((frame_count * HEADS, 1, rows), jnp.float32),
        ],
        "spatial_forward",
    )(query, key_value, key_value)


def spatial_backward(query, key_value, log_total, upstream, frame_count, frame):
    model_width, total_rows = query.shape
    head_size = model_width // HEADS
    rows = total_rows // frame_count
    keys = key_value.shape[1] // frame_count
    scale = 1.0 / math.sqrt(head_size)

    def body(q_ref, k_ref, v_ref, lse_ref, up_ref, dq_ref, dkv_ref):
        query_head, key_head, up_head = (q_ref[...], k_ref[...], up_ref[...])
        probs = jnp.exp(contract(key_head, query_head, 0, 0) * scale - lse_ref[0])
        dkv_ref[1] = contract(up_head, probs.astype(jnp.bfloat16), 1, 1).astype(jnp.bfloat16)
        prob_grad = contract(v_ref[...], up_head, 0, 0)
        delta = jnp.sum(probs * prob_grad, axis=0, keepdims=True)
        score_grad = (probs * (prob_grad - delta)).astype(jnp.bfloat16)
        dq_ref[...] = (product(key_head, score_grad) * scale).astype(jnp.bfloat16)
        dkv_ref[0] = (contract(query_head, score_grad, 1, 1) * scale).astype(jnp.bfloat16)

    query_grad, pair_grad = call(
        body,
        (HEADS,),
        [
            pl.BlockSpec((head_size, rows), lambda h: (h, frame)),
            pl.BlockSpec((head_size, keys), lambda h: (h, frame)),
            pl.BlockSpec((head_size, keys), lambda h: (HEADS + h, frame)),
            pl.BlockSpec((1, 1, rows), lambda h: (frame * HEADS + h, 0, 0)),
            pl.BlockSpec((head_size, rows), lambda h: (h, frame)),
        ],
        [
            pl.BlockSpec((head_size, rows), lambda h: (h, 0)),
            pl.BlockSpec((2, head_size, keys), lambda h: (0, h, 0)),
        ],
        [
            jax.ShapeDtypeStruct((model_width, rows), jnp.bfloat16),
            jax.ShapeDtypeStruct((2, model_width, keys), jnp.bfloat16),
        ],
        "spatial_backward",
    )(query, key_value, key_value, log_total, upstream)
    return (query_grad, pair_grad.reshape(2 * model_width, keys))


def cross_probs_of(length_ref, q_ref, k_ref, scale):
    scores = contract(k_ref[...], q_ref[...], 0, 0) * scale
    live = lax.broadcasted_iota(jnp.int32, scores.shape, 0) < length_ref[0]
    scores = jnp.where(live, scores, masked_fill)
    weights = jnp.exp(scores - jnp.max(scores, axis=0, keepdims=True))
    return weights / jnp.sum(weights, axis=0, keepdims=True)


def cross_forward(length, query, text_pair):
    model_width, total_rows = query.shape
    head_size = model_width // HEADS
    keys = text_pair.shape[1]
    scale = 1.0 / math.sqrt(head_size)

    def body(length_ref, q_ref, k_ref, v_ref, out_ref):
        probs = cross_probs_of(length_ref, q_ref, k_ref, scale)
        out_ref[...] = product(v_ref[...], probs.astype(jnp.bfloat16)).astype(jnp.bfloat16)

    return call(
        body,
        (HEADS,),
        [
            pl.BlockSpec(memory_space=pltpu.SMEM),
            pl.BlockSpec((head_size, total_rows), lambda h: (h, 0)),
            pl.BlockSpec((head_size, keys), lambda h: (h, 0)),
            pl.BlockSpec((head_size, keys), lambda h: (HEADS + h, 0)),
        ],
        pl.BlockSpec((head_size, total_rows), lambda h: (h, 0)),
        jax.ShapeDtypeStruct(query.shape, jnp.bfloat16),
        "cross_forward",
    )(length, query, text_pair, text_pair)


def cross_backward(length, query, text_pair, upstream):
    model_width, total_rows = query.shape
    head_size = model_width // HEADS
    keys = text_pair.shape[1]
    scale = 1.0 / math.sqrt(head_size)

    def body(length_ref, q_ref, k_ref, v_ref, up_ref, dq_ref, dkv_ref):
        up_head = up_ref[...]
        probs = cross_probs_of(length_ref, q_ref, k_ref, scale)
        prob_grad = contract(v_ref[...], up_head, 0, 0)
        delta = jnp.sum(probs * prob_grad, axis=0, keepdims=True)
        score_grad = (probs * (prob_grad - delta)).astype(jnp.bfloat16)
        dq_ref[...] = (product(k_ref[...], score_grad) * scale).astype(jnp.bfloat16)
        dkv_ref[0] = contract(q_ref[...], score_grad, 1, 1) * scale
        dkv_ref[1] = contract(up_head, probs.astype(jnp.bfloat16), 1, 1)

    query_grad, pair_grad = call(
        body,
        (HEADS,),
        [
            pl.BlockSpec(memory_space=pltpu.SMEM),
            pl.BlockSpec((head_size, total_rows), lambda h: (h, 0)),
            pl.BlockSpec((head_size, keys), lambda h: (h, 0)),
            pl.BlockSpec((head_size, keys), lambda h: (HEADS + h, 0)),
            pl.BlockSpec((head_size, total_rows), lambda h: (h, 0)),
        ],
        [
            pl.BlockSpec((head_size, total_rows), lambda h: (h, 0)),
            pl.BlockSpec((2, head_size, keys), lambda h: (0, h, 0)),
        ],
        [
            jax.ShapeDtypeStruct(query.shape, jnp.bfloat16),
            jax.ShapeDtypeStruct((2, model_width, keys), jnp.float32),
        ],
        "cross_backward",
    )(length, query, text_pair, text_pair, upstream)
    return (query_grad, pair_grad.reshape(text_pair.shape))


def temporal_probs_of(live_ref, query_frame, key_frames, frame, scale):
    scores = []
    for index in range(3):
        score = jnp.sum(query_frame * key_frames[index], axis=0, keepdims=True) * scale
        if index != 1:
            score = jnp.where(live_ref[frame, index // 2] != 0, score, masked_fill)
        scores.append(score)
    top = jnp.maximum(jnp.maximum(scores[0], scores[1]), scores[2])
    weights = [jnp.exp(score - top) for score in scores]
    inverse = 1.0 / (weights[0] + weights[1] + weights[2])
    return [weight * inverse for weight in weights]


def temporal_forward(live, query, key_value, frame_count):
    model_width, total_rows = query.shape
    head_size = model_width // HEADS
    rows = total_rows // frame_count
    extended_rows = key_value.shape[1]
    scale = 1.0 / math.sqrt(head_size)

    def body(live_ref, q_ref, k_ref, v_ref, out_ref):
        for frame in range(frame_count):
            query_frame = q_ref[:, frame * rows : (frame + 1) * rows].astype(jnp.float32)
            spans = [slice((frame + j) * rows, (frame + j + 1) * rows) for j in range(3)]
            key_frames = [k_ref[:, span].astype(jnp.float32) for span in spans]
            probs = temporal_probs_of(live_ref, query_frame, key_frames, frame, scale)
            mixed = sum(
                prob * v_ref[:, span].astype(jnp.float32) for prob, span in zip(probs, spans)
            )
            out_ref[:, frame * rows : (frame + 1) * rows] = mixed.astype(jnp.bfloat16)

    return call(
        body,
        (HEADS,),
        [
            pl.BlockSpec(memory_space=pltpu.SMEM),
            pl.BlockSpec((head_size, total_rows), lambda h: (h, 0)),
            pl.BlockSpec((head_size, extended_rows), lambda h: (h, 0)),
            pl.BlockSpec((head_size, extended_rows), lambda h: (HEADS + h, 0)),
        ],
        pl.BlockSpec((head_size, total_rows), lambda h: (h, 0)),
        jax.ShapeDtypeStruct(query.shape, jnp.bfloat16),
        "temporal_forward",
    )(live, query, key_value, key_value)


def temporal_backward(live, query, key_value, upstream, frame_count):
    model_width, total_rows = query.shape
    head_size = model_width // HEADS
    rows = total_rows // frame_count
    extended_rows = key_value.shape[1]
    scale = 1.0 / math.sqrt(head_size)

    def body(live_ref, q_ref, k_ref, v_ref, up_ref, dq_ref, dkv_ref):
        key_sums = [None] * (frame_count + 2)
        value_sums = [None] * (frame_count + 2)
        for frame in range(frame_count):
            own = slice(frame * rows, (frame + 1) * rows)
            query_frame = q_ref[:, own].astype(jnp.float32)
            up_frame = up_ref[:, own]
            spans = [slice((frame + j) * rows, (frame + j + 1) * rows) for j in range(3)]
            key_frames = [k_ref[:, span].astype(jnp.float32) for span in spans]
            probs = temporal_probs_of(live_ref, query_frame, key_frames, frame, scale)
            prob_grads = [
                jnp.sum(up_frame * v_ref[:, span].astype(jnp.float32), axis=0, keepdims=True)
                for span in spans
            ]
            delta = sum(prob * grad for prob, grad in zip(probs, prob_grads))
            score_grads = [
                prob * (grad - delta) * scale for prob, grad in zip(probs, prob_grads)
            ]
            dq_ref[:, own] = sum(
                grad * key_frame for grad, key_frame in zip(score_grads, key_frames)
            ).astype(jnp.bfloat16)
            for j in range(3):
                key_part = score_grads[j] * query_frame
                value_part = probs[j] * up_frame
                at = frame + j
                key_sums[at] = key_part if key_sums[at] is None else key_sums[at] + key_part
                value_sums[at] = (
                    value_part if value_sums[at] is None else value_sums[at] + value_part
                )
        for at in range(frame_count + 2):
            dkv_ref[0, :, at * rows : (at + 1) * rows] = key_sums[at].astype(jnp.bfloat16)
            dkv_ref[1, :, at * rows : (at + 1) * rows] = value_sums[at].astype(jnp.bfloat16)

    query_grad, pair_grad = call(
        body,
        (HEADS,),
        [
            pl.BlockSpec(memory_space=pltpu.SMEM),
            pl.BlockSpec((head_size, total_rows), lambda h: (h, 0)),
            pl.BlockSpec((head_size, extended_rows), lambda h: (h, 0)),
            pl.BlockSpec((head_size, extended_rows), lambda h: (HEADS + h, 0)),
            pl.BlockSpec((head_size, total_rows), lambda h: (h, 0)),
        ],
        [
            pl.BlockSpec((head_size, total_rows), lambda h: (h, 0)),
            pl.BlockSpec((2, head_size, extended_rows), lambda h: (0, h, 0)),
        ],
        [
            jax.ShapeDtypeStruct(query.shape, jnp.bfloat16),
            jax.ShapeDtypeStruct((2, model_width, extended_rows), jnp.bfloat16),
        ],
        "temporal_backward",
    )(live, query, key_value, key_value, upstream)
    return (query_grad, pair_grad.reshape(key_value.shape))


def normalize(values):
    centred = values - jnp.mean(values, axis=-1, keepdims=True)
    reciprocal = lax.rsqrt(jnp.mean(centred * centred, axis=-1, keepdims=True) + epsilon)
    return (centred * reciprocal, reciprocal)


def normalize_back(upstream, normed, reciprocal):
    return reciprocal * (
        upstream
        - jnp.mean(upstream, axis=-1, keepdims=True)
        - normed * jnp.mean(upstream * normed, axis=-1, keepdims=True)
    )


def gelu_tanh(values):
    return jax.nn.gelu(values, approximate=True)


def gather_halves(is_first, lower, upper):
    return lax.all_gather(
        jnp.where(is_first, lower, upper), ("bucket", "frame", "seq"), axis=0, tiled=True
    )


def tree_bits():
    return [
        (axis, step)
        for axis in ("frame", "seq")
        for step in reversed(range(lax.axis_size(axis).bit_length() - 1))
    ]


def tree_order(turn):
    bits = tree_bits()
    last = bits[0]
    first = [bit for bit in bits[::-1] if bit != last]
    turn = turn % len(first)
    return first[turn:] + first[:turn] + [last]


def column_halves(value):
    middle = value.shape[1] // 2
    return (value[:, :middle], value[:, middle:])


def my_bit(bit):
    return (lax.axis_index(bit[0]) >> bit[1]) & 1


def across(value, bit):
    axis, step = bit
    return lax.ppermute(
        value, axis, [(i, i ^ (1 << step)) for i in range(lax.axis_size(axis))]
    )


def gather_tree(value):
    for bit in tree_bits()[::-1]:
        other = across(value, bit)
        mine = my_bit(bit) == 0
        value = jnp.concatenate(
            [jnp.where(mine, value, other), jnp.where(mine, other, value)], axis=0
        )
    return value


class Chain:
    def __init__(self, is_first, pair, turn):
        self.order = tree_order(turn)
        self.dims = tree_bits()
        self.is_first = is_first
        self.received = None
        if len(pair) == 2:
            lower, upper = pair
            self.kept = jnp.where(is_first, lower, upper)
            self.received = swapped(jnp.where(is_first, upper, lower))
        else:
            self.kept = pair[0]

    def advance(self):
        value = self.kept
        if self.received is not None:
            value = (
                value.astype(jnp.float32) + self.received.astype(jnp.float32)
            ).astype(value.dtype)
        if self.dims and value.ndim == 2:
            count = 1 << len(self.dims)
            value = value.reshape(
                (2,) * len(self.dims) + (value.shape[0] // count, value.shape[1])
            )
        if self.order:
            bit = self.order.pop(0)
            dim = self.dims.index(bit)
            self.dims.remove(bit)
            index = my_bit(bit)
            self.received = across(
                lax.dynamic_index_in_dim(value, 1 - index, dim, keepdims=False), bit
            )
            self.kept = lax.dynamic_index_in_dim(value, index, dim, keepdims=False)
        else:
            self.kept = value
            self.received = None

    def finish(self):
        while self.received is not None or self.order:
            self.advance()
        return self.kept


def tick(main, chains):
    main, received = lax.optimization_barrier((main, [chain.received for chain in chains]))
    for chain, value in zip(chains, received):
        chain.received = value
        chain.advance()
    return main


def both_of(chain):
    own = chain.finish()
    other = swapped(own)
    return (
        jnp.where(chain.is_first, own, other).astype(jnp.float32),
        jnp.where(chain.is_first, other, own).astype(jnp.float32),
    )


def low(value):
    return value.astype(jnp.bfloat16)


def swapped(value):
    return lax.ppermute(value, "bucket", [(0, 1), (1, 0)])


def per_device(
    latent,
    condition,
    text,
    text_len,
    clip_ids,
    video_flag,
    ada_weight,
    text_kv_weight,
    qkv_weight,
    proj_weight,
    cross_q_weight,
    cross_proj_weight,
    up_weight,
    down_weight,
    temporal_qkv_weight,
    temporal_proj_weight,
    cotangent,
):
    frame_count, row_count, width = (latent.shape[1], latent.shape[2], latent.shape[3])
    total_rows = frame_count * row_count
    seq_size = lax.axis_size("seq")
    frame_size = lax.axis_size("frame")
    shards = seq_size * frame_size
    is_first = lax.axis_index("bucket") == 0
    ff_width = up_weight.shape[1]
    shard_rows = up_weight.shape[0]
    ff_blocks = ff_width // width
    half_ff = ff_width // 2

    shifts = [
        [((i + s) % seq_size, i) for i in range(seq_size)] for s in range(1, seq_size)
    ]
    latent_rest = [lax.ppermute(latent[0], "seq", shift) for shift in shifts]

    gathered_a = gather_halves(
        is_first,
        qkv_weight,
        jnp.concatenate([proj_weight, cross_q_weight, cross_proj_weight], axis=1),
    )
    up_mixed = (
        up_weight.reshape(shard_rows, shards, ff_blocks, shard_rows)
        .transpose(0, 2, 1, 3)
        .reshape(shard_rows, ff_width)
    )
    down_wide = (
        down_weight.reshape(ff_blocks, shard_rows, width)
        .transpose(1, 0, 2)
        .reshape(shard_rows, ff_width)
    )
    gathered_b = gather_halves(
        is_first,
        jnp.concatenate(
            [
                up_mixed[:, :half_ff],
                down_wide[:, :half_ff],
                temporal_qkv_weight[:, :width],
                temporal_proj_weight,
            ],
            axis=1,
        ),
        jnp.concatenate(
            [up_mixed[:, half_ff:], down_wide[:, half_ff:], temporal_qkv_weight[:, width:]],
            axis=1,
        ),
    )

    silu_cond = jax.nn.silu(condition.astype(jnp.float32))
    mod_part = jnp.dot(silu_cond, ada_weight.astype(jnp.float32), precision=highest)
    modulation = gather_tree(mod_part).reshape(9, width)
    text_part = contract(text_kv_weight, text[0], 0, 1).astype(jnp.bfloat16)
    text_pair = gather_tree(text_part)

    inputs = latent[0].reshape(total_rows, width).astype(jnp.float32)
    normed_a, recip_a = normalize(inputs)
    hidden_a = (normed_a * (1.0 + modulation[1]) + modulation[0]).astype(jnp.bfloat16)
    normed_rest = [
        normalize(rest.reshape(total_rows, width).astype(jnp.float32))[0] for rest in latent_rest
    ]
    hidden_rest = [
        (normed * (1.0 + modulation[1]) + modulation[0]).astype(jnp.bfloat16)
        for normed in normed_rest
    ]
    hidden_all = jnp.concatenate(
        [part.reshape(frame_count, row_count, width) for part in [hidden_a] + hidden_rest], axis=1
    ).reshape(frame_count * seq_size * row_count, width)
    hidden_a, hidden_all, text_pair, gathered_a = lax.optimization_barrier(
        (hidden_a, hidden_all, text_pair, gathered_a)
    )
    query_full = gathered_a[:width, :width]
    pair_full = gathered_a[:width, width:]
    proj_full = gathered_a[width:, :width]
    cross_q_full = gathered_a[width:, width : 2 * width]
    cross_proj_full = gathered_a[width:, 2 * width :]
    query = contract(query_full, hidden_a, 0, 1).astype(jnp.bfloat16)
    key_value = contract(pair_full, hidden_all, 0, 1).astype(jnp.bfloat16)
    attended, log_total = spatial_forward(query, key_value, frame_count)
    branch_a = contract(attended, proj_full, 0, 0)
    after_a = inputs + modulation[2] * branch_a
    after_low = after_a.astype(jnp.bfloat16)
    cross_query = contract(cross_q_full, after_low, 0, 1).astype(jnp.bfloat16)
    cross_out = cross_forward(text_len, cross_query, text_pair)
    after_c = after_a + contract(cross_out, cross_proj_full, 0, 0)
    normed_m, recip_m = normalize(after_c)
    hidden_m = (normed_m * (1.0 + modulation[4]) + modulation[3]).astype(jnp.bfloat16)

    up_halves = (gathered_b[:width, :half_ff], gathered_b[width:, :half_ff])
    per_half = ff_blocks // 2
    down_halves = (gathered_b[:width, half_ff:ff_width], gathered_b[width:, half_ff:ff_width])
    down_parts = [
        down_halves[index // per_half][
            :, width * (index % per_half) : width * (index % per_half + 1)
        ]
        for index in range(ff_blocks)
    ]
    tquery_full = gathered_b[:width, ff_width : ff_width + width]
    tproj_full = gathered_b[:width, ff_width + width :]
    tpair_full = gathered_b[width:, ff_width:]

    upward_halves = [product(hidden_m, part) for part in up_halves]
    activated_halves = [gelu_tanh(part).astype(jnp.bfloat16) for part in upward_halves]
    activated_parts = [
        activated_halves[index // per_half][
            :, width * (index % per_half) : width * (index % per_half + 1)
        ]
        for index in range(ff_blocks)
    ]
    branch_m = sum(product(left, right) for left, right in zip(activated_parts, down_parts))
    after_m = after_c + modulation[5] * branch_m
    normed_t, recip_t = normalize(after_m)
    hidden_t = (normed_t * (1.0 + modulation[7]) + modulation[6]).astype(jnp.bfloat16)
    ahead = [(i, i + 1) for i in range(frame_size - 1)]
    back = [(i + 1, i) for i in range(frame_size - 1)]
    hidden_prev = lax.ppermute(hidden_t[total_rows - row_count :], "frame", ahead)
    hidden_next = lax.ppermute(hidden_t[:row_count], "frame", back)
    hidden_ext = jnp.concatenate([hidden_prev, hidden_t, hidden_next], axis=0)
    tquery = contract(tquery_full, hidden_t, 0, 1).astype(jnp.bfloat16)
    tpair = jnp.concatenate(
        [
            low(contract(tpair_full, part, 0, 1))
            for part in (hidden_prev, hidden_t, hidden_next)
        ],
        axis=1,
    )
    first_frame = lax.axis_index("frame") * frame_count
    clips_ext = jnp.concatenate(
        [jnp.full((1,), -1, jnp.int32), clip_ids[0], jnp.full((1,), -1, jnp.int32)]
    )
    clips_local = lax.dynamic_slice_in_dim(clips_ext, first_frame, frame_count + 2)
    live = jnp.stack(
        [clips_local[:-2] == clips_local[1:-1], clips_local[2:] == clips_local[1:-1]], axis=1
    ).astype(jnp.int32)
    flag_local = lax.dynamic_slice_in_dim(video_flag[0], first_frame, frame_count).astype(
        jnp.float32
    )
    mixed = temporal_forward(live, tquery, tpair, frame_count)
    branch_t = contract(mixed, tproj_full, 0, 0)
    flag_rows = jnp.repeat(flag_local, row_count)[:, None]
    result_rows = after_m + flag_rows * modulation[8] * branch_t
    result = result_rows.astype(jnp.bfloat16).reshape(latent.shape)

    result_grad = cotangent[0].reshape(total_rows, width).astype(jnp.float32)
    gate_t_grad = jnp.sum(flag_rows * branch_t * result_grad, axis=0)
    branch_t_grad = (flag_rows * modulation[8] * result_grad).astype(jnp.bfloat16)
    mixed_grad = contract(tproj_full, branch_t_grad, 1, 1)
    tquery_grad, tpair_grad = temporal_backward(live, tquery, tpair, mixed_grad, frame_count)
    halo_prev, halo_next, tpair_grad = lax.optimization_barrier(
        (
            low(contract(tpair_grad[:, :row_count], tpair_full, 0, 1)),
            low(contract(tpair_grad[:, -row_count:], tpair_full, 0, 1)),
            tpair_grad,
        )
    )
    to_prev = lax.ppermute(halo_prev, "frame", back)
    to_next = lax.ppermute(halo_next, "frame", ahead)
    tpair_weight_grad = low(contract(hidden_ext, tpair_grad, 0, 1))
    tquery_weight_grad = low(contract(hidden_t, tquery_grad, 0, 1))
    tproj_weight_grad = low(contract(mixed, branch_t_grad, 1, 0))
    hidden_t_grad = contract(tpair_grad[:, row_count:-row_count], tpair_full, 0, 1) + contract(
        tquery_grad, tquery_full, 0, 1
    )
    hidden_t_grad = jnp.concatenate(
        [
            hidden_t_grad[:row_count] + to_next.astype(jnp.float32),
            hidden_t_grad[row_count : total_rows - row_count],
            hidden_t_grad[total_rows - row_count :] + to_prev.astype(jnp.float32),
        ],
        axis=0,
    )
    hidden_t_grad, tpair_weight_grad, tquery_weight_grad, tproj_weight_grad = (
        lax.optimization_barrier(
            (hidden_t_grad, tpair_weight_grad, tquery_weight_grad, tproj_weight_grad)
        )
    )
    chain_tqk = Chain(is_first, (tquery_weight_grad, tpair_weight_grad[:, :width]), 0)
    chain_tpv = Chain(is_first, (tproj_weight_grad, tpair_weight_grad[:, width:]), 1)
    chains_t = [chain_tqk, chain_tpv]
    grad_m = result_grad + normalize_back(hidden_t_grad * (1.0 + modulation[7]), normed_t, recip_t)
    gate_m_grad = jnp.sum(branch_m * grad_m, axis=0)
    branch_m_grad = low(modulation[5] * grad_m)
    upward_grads = []
    for index in range(2):
        activated_grad = jnp.concatenate(
            [
                contract(branch_m_grad, part, 1, 1)
                for part in down_parts[index * per_half : (index + 1) * per_half]
            ],
            axis=1,
        )
        if index == 0:
            activated_grad = tick(activated_grad, chains_t)
        gelu_back = jax.vjp(gelu_tanh, upward_halves[index])[1]
        upward_grads.append(low(gelu_back(activated_grad)[0]))
    hidden_m_grad = contract(upward_grads[0], up_halves[0], 1, 1) + contract(
        upward_grads[1], up_halves[1], 1, 1
    )
    hidden_m_grad = tick(hidden_m_grad, chains_t)
    up_grads = [low(contract(hidden_m, part, 0, 0)) for part in upward_grads]
    down_grads = [low(contract(part, branch_m_grad, 0, 0)) for part in activated_parts]
    hidden_m_grad, up_grads, down_grads = lax.optimization_barrier(
        (hidden_m_grad, up_grads, down_grads)
    )
    chains_m = [
        Chain(
            is_first,
            (
                up_grads[0][:, width * index : width * (index + 1)],
                up_grads[1][:, width * index : width * (index + 1)],
            ),
            index,
        )
        for index in range(per_half)
    ] + [
        Chain(is_first, (down_grads[index], down_grads[per_half + index]), per_half + index)
        for index in range(per_half)
    ]
    hidden_m_grad = tick(hidden_m_grad, chains_t)
    grad_c = grad_m + normalize_back(hidden_m_grad * (1.0 + modulation[4]), normed_m, recip_m)
    cross_branch_grad = low(grad_c)
    cross_out_grad = low(contract(cross_proj_full, cross_branch_grad, 1, 1))
    cross_out_grad = tick(cross_out_grad, chains_t + chains_m)
    cross_query_grad, text_grad = cross_backward(text_len, cross_query, text_pair, cross_out_grad)
    chain_text = Chain(is_first, (low(text_grad),), 1)
    chain_text.advance()
    grad_a = grad_c + contract(cross_query_grad, cross_q_full, 0, 1)
    gate_a_grad = jnp.sum(branch_a * grad_a, axis=0)
    branch_a_grad = low(modulation[2] * grad_a)
    attended_grad = low(contract(proj_full, branch_a_grad, 1, 1))
    attended_grad = tick(attended_grad, chains_t + [chain_text])
    proj_grad = low(contract(attended, branch_a_grad, 1, 0))
    cross_q_grad = low(contract(after_low, cross_query_grad, 0, 1))
    cross_proj_grad = low(contract(cross_out, cross_branch_grad, 1, 0))
    attended_grad, proj_grad, cross_q_grad, cross_proj_grad = lax.optimization_barrier(
        (attended_grad, proj_grad, cross_q_grad, cross_proj_grad)
    )
    chain_pq = Chain(is_first, (proj_grad, cross_q_grad), 2)
    chain_cp = Chain(is_first, column_halves(cross_proj_grad), 1)
    chains_c = [chain_pq, chain_cp, chain_text]
    attended_grad = tick(attended_grad, chains_m + [chain_text])
    query_grads, pair_grads, rest_grads, rest_received = ([], [], [], [])
    for frame in range(frame_count):
        query_grad, pair_grad = spatial_backward(
            query, key_value, log_total, attended_grad, frame_count, frame
        )
        rest_sent = contract(pair_grad[:, row_count:], pair_full, 0, 1)
        rest_low = low(rest_sent)
        pair_grad, rest_low, attended_grad = lax.optimization_barrier(
            (pair_grad, rest_low, attended_grad)
        )
        query_grads.append(query_grad)
        pair_grads.append(pair_grad)
        rest_grads.append(rest_sent)
        rest_received.append(
            [
                lax.ppermute(
                    rest_low[s * row_count : (s + 1) * row_count],
                    "seq",
                    [(j, i) for i, j in shifts[s]],
                )
                for s in range(seq_size - 1)
            ]
        )
        if frame == 0:
            attended_grad = tick(attended_grad, chains_m + chains_c)
        else:
            query_grads, pair_grads, rest_received[frame - 1] = lax.optimization_barrier(
                (query_grads, pair_grads, rest_received[frame - 1])
            )
    query_grad = jnp.concatenate(query_grads, axis=1)
    pair_grad = jnp.concatenate(pair_grads, axis=1)
    query_weight_grad = low(contract(hidden_a, query_grad, 0, 1))
    pair_weight_grad = low(contract(hidden_all, pair_grad, 0, 1))
    query_grad, pair_grads, query_weight_grad, pair_weight_grad = lax.optimization_barrier(
        (query_grad, pair_grads, query_weight_grad, pair_weight_grad)
    )
    chains_a = [
        Chain(is_first, column_halves(part), turn)
        for turn, part in enumerate(
            (query_weight_grad, pair_weight_grad[:, :width], pair_weight_grad[:, width:])
        )
    ]
    query_grad = tick(query_grad, chains_m + chains_c)
    own_grad = jnp.concatenate(
        [contract(part[:, :row_count], pair_full, 0, 1) for part in pair_grads], axis=0
    ) + contract(query_grad, query_full, 0, 1)
    own_grad, rest_received = tick((own_grad, rest_received), chains_a + chains_c)
    shift_a_grad = jnp.sum(own_grad, axis=0)
    scale_a_grad = jnp.sum(own_grad * normed_a, axis=0)
    for frame in range(frame_count):
        for s in range(seq_size - 1):
            rest_rows = rest_grads[frame][s * row_count : (s + 1) * row_count]
            rest_normed = normed_rest[s][frame * row_count : (frame + 1) * row_count]
            shift_a_grad = shift_a_grad + jnp.sum(rest_rows, axis=0)
            scale_a_grad = scale_a_grad + jnp.sum(rest_rows * rest_normed, axis=0)
    hidden_a_grad = own_grad + jnp.concatenate(
        [sum(part.astype(jnp.float32) for part in parts) for parts in rest_received], axis=0
    )
    input_grad = grad_a + normalize_back(hidden_a_grad * (1.0 + modulation[1]), normed_a, recip_a)
    latent_grad = input_grad.reshape(latent.shape)
    mod_grad = jnp.stack(
        [
            shift_a_grad,
            scale_a_grad,
            gate_a_grad,
            jnp.sum(hidden_m_grad, axis=0),
            jnp.sum(hidden_m_grad * normed_m, axis=0),
            gate_m_grad,
            jnp.sum(hidden_t_grad, axis=0),
            jnp.sum(hidden_t_grad * normed_t, axis=0),
            gate_t_grad,
        ]
    ).reshape(shards, 9 * width // shards)
    latent_grad, mod_grad = tick((latent_grad, mod_grad), chains_a)
    mod_slice = Chain(is_first, (mod_grad,), 0).finish()
    text_low = chain_text.finish()
    silu_pair = jnp.concatenate([silu_cond, swapped(silu_cond)], axis=0)
    mod_pair = jnp.concatenate([mod_slice, swapped(mod_slice)], axis=0)
    ada_grad = lax.dot_general(
        silu_pair, mod_pair, (((0,), (0,)), ((), ())), precision=highest
    )
    text_both = jnp.concatenate([text[0], swapped(text[0])], axis=0)
    slice_both = jnp.concatenate([text_low, swapped(text_low)], axis=1)
    text_kv_grad = contract(text_both, slice_both, 0, 1)
    proj_shard, cross_q_shard = both_of(chain_pq)
    cross_proj_shard = jnp.concatenate(both_of(chain_cp), axis=1)
    qkv_shard = jnp.concatenate([part for chain in chains_a for part in both_of(chain)], axis=1)
    tquery_shard, tkey_shard = both_of(chain_tqk)
    tproj_shard, tvalue_shard = both_of(chain_tpv)
    ff_shards = [both_of(chain) for chain in chains_m]
    up_shard = (
        jnp.concatenate(
            [pair[side] for side in range(2) for pair in ff_shards[:per_half]], axis=1
        )
        .reshape(shard_rows, ff_blocks, shards, shard_rows)
        .transpose(0, 2, 1, 3)
        .reshape(shard_rows, ff_width)
    )
    down_shard = jnp.concatenate(
        [pair[side] for side in range(2) for pair in ff_shards[per_half:]], axis=0
    )
    return (
        result,
        latent_grad,
        ada_grad,
        text_kv_grad,
        qkv_shard,
        proj_shard,
        cross_q_shard,
        cross_proj_shard,
        up_shard,
        down_shard,
        jnp.concatenate([tquery_shard, tkey_shard, tvalue_shard], axis=1),
        tproj_shard,
    )


def solution(mesh):
    return jax.shard_map(
        per_device,
        mesh=mesh,
        in_specs=(
            P("bucket", "frame", "seq", None),
            P("bucket", None),
            P("bucket", None, None),
            P("bucket"),
            P("bucket", None),
            P("bucket", None),
            P(None, ("frame", "seq")),
            P(None, ("frame", "seq")),
            P(("frame", "seq"), None),
            P(("frame", "seq"), None),
            P(("frame", "seq"), None),
            P(("frame", "seq"), None),
            P(("frame", "seq"), None),
            P(("frame", "seq"), None),
            P(("frame", "seq"), None),
            P(("frame", "seq"), None),
            P("bucket", "frame", "seq", None),
        ),
        out_specs=(
            P("bucket", "frame", "seq", None),
            P("bucket", "frame", "seq", None),
            P(None, ("frame", "seq")),
            P(None, ("frame", "seq")),
            P(("frame", "seq"), None),
            P(("frame", "seq"), None),
            P(("frame", "seq"), None),
            P(("frame", "seq"), None),
            P(("frame", "seq"), None),
            P(("frame", "seq"), None),
            P(("frame", "seq"), None),
            P(("frame", "seq"), None),
        ),
        check_vma=False,
    )
```

```python
import math

import jax
import jax.numpy as jnp
from jax import lax
from jax.experimental import pallas as pl
from jax.experimental.pallas import tpu as pltpu
from jax.sharding import PartitionSpec as P

HEADS = 16


epsilon = 1e-06
highest = lax.Precision.HIGHEST
masked_fill = -1e30
vmem_limit = 48 * 1024 * 1024


def product(left, right):
    return jnp.dot(left, right, preferred_element_type=jnp.float32)


def contract(left, right, left_dim, right_dim):
    return lax.dot_general(
        left, right, (((left_dim,), (right_dim,)), ((), ())), preferred_element_type=jnp.float32
    )


def call(body, grid, in_specs, out_specs, out_shape, name):
    return pl.pallas_call(
        body,
        grid=grid,
        in_specs=in_specs,
        out_specs=out_specs,
        out_shape=out_shape,
        name=name,
        compiler_params=pltpu.CompilerParams(vmem_limit_bytes=vmem_limit),
    )


def spatial_forward(query, key_value, frame_count):
    model_width, total_rows = query.shape
    head_size = model_width // HEADS
    rows = total_rows // frame_count
    keys = key_value.shape[1] // frame_count
    scale = 1.0 / math.sqrt(head_size)

    def body(q_ref, k_ref, v_ref, out_ref, lse_ref):
        scores = contract(k_ref[...], q_ref[...], 0, 0) * scale
        top = jnp.max(scores, axis=0, keepdims=True)
        weights = jnp.exp(scores - top)
        total = jnp.sum(weights, axis=0, keepdims=True)
        out = product(v_ref[...], weights.astype(jnp.bfloat16))
        out_ref[...] = (out / total).astype(jnp.bfloat16)
        lse_ref[0] = top + jnp.log(total)

    return call(
        body,
        (frame_count, HEADS),
        [
            pl.BlockSpec((head_size, rows), lambda f, h: (h, f)),
            pl.BlockSpec((head_size, keys), lambda f, h: (h, f)),
            pl.BlockSpec((head_size, keys), lambda f, h: (HEADS + h, f)),
        ],
        [
            pl.BlockSpec((head_size, rows), lambda f, h: (h, f)),
            pl.BlockSpec((1, 1, rows), lambda f, h: (f * HEADS + h, 0, 0)),
        ],
        [
            jax.ShapeDtypeStruct(query.shape, jnp.bfloat16),
            jax.ShapeDtypeStruct((frame_count * HEADS, 1, rows), jnp.float32),
        ],
        "spatial_forward",
    )(query, key_value, key_value)


def spatial_backward(query, key_value, log_total, upstream, frame_count, frame):
    model_width, total_rows = query.shape
    head_size = model_width // HEADS
    rows = total_rows // frame_count
    keys = key_value.shape[1] // frame_count
    scale = 1.0 / math.sqrt(head_size)

    def body(q_ref, k_ref, v_ref, lse_ref, up_ref, dq_ref, dkv_ref):
        query_head, key_head, up_head = (q_ref[...], k_ref[...], up_ref[...])
        probs = jnp.exp(contract(key_head, query_head, 0, 0) * scale - lse_ref[0])
        dkv_ref[1] = contract(up_head, probs.astype(jnp.bfloat16), 1, 1).astype(jnp.bfloat16)
        prob_grad = contract(v_ref[...], up_head, 0, 0)
        delta = jnp.sum(probs * prob_grad, axis=0, keepdims=True)
        score_grad = (probs * (prob_grad - delta)).astype(jnp.bfloat16)
        dq_ref[...] = (product(key_head, score_grad) * scale).astype(jnp.bfloat16)
        dkv_ref[0] = (contract(query_head, score_grad, 1, 1) * scale).astype(jnp.bfloat16)

    query_grad, pair_grad = call(
        body,
        (HEADS,),
        [
            pl.BlockSpec((head_size, rows), lambda h: (h, frame)),
            pl.BlockSpec((head_size, keys), lambda h: (h, frame)),
            pl.BlockSpec((head_size, keys), lambda h: (HEADS + h, frame)),
            pl.BlockSpec((1, 1, rows), lambda h: (frame * HEADS + h, 0, 0)),
            pl.BlockSpec((head_size, rows), lambda h: (h, frame)),
        ],
        [
            pl.BlockSpec((head_size, rows), lambda h: (h, 0)),
            pl.BlockSpec((2, head_size, keys), lambda h: (0, h, 0)),
        ],
        [
            jax.ShapeDtypeStruct((model_width, rows), jnp.bfloat16),
            jax.ShapeDtypeStruct((2, model_width, keys), jnp.bfloat16),
        ],
        "spatial_backward",
    )(query, key_value, key_value, log_total, upstream)
    return (query_grad, pair_grad.reshape(2 * model_width, keys))


def cross_probs_of(length_ref, q_ref, k_ref, scale):
    scores = contract(k_ref[...], q_ref[...], 0, 0) * scale
    live = lax.broadcasted_iota(jnp.int32, scores.shape, 0) < length_ref[0]
    scores = jnp.where(live, scores, masked_fill)
    weights = jnp.exp(scores - jnp.max(scores, axis=0, keepdims=True))
    return weights / jnp.sum(weights, axis=0, keepdims=True)


def cross_forward(length, query, text_pair):
    model_width, total_rows = query.shape
    head_size = model_width // HEADS
    keys = text_pair.shape[1]
    scale = 1.0 / math.sqrt(head_size)

    def body(length_ref, q_ref, k_ref, v_ref, out_ref):
        probs = cross_probs_of(length_ref, q_ref, k_ref, scale)
        out_ref[...] = product(v_ref[...], probs.astype(jnp.bfloat16)).astype(jnp.bfloat16)

    return call(
        body,
        (HEADS,),
        [
            pl.BlockSpec(memory_space=pltpu.SMEM),
            pl.BlockSpec((head_size, total_rows), lambda h: (h, 0)),
            pl.BlockSpec((head_size, keys), lambda h: (h, 0)),
            pl.BlockSpec((head_size, keys), lambda h: (HEADS + h, 0)),
        ],
        pl.BlockSpec((head_size, total_rows), lambda h: (h, 0)),
        jax.ShapeDtypeStruct(query.shape, jnp.bfloat16),
        "cross_forward",
    )(length, query, text_pair, text_pair)


def cross_backward(length, query, text_pair, upstream):
    model_width, total_rows = query.shape
    head_size = model_width // HEADS
    keys = text_pair.shape[1]
    scale = 1.0 / math.sqrt(head_size)

    def body(length_ref, q_ref, k_ref, v_ref, up_ref, dq_ref, dkv_ref):
        up_head = up_ref[...]
        probs = cross_probs_of(length_ref, q_ref, k_ref, scale)
        prob_grad = contract(v_ref[...], up_head, 0, 0)
        delta = jnp.sum(probs * prob_grad, axis=0, keepdims=True)
        score_grad = (probs * (prob_grad - delta)).astype(jnp.bfloat16)
        dq_ref[...] = (product(k_ref[...], score_grad) * scale).astype(jnp.bfloat16)
        dkv_ref[0] = contract(q_ref[...], score_grad, 1, 1) * scale
        dkv_ref[1] = contract(up_head, probs.astype(jnp.bfloat16), 1, 1)

    query_grad, pair_grad = call(
        body,
        (HEADS,),
        [
            pl.BlockSpec(memory_space=pltpu.SMEM),
            pl.BlockSpec((head_size, total_rows), lambda h: (h, 0)),
            pl.BlockSpec((head_size, keys), lambda h: (h, 0)),
            pl.BlockSpec((head_size, keys), lambda h: (HEADS + h, 0)),
            pl.BlockSpec((head_size, total_rows), lambda h: (h, 0)),
        ],
        [
            pl.BlockSpec((head_size, total_rows), lambda h: (h, 0)),
            pl.BlockSpec((2, head_size, keys), lambda h: (0, h, 0)),
        ],
        [
            jax.ShapeDtypeStruct(query.shape, jnp.bfloat16),
            jax.ShapeDtypeStruct((2, model_width, keys), jnp.float32),
        ],
        "cross_backward",
    )(length, query, text_pair, text_pair, upstream)
    return (query_grad, pair_grad.reshape(text_pair.shape))


def temporal_probs_of(live_ref, query_frame, key_frames, frame, scale):
    scores = []
    for index in range(3):
        score = jnp.sum(query_frame * key_frames[index], axis=0, keepdims=True) * scale
        if index != 1:
            score = jnp.where(live_ref[frame, index // 2] != 0, score, masked_fill)
        scores.append(score)
    top = jnp.maximum(jnp.maximum(scores[0], scores[1]), scores[2])
    weights = [jnp.exp(score - top) for score in scores]
    inverse = 1.0 / (weights[0] + weights[1] + weights[2])
    return [weight * inverse for weight in weights]


def temporal_forward(live, query, key_value, frame_count):
    model_width, total_rows = query.shape
    head_size = model_width // HEADS
    rows = total_rows // frame_count
    extended_rows = key_value.shape[1]
    scale = 1.0 / math.sqrt(head_size)

    def body(live_ref, q_ref, k_ref, v_ref, out_ref):
        for frame in range(frame_count):
            query_frame = q_ref[:, frame * rows : (frame + 1) * rows].astype(jnp.float32)
            spans = [slice((frame + j) * rows, (frame + j + 1) * rows) for j in range(3)]
            key_frames = [k_ref[:, span].astype(jnp.float32) for span in spans]
            probs = temporal_probs_of(live_ref, query_frame, key_frames, frame, scale)
            mixed = sum(
                prob * v_ref[:, span].astype(jnp.float32) for prob, span in zip(probs, spans)
            )
            out_ref[:, frame * rows : (frame + 1) * rows] = mixed.astype(jnp.bfloat16)

    return call(
        body,
        (HEADS,),
        [
            pl.BlockSpec(memory_space=pltpu.SMEM),
            pl.BlockSpec((head_size, total_rows), lambda h: (h, 0)),
            pl.BlockSpec((head_size, extended_rows), lambda h: (h, 0)),
            pl.BlockSpec((head_size, extended_rows), lambda h: (HEADS + h, 0)),
        ],
        pl.BlockSpec((head_size, total_rows), lambda h: (h, 0)),
        jax.ShapeDtypeStruct(query.shape, jnp.bfloat16),
        "temporal_forward",
    )(live, query, key_value, key_value)


def temporal_backward(live, query, key_value, upstream, frame_count):
    model_width, total_rows = query.shape
    head_size = model_width // HEADS
    rows = total_rows // frame_count
    extended_rows = key_value.shape[1]
    scale = 1.0 / math.sqrt(head_size)

    def body(live_ref, q_ref, k_ref, v_ref, up_ref, dq_ref, dkv_ref):
        key_sums = [None] * (frame_count + 2)
        value_sums = [None] * (frame_count + 2)
        for frame in range(frame_count):
            own = slice(frame * rows, (frame + 1) * rows)
            query_frame = q_ref[:, own].astype(jnp.float32)
            up_frame = up_ref[:, own]
            spans = [slice((frame + j) * rows, (frame + j + 1) * rows) for j in range(3)]
            key_frames = [k_ref[:, span].astype(jnp.float32) for span in spans]
            probs = temporal_probs_of(live_ref, query_frame, key_frames, frame, scale)
            prob_grads = [
                jnp.sum(up_frame * v_ref[:, span].astype(jnp.float32), axis=0, keepdims=True)
                for span in spans
            ]
            delta = sum(prob * grad for prob, grad in zip(probs, prob_grads))
            score_grads = [
                prob * (grad - delta) * scale for prob, grad in zip(probs, prob_grads)
            ]
            dq_ref[:, own] = sum(
                grad * key_frame for grad, key_frame in zip(score_grads, key_frames)
            ).astype(jnp.bfloat16)
            for j in range(3):
                key_part = score_grads[j] * query_frame
                value_part = probs[j] * up_frame
                at = frame + j
                key_sums[at] = key_part if key_sums[at] is None else key_sums[at] + key_part
                value_sums[at] = (
                    value_part if value_sums[at] is None else value_sums[at] + value_part
                )
        for at in range(frame_count + 2):
            dkv_ref[0, :, at * rows : (at + 1) * rows] = key_sums[at].astype(jnp.bfloat16)
            dkv_ref[1, :, at * rows : (at + 1) * rows] = value_sums[at].astype(jnp.bfloat16)

    query_grad, pair_grad = call(
        body,
        (HEADS,),
        [
            pl.BlockSpec(memory_space=pltpu.SMEM),
            pl.BlockSpec((head_size, total_rows), lambda h: (h, 0)),
            pl.BlockSpec((head_size, extended_rows), lambda h: (h, 0)),
            pl.BlockSpec((head_size, extended_rows), lambda h: (HEADS + h, 0)),
            pl.BlockSpec((head_size, total_rows), lambda h: (h, 0)),
        ],
        [
            pl.BlockSpec((head_size, total_rows), lambda h: (h, 0)),
            pl.BlockSpec((2, head_size, extended_rows), lambda h: (0, h, 0)),
        ],
        [
            jax.ShapeDtypeStruct(query.shape, jnp.bfloat16),
            jax.ShapeDtypeStruct((2, model_width, extended_rows), jnp.bfloat16),
        ],
        "temporal_backward",
    )(live, query, key_value, key_value, upstream)
    return (query_grad, pair_grad.reshape(key_value.shape))


def normalize(values):
    centred = values - jnp.mean(values, axis=-1, keepdims=True)
    reciprocal = lax.rsqrt(jnp.mean(centred * centred, axis=-1, keepdims=True) + epsilon)
    return (centred * reciprocal, reciprocal)


def normalize_back(upstream, normed, reciprocal):
    return reciprocal * (
        upstream
        - jnp.mean(upstream, axis=-1, keepdims=True)
        - normed * jnp.mean(upstream * normed, axis=-1, keepdims=True)
    )


def gelu_tanh(values):
    return jax.nn.gelu(values, approximate=True)


def gather_halves(is_first, lower, upper):
    return lax.all_gather(
        jnp.where(is_first, lower, upper), ("bucket", "frame", "seq"), axis=0, tiled=True
    )


def tree_bits():
    return [
        (axis, step)
        for axis in ("frame", "seq")
        for step in reversed(range(lax.axis_size(axis).bit_length() - 1))
    ]


def tree_order(turn):
    bits = tree_bits()
    last = bits[0]
    first = [bit for bit in bits[::-1] if bit != last]
    turn = turn % len(first)
    return first[turn:] + first[:turn] + [last]


def blank(shape):
    return pl.pallas_call(
        lambda out_ref: None,
        out_specs=pl.BlockSpec(memory_space=pl.ANY),
        out_shape=jax.ShapeDtypeStruct(shape, jnp.bfloat16),
        name="blank",
    )()


def stack_halves(lower, upper):
    depth = lower[0].shape[0]
    stacked = blank((2 * depth, sum(part.shape[1] for part in lower)))
    for index, parts in enumerate((lower, upper)):
        column = 0
        for part in parts:
            stacked = lax.dynamic_update_slice(stacked, low(part), (index * depth, column))
            column += part.shape[1]
    return stacked


def scatter_halves(stacked):
    return lax.psum_scatter(stacked, ("bucket", "frame", "seq"), scatter_dimension=0, tiled=True)


def whole_halves(is_first, own):
    other = swapped(own)
    return (
        jnp.where(is_first, own, other).astype(jnp.float32),
        jnp.where(is_first, other, own).astype(jnp.float32),
    )


def my_bit(bit):
    return (lax.axis_index(bit[0]) >> bit[1]) & 1


def across(value, bit):
    axis, step = bit
    return lax.ppermute(
        value, axis, [(i, i ^ (1 << step)) for i in range(lax.axis_size(axis))]
    )


def gather_tree(value):
    for bit in tree_bits()[::-1]:
        other = across(value, bit)
        mine = my_bit(bit) == 0
        value = jnp.concatenate(
            [jnp.where(mine, value, other), jnp.where(mine, other, value)], axis=0
        )
    return value


class Chain:
    def __init__(self, is_first, pair, turn):
        self.order = tree_order(turn)
        self.dims = tree_bits()
        self.is_first = is_first
        self.received = None
        if len(pair) == 2:
            lower, upper = pair
            self.kept = jnp.where(is_first, lower, upper)
            self.received = swapped(jnp.where(is_first, upper, lower))
        else:
            self.kept = pair[0]

    def advance(self):
        value = self.kept
        if self.received is not None:
            value = (
                value.astype(jnp.float32) + self.received.astype(jnp.float32)
            ).astype(value.dtype)
        if self.dims and value.ndim == 2:
            count = 1 << len(self.dims)
            value = value.reshape(
                (2,) * len(self.dims) + (value.shape[0] // count, value.shape[1])
            )
        if self.order:
            bit = self.order.pop(0)
            dim = self.dims.index(bit)
            self.dims.remove(bit)
            index = my_bit(bit)
            self.received = across(
                lax.dynamic_index_in_dim(value, 1 - index, dim, keepdims=False), bit
            )
            self.kept = lax.dynamic_index_in_dim(value, index, dim, keepdims=False)
        else:
            self.kept = value
            self.received = None

    def finish(self):
        while self.received is not None or self.order:
            self.advance()
        return self.kept


def finish_together(chains):
    for chain in chains:
        while len(chain.order) > 1:
            chain.advance()
    first = chains[0]
    parts = [
        low(chain.kept.astype(jnp.float32) + chain.received.astype(jnp.float32))
        for chain in chains
    ]
    bit = first.order[0]
    index = my_bit(bit)
    kept = [lax.dynamic_index_in_dim(part, index, 0, keepdims=False) for part in parts]
    sent = [lax.dynamic_index_in_dim(part, 1 - index, 0, keepdims=False) for part in parts]
    received = across(jnp.concatenate(sent, axis=1), bit)
    own = jnp.concatenate(kept, axis=1).astype(jnp.float32) + received.astype(jnp.float32)
    return whole_halves(first.is_first, low(own))


def tick(main, chains):
    main, received = lax.optimization_barrier((main, [chain.received for chain in chains]))
    for chain, value in zip(chains, received):
        chain.received = value
        chain.advance()
    return main


def low(value):
    return value.astype(jnp.bfloat16)


def swapped(value):
    return lax.ppermute(value, "bucket", [(0, 1), (1, 0)])


def per_device(
    latent,
    condition,
    text,
    text_len,
    clip_ids,
    video_flag,
    ada_weight,
    text_kv_weight,
    qkv_weight,
    proj_weight,
    cross_q_weight,
    cross_proj_weight,
    up_weight,
    down_weight,
    temporal_qkv_weight,
    temporal_proj_weight,
    cotangent,
):
    frame_count, row_count, width = (latent.shape[1], latent.shape[2], latent.shape[3])
    total_rows = frame_count * row_count
    seq_size = lax.axis_size("seq")
    frame_size = lax.axis_size("frame")
    shards = seq_size * frame_size
    is_first = lax.axis_index("bucket") == 0
    ff_width = up_weight.shape[1]
    shard_rows = up_weight.shape[0]
    ff_blocks = ff_width // width
    half_ff = ff_width // 2

    shifts = [
        [((i + s) % seq_size, i) for i in range(seq_size)] for s in range(1, seq_size)
    ]
    latent_rest = [lax.ppermute(latent[0], "seq", shift) for shift in shifts]

    gathered_a = gather_halves(
        is_first,
        qkv_weight,
        jnp.concatenate([proj_weight, cross_q_weight, cross_proj_weight], axis=1),
    )
    up_mixed = (
        up_weight.reshape(shard_rows, shards, ff_blocks, shard_rows)
        .transpose(0, 2, 1, 3)
        .reshape(shard_rows, ff_width)
    )
    down_wide = (
        down_weight.reshape(ff_blocks, shard_rows, width)
        .transpose(1, 0, 2)
        .reshape(shard_rows, ff_width)
    )
    gathered_b = gather_halves(
        is_first,
        jnp.concatenate([up_mixed[:, :half_ff], down_wide[:, :half_ff]], axis=1),
        jnp.concatenate([up_mixed[:, half_ff:], down_wide[:, half_ff:]], axis=1),
    )

    silu_cond = jax.nn.silu(condition.astype(jnp.float32))
    mod_part = jnp.dot(silu_cond, ada_weight.astype(jnp.float32), precision=highest)
    modulation = gather_tree(mod_part).reshape(9, width)
    text_part = contract(text_kv_weight, text[0], 0, 1).astype(jnp.bfloat16)
    text_pair = gather_tree(text_part)

    inputs = latent[0].reshape(total_rows, width).astype(jnp.float32)
    normed_a, recip_a = normalize(inputs)
    hidden_a = (normed_a * (1.0 + modulation[1]) + modulation[0]).astype(jnp.bfloat16)
    normed_rest = [
        normalize(rest.reshape(total_rows, width).astype(jnp.float32))[0] for rest in latent_rest
    ]
    hidden_rest = [
        (normed * (1.0 + modulation[1]) + modulation[0]).astype(jnp.bfloat16)
        for normed in normed_rest
    ]
    hidden_all = jnp.concatenate(
        [part.reshape(frame_count, row_count, width) for part in [hidden_a] + hidden_rest], axis=1
    ).reshape(frame_count * seq_size * row_count, width)
    hidden_a, hidden_all, text_pair, gathered_a = lax.optimization_barrier(
        (hidden_a, hidden_all, text_pair, gathered_a)
    )
    query_full = gathered_a[:width, :width]
    pair_full = gathered_a[:width, width:]
    proj_full = gathered_a[width:, :width]
    cross_q_full = gathered_a[width:, width : 2 * width]
    cross_proj_full = gathered_a[width:, 2 * width :]
    query = contract(query_full, hidden_a, 0, 1).astype(jnp.bfloat16)
    key_value = contract(pair_full, hidden_all, 0, 1).astype(jnp.bfloat16)
    attended, log_total = spatial_forward(query, key_value, frame_count)
    branch_a = contract(attended, proj_full, 0, 0)
    after_a = inputs + modulation[2] * branch_a
    after_low = after_a.astype(jnp.bfloat16)
    cross_query = contract(cross_q_full, after_low, 0, 1).astype(jnp.bfloat16)
    cross_out = cross_forward(text_len, cross_query, text_pair)
    after_c = after_a + contract(cross_out, cross_proj_full, 0, 0)
    normed_m, recip_m = normalize(after_c)
    hidden_m = (normed_m * (1.0 + modulation[4]) + modulation[3]).astype(jnp.bfloat16)

    temporal_lower, temporal_upper = lax.optimization_barrier(
        (
            jnp.concatenate([temporal_qkv_weight[:, :width], temporal_proj_weight], axis=1),
            temporal_qkv_weight[:, width:],
            query,
        )
    )[:2]
    gathered_c = gather_halves(is_first, temporal_lower, temporal_upper)
    up_halves = (gathered_b[:width, :half_ff], gathered_b[width:, :half_ff])
    per_half = ff_blocks // 2
    down_halves = (gathered_b[:width, half_ff:ff_width], gathered_b[width:, half_ff:ff_width])
    down_parts = [
        down_halves[index // per_half][
            :, width * (index % per_half) : width * (index % per_half + 1)
        ]
        for index in range(ff_blocks)
    ]
    tquery_full = gathered_c[:width, :width]
    tproj_full = gathered_c[:width, width:]
    tpair_full = gathered_c[width:]

    upward_halves = [product(hidden_m, part) for part in up_halves]
    activated_halves = [gelu_tanh(part).astype(jnp.bfloat16) for part in upward_halves]
    activated_parts = [
        activated_halves[index // per_half][
            :, width * (index % per_half) : width * (index % per_half + 1)
        ]
        for index in range(ff_blocks)
    ]
    branch_m = sum(product(left, right) for left, right in zip(activated_parts, down_parts))
    after_m = after_c + modulation[5] * branch_m
    normed_t, recip_t = normalize(after_m)
    hidden_t = (normed_t * (1.0 + modulation[7]) + modulation[6]).astype(jnp.bfloat16)
    ahead = [(i, i + 1) for i in range(frame_size - 1)]
    back = [(i + 1, i) for i in range(frame_size - 1)]
    hidden_prev = lax.ppermute(hidden_t[total_rows - row_count :], "frame", ahead)
    hidden_next = lax.ppermute(hidden_t[:row_count], "frame", back)
    hidden_ext = jnp.concatenate([hidden_prev, hidden_t, hidden_next], axis=0)
    tquery = contract(tquery_full, hidden_t, 0, 1).astype(jnp.bfloat16)
    tpair = low(contract(tpair_full, hidden_ext, 0, 1))
    first_frame = lax.axis_index("frame") * frame_count
    clips_ext = jnp.concatenate(
        [jnp.full((1,), -1, jnp.int32), clip_ids[0], jnp.full((1,), -1, jnp.int32)]
    )
    clips_local = lax.dynamic_slice_in_dim(clips_ext, first_frame, frame_count + 2)
    live = jnp.stack(
        [clips_local[:-2] == clips_local[1:-1], clips_local[2:] == clips_local[1:-1]], axis=1
    ).astype(jnp.int32)
    flag_local = lax.dynamic_slice_in_dim(video_flag[0], first_frame, frame_count).astype(
        jnp.float32
    )
    mixed = temporal_forward(live, tquery, tpair, frame_count)
    branch_t = contract(mixed, tproj_full, 0, 0)
    flag_rows = jnp.repeat(flag_local, row_count)[:, None]
    result_rows = after_m + flag_rows * modulation[8] * branch_t
    result = result_rows.astype(jnp.bfloat16).reshape(latent.shape)

    result_grad = cotangent[0].reshape(total_rows, width).astype(jnp.float32)
    gate_t_grad = jnp.sum(flag_rows * branch_t * result_grad, axis=0)
    branch_t_grad = (flag_rows * modulation[8] * result_grad).astype(jnp.bfloat16)
    mixed_grad = contract(tproj_full, branch_t_grad, 1, 1)
    tquery_grad, tpair_grad = temporal_backward(live, tquery, tpair, mixed_grad, frame_count)
    halo_prev, halo_next, tpair_grad = lax.optimization_barrier(
        (
            low(contract(tpair_grad[:, :row_count], tpair_full, 0, 1)),
            low(contract(tpair_grad[:, -row_count:], tpair_full, 0, 1)),
            tpair_grad,
        )
    )
    to_prev = lax.ppermute(halo_prev, "frame", back)
    to_next = lax.ppermute(halo_next, "frame", ahead)
    stacked_c = stack_halves(
        [contract(hidden_t, tquery_grad, 0, 1), contract(mixed, branch_t_grad, 1, 0)],
        [contract(hidden_ext, tpair_grad, 0, 1)],
    )
    hidden_t_grad = contract(tpair_grad[:, row_count:-row_count], tpair_full, 0, 1) + contract(
        tquery_grad, tquery_full, 0, 1
    )
    hidden_t_grad = jnp.concatenate(
        [
            hidden_t_grad[:row_count] + to_next.astype(jnp.float32),
            hidden_t_grad[row_count : total_rows - row_count],
            hidden_t_grad[total_rows - row_count :] + to_prev.astype(jnp.float32),
        ],
        axis=0,
    )
    hidden_t_grad, stacked_c = lax.optimization_barrier((hidden_t_grad, stacked_c))
    scattered_c = scatter_halves(stacked_c)
    grad_m = result_grad + normalize_back(hidden_t_grad * (1.0 + modulation[7]), normed_t, recip_t)
    gate_m_grad = jnp.sum(branch_m * grad_m, axis=0)
    branch_m_grad = low(modulation[5] * grad_m)
    upward_grads = []
    for index in range(2):
        activated_grad = jnp.concatenate(
            [
                contract(branch_m_grad, part, 1, 1)
                for part in down_parts[index * per_half : (index + 1) * per_half]
            ],
            axis=1,
        )
        gelu_back = jax.vjp(gelu_tanh, upward_halves[index])[1]
        upward_grads.append(low(gelu_back(activated_grad)[0]))
    hidden_m_grad = contract(upward_grads[0], up_halves[0], 1, 1) + contract(
        upward_grads[1], up_halves[1], 1, 1
    )
    up_grads = [contract(hidden_m, part, 0, 0) for part in upward_grads]
    down_grads = [contract(part, branch_m_grad, 0, 0) for part in activated_parts]
    stacked_b = stack_halves(
        [up_grads[0]] + down_grads[:per_half], [up_grads[1]] + down_grads[per_half:]
    )
    hidden_m_grad, stacked_b = lax.optimization_barrier((hidden_m_grad, stacked_b))
    grad_c = grad_m + normalize_back(hidden_m_grad * (1.0 + modulation[4]), normed_m, recip_m)
    cross_branch_grad = low(grad_c)
    cross_out_grad = low(contract(cross_proj_full, cross_branch_grad, 1, 1))
    cross_query_grad, text_grad = cross_backward(text_len, cross_query, text_pair, cross_out_grad)
    chain_text = Chain(is_first, (low(text_grad),), 1)
    chain_text.advance()
    grad_a = grad_c + contract(cross_query_grad, cross_q_full, 0, 1)
    gate_a_grad = jnp.sum(branch_a * grad_a, axis=0)
    branch_a_grad = low(modulation[2] * grad_a)
    attended_grad = low(contract(proj_full, branch_a_grad, 1, 1))
    attended_grad, scattered_c, stacked_b = lax.optimization_barrier(
        (attended_grad, scattered_c, stacked_b)
    )
    scattered_b = scatter_halves(stacked_b)
    attended_grad = tick(attended_grad, [chain_text])
    proj_grad = low(contract(attended, branch_a_grad, 1, 0))
    cross_q_grad = low(contract(after_low, cross_query_grad, 0, 1))
    cross_proj_grad = low(contract(cross_out, cross_branch_grad, 1, 0))
    attended_grad, proj_grad, cross_q_grad, cross_proj_grad = lax.optimization_barrier(
        (attended_grad, proj_grad, cross_q_grad, cross_proj_grad)
    )
    query_grads, pair_grads, rest_grads, rest_received = ([], [], [], [])
    for frame in range(frame_count):
        query_grad, pair_grad = spatial_backward(
            query, key_value, log_total, attended_grad, frame_count, frame
        )
        rest_sent = contract(pair_grad[:, row_count:], pair_full, 0, 1)
        rest_low = low(rest_sent)
        pair_grad, rest_low, attended_grad = lax.optimization_barrier(
            (pair_grad, rest_low, attended_grad)
        )
        query_grads.append(query_grad)
        pair_grads.append(pair_grad)
        rest_grads.append(rest_sent)
        rest_received.append(
            [
                lax.ppermute(
                    rest_low[s * row_count : (s + 1) * row_count],
                    "seq",
                    [(j, i) for i, j in shifts[s]],
                )
                for s in range(seq_size - 1)
            ]
        )
        if frame == 0:
            attended_grad = tick(attended_grad, [chain_text])
        else:
            query_grads, pair_grads, rest_received[frame - 1] = lax.optimization_barrier(
                (query_grads, pair_grads, rest_received[frame - 1])
            )
    query_grad = jnp.concatenate(query_grads, axis=1)
    pair_grad = jnp.concatenate(pair_grads, axis=1)
    query_weight_grad = low(contract(hidden_a, query_grad, 0, 1))
    pair_weight_grad = low(contract(hidden_all, pair_grad, 0, 1))
    query_grad, pair_grads, query_weight_grad, pair_weight_grad = lax.optimization_barrier(
        (query_grad, pair_grads, query_weight_grad, pair_weight_grad)
    )
    chains_a = [
        Chain(is_first, pair, turn)
        for turn, pair in enumerate(
            (
                (pair_weight_grad[:, width:], cross_proj_grad),
                (query_weight_grad, proj_grad),
                (pair_weight_grad[:, :width], cross_q_grad),
            )
        )
    ]
    pair_own = jnp.concatenate(
        [contract(part[:, :row_count], pair_full, 0, 1) for part in pair_grads], axis=0
    )
    pair_own = tick(pair_own, chains_a + [chain_text])
    own_grad = pair_own + contract(query_grad, query_full, 0, 1)
    shift_a_grad = jnp.sum(own_grad, axis=0)
    scale_a_grad = jnp.sum(own_grad * normed_a, axis=0)
    for frame in range(frame_count):
        for s in range(seq_size - 1):
            rest_rows = rest_grads[frame][s * row_count : (s + 1) * row_count]
            rest_normed = normed_rest[s][frame * row_count : (frame + 1) * row_count]
            shift_a_grad = shift_a_grad + jnp.sum(rest_rows, axis=0)
            scale_a_grad = scale_a_grad + jnp.sum(rest_rows * rest_normed, axis=0)
    shift_a_grad, scale_a_grad, rest_received = lax.optimization_barrier(
        (shift_a_grad, scale_a_grad, rest_received)
    )
    hidden_a_grad = own_grad + jnp.concatenate(
        [sum(part.astype(jnp.float32) for part in parts) for parts in rest_received], axis=0
    )
    input_grad = grad_a + normalize_back(hidden_a_grad * (1.0 + modulation[1]), normed_a, recip_a)
    latent_grad = input_grad.reshape(latent.shape)
    mod_grad = jnp.stack(
        [
            shift_a_grad,
            scale_a_grad,
            gate_a_grad,
            jnp.sum(hidden_m_grad, axis=0),
            jnp.sum(hidden_m_grad * normed_m, axis=0),
            gate_m_grad,
            jnp.sum(hidden_t_grad, axis=0),
            jnp.sum(hidden_t_grad * normed_t, axis=0),
            gate_t_grad,
        ]
    ).reshape(shards, 9 * width // shards)
    latent_grad, mod_grad = tick((latent_grad, mod_grad), chains_a)
    mod_slice = Chain(is_first, (mod_grad,), 0).finish()
    text_low = chain_text.finish()
    silu_pair = jnp.concatenate([silu_cond, swapped(silu_cond)], axis=0)
    mod_pair = jnp.concatenate([mod_slice, swapped(mod_slice)], axis=0)
    ada_grad = lax.dot_general(
        silu_pair, mod_pair, (((0,), (0,)), ((), ())), precision=highest
    )
    text_both = jnp.concatenate([text[0], swapped(text[0])], axis=0)
    slice_both = jnp.concatenate([text_low, swapped(text_low)], axis=1)
    text_kv_grad = contract(text_both, slice_both, 0, 1)
    lower_a, upper_a = finish_together(chains_a)
    lower_b, upper_b = whole_halves(is_first, scattered_b)
    lower_c, upper_c = whole_halves(is_first, scattered_c)
    up_shard = (
        jnp.concatenate([lower_b[:, :half_ff], upper_b[:, :half_ff]], axis=1)
        .reshape(shard_rows, ff_blocks, shards, shard_rows)
        .transpose(0, 2, 1, 3)
        .reshape(shard_rows, ff_width)
    )
    down_shard = jnp.concatenate(
        [
            half[:, half_ff + width * index : half_ff + width * (index + 1)]
            for half in (lower_b, upper_b)
            for index in range(per_half)
        ],
        axis=0,
    )
    return (
        result,
        latent_grad,
        ada_grad,
        text_kv_grad,
        jnp.concatenate([lower_a[:, width : 2 * width], lower_a[:, 2 * width :], lower_a[:, :width]], axis=1),
        upper_a[:, width : 2 * width],
        upper_a[:, 2 * width :],
        upper_a[:, :width],
        up_shard,
        down_shard,
        jnp.concatenate([lower_c[:, :width], upper_c], axis=1),
        lower_c[:, width:],
    )


def solution(mesh):
    return jax.shard_map(
        per_device,
        mesh=mesh,
        in_specs=(
            P("bucket", "frame", "seq", None),
            P("bucket", None),
            P("bucket", None, None),
            P("bucket"),
            P("bucket", None),
            P("bucket", None),
            P(None, ("frame", "seq")),
            P(None, ("frame", "seq")),
            P(("frame", "seq"), None),
            P(("frame", "seq"), None),
            P(("frame", "seq"), None),
            P(("frame", "seq"), None),
            P(("frame", "seq"), None),
            P(("frame", "seq"), None),
            P(("frame", "seq"), None),
            P(("frame", "seq"), None),
            P("bucket", "frame", "seq", None),
        ),
        out_specs=(
            P("bucket", "frame", "seq", None),
            P("bucket", "frame", "seq", None),
            P(None, ("frame", "seq")),
            P(None, ("frame", "seq")),
            P(("frame", "seq"), None),
            P(("frame", "seq"), None),
            P(("frame", "seq"), None),
            P(("frame", "seq"), None),
            P(("frame", "seq"), None),
            P(("frame", "seq"), None),
            P(("frame", "seq"), None),
            P(("frame", "seq"), None),
        ),
        check_vma=False,
    )
```

```python
import math

import jax
import jax.numpy as jnp
from jax import lax
from jax.experimental import pallas as pl
from jax.experimental.pallas import tpu as pltpu
from jax.sharding import PartitionSpec as P

HEADS = 16


epsilon = 1e-06
highest = lax.Precision.HIGHEST
masked_fill = -1e30
vmem_limit = 48 * 1024 * 1024


def product(left, right):
    return jnp.dot(left, right, preferred_element_type=jnp.float32)


def contract(left, right, left_dim, right_dim):
    return lax.dot_general(
        left, right, (((left_dim,), (right_dim,)), ((), ())), preferred_element_type=jnp.float32
    )


def call(body, grid, in_specs, out_specs, out_shape, name):
    return pl.pallas_call(
        body,
        grid=grid,
        in_specs=in_specs,
        out_specs=out_specs,
        out_shape=out_shape,
        name=name,
        compiler_params=pltpu.CompilerParams(vmem_limit_bytes=vmem_limit),
    )


def spatial_forward(query, key_value, frame_count):
    model_width, total_rows = query.shape
    head_size = model_width // HEADS
    rows = total_rows // frame_count
    keys = key_value.shape[1] // frame_count
    scale = 1.0 / math.sqrt(head_size)

    def body(q_ref, k_ref, v_ref, out_ref, lse_ref):
        scores = contract(k_ref[...], q_ref[...], 0, 0) * scale
        top = jnp.max(scores, axis=0, keepdims=True)
        weights = jnp.exp(scores - top)
        total = jnp.sum(weights, axis=0, keepdims=True)
        out = product(v_ref[...], weights.astype(jnp.bfloat16))
        out_ref[...] = (out / total).astype(jnp.bfloat16)
        lse_ref[0] = top + jnp.log(total)

    return call(
        body,
        (frame_count, HEADS),
        [
            pl.BlockSpec((head_size, rows), lambda f, h: (h, f)),
            pl.BlockSpec((head_size, keys), lambda f, h: (h, f)),
            pl.BlockSpec((head_size, keys), lambda f, h: (HEADS + h, f)),
        ],
        [
            pl.BlockSpec((head_size, rows), lambda f, h: (h, f)),
            pl.BlockSpec((1, 1, rows), lambda f, h: (f * HEADS + h, 0, 0)),
        ],
        [
            jax.ShapeDtypeStruct(query.shape, jnp.bfloat16),
            jax.ShapeDtypeStruct((frame_count * HEADS, 1, rows), jnp.float32),
        ],
        "spatial_forward",
    )(query, key_value, key_value)


def spatial_backward(query, key_value, log_total, upstream, frame_count, frame):
    model_width, total_rows = query.shape
    head_size = model_width // HEADS
    rows = total_rows // frame_count
    keys = key_value.shape[1] // frame_count
    scale = 1.0 / math.sqrt(head_size)

    def body(q_ref, k_ref, v_ref, lse_ref, up_ref, dq_ref, dkv_ref):
        query_head, key_head, up_head = (q_ref[...], k_ref[...], up_ref[...])
        probs = jnp.exp(contract(key_head, query_head, 0, 0) * scale - lse_ref[0])
        dkv_ref[1] = contract(up_head, probs.astype(jnp.bfloat16), 1, 1).astype(jnp.bfloat16)
        prob_grad = contract(v_ref[...], up_head, 0, 0)
        delta = jnp.sum(probs * prob_grad, axis=0, keepdims=True)
        score_grad = (probs * (prob_grad - delta)).astype(jnp.bfloat16)
        dq_ref[...] = (product(key_head, score_grad) * scale).astype(jnp.bfloat16)
        dkv_ref[0] = (contract(query_head, score_grad, 1, 1) * scale).astype(jnp.bfloat16)

    query_grad, pair_grad = call(
        body,
        (HEADS,),
        [
            pl.BlockSpec((head_size, rows), lambda h: (h, frame)),
            pl.BlockSpec((head_size, keys), lambda h: (h, frame)),
            pl.BlockSpec((head_size, keys), lambda h: (HEADS + h, frame)),
            pl.BlockSpec((1, 1, rows), lambda h: (frame * HEADS + h, 0, 0)),
            pl.BlockSpec((head_size, rows), lambda h: (h, frame)),
        ],
        [
            pl.BlockSpec((head_size, rows), lambda h: (h, 0)),
            pl.BlockSpec((2, head_size, keys), lambda h: (0, h, 0)),
        ],
        [
            jax.ShapeDtypeStruct((model_width, rows), jnp.bfloat16),
            jax.ShapeDtypeStruct((2, model_width, keys), jnp.bfloat16),
        ],
        "spatial_backward",
    )(query, key_value, key_value, log_total, upstream)
    return (query_grad, pair_grad.reshape(2 * model_width, keys))


def cross_probs_of(length_ref, q_ref, k_ref, scale):
    scores = contract(k_ref[...], q_ref[...], 0, 0) * scale
    live = lax.broadcasted_iota(jnp.int32, scores.shape, 0) < length_ref[0]
    scores = jnp.where(live, scores, masked_fill)
    weights = jnp.exp(scores - jnp.max(scores, axis=0, keepdims=True))
    return weights / jnp.sum(weights, axis=0, keepdims=True)


def cross_forward(length, query, text_pair):
    model_width, total_rows = query.shape
    head_size = model_width // HEADS
    keys = text_pair.shape[1]
    scale = 1.0 / math.sqrt(head_size)

    def body(length_ref, q_ref, k_ref, v_ref, out_ref):
        probs = cross_probs_of(length_ref, q_ref, k_ref, scale)
        out_ref[...] = product(v_ref[...], probs.astype(jnp.bfloat16)).astype(jnp.bfloat16)

    return call(
        body,
        (HEADS,),
        [
            pl.BlockSpec(memory_space=pltpu.SMEM),
            pl.BlockSpec((head_size, total_rows), lambda h: (h, 0)),
            pl.BlockSpec((head_size, keys), lambda h: (h, 0)),
            pl.BlockSpec((head_size, keys), lambda h: (HEADS + h, 0)),
        ],
        pl.BlockSpec((head_size, total_rows), lambda h: (h, 0)),
        jax.ShapeDtypeStruct(query.shape, jnp.bfloat16),
        "cross_forward",
    )(length, query, text_pair, text_pair)


def cross_backward(length, query, text_pair, upstream):
    model_width, total_rows = query.shape
    head_size = model_width // HEADS
    keys = text_pair.shape[1]
    scale = 1.0 / math.sqrt(head_size)

    def body(length_ref, q_ref, k_ref, v_ref, up_ref, dq_ref, dkv_ref):
        up_head = up_ref[...]
        probs = cross_probs_of(length_ref, q_ref, k_ref, scale)
        prob_grad = contract(v_ref[...], up_head, 0, 0)
        delta = jnp.sum(probs * prob_grad, axis=0, keepdims=True)
        score_grad = (probs * (prob_grad - delta)).astype(jnp.bfloat16)
        dq_ref[...] = (product(k_ref[...], score_grad) * scale).astype(jnp.bfloat16)
        dkv_ref[0] = contract(q_ref[...], score_grad, 1, 1) * scale
        dkv_ref[1] = contract(up_head, probs.astype(jnp.bfloat16), 1, 1)

    query_grad, pair_grad = call(
        body,
        (HEADS,),
        [
            pl.BlockSpec(memory_space=pltpu.SMEM),
            pl.BlockSpec((head_size, total_rows), lambda h: (h, 0)),
            pl.BlockSpec((head_size, keys), lambda h: (h, 0)),
            pl.BlockSpec((head_size, keys), lambda h: (HEADS + h, 0)),
            pl.BlockSpec((head_size, total_rows), lambda h: (h, 0)),
        ],
        [
            pl.BlockSpec((head_size, total_rows), lambda h: (h, 0)),
            pl.BlockSpec((2, head_size, keys), lambda h: (0, h, 0)),
        ],
        [
            jax.ShapeDtypeStruct(query.shape, jnp.bfloat16),
            jax.ShapeDtypeStruct((2, model_width, keys), jnp.float32),
        ],
        "cross_backward",
    )(length, query, text_pair, text_pair, upstream)
    return (query_grad, pair_grad.reshape(text_pair.shape))


def temporal_probs_of(live_ref, query_frame, key_frames, frame, scale):
    scores = []
    for index in range(3):
        score = jnp.sum(query_frame * key_frames[index], axis=0, keepdims=True) * scale
        if index != 1:
            score = jnp.where(live_ref[frame, index // 2] != 0, score, masked_fill)
        scores.append(score)
    top = jnp.maximum(jnp.maximum(scores[0], scores[1]), scores[2])
    weights = [jnp.exp(score - top) for score in scores]
    inverse = 1.0 / (weights[0] + weights[1] + weights[2])
    return [weight * inverse for weight in weights]


def temporal_forward(live, query, key_value, frame_count):
    model_width, total_rows = query.shape
    head_size = model_width // HEADS
    rows = total_rows // frame_count
    extended_rows = key_value.shape[1]
    scale = 1.0 / math.sqrt(head_size)

    def body(live_ref, q_ref, k_ref, v_ref, out_ref):
        for frame in range(frame_count):
            query_frame = q_ref[:, frame * rows : (frame + 1) * rows].astype(jnp.float32)
            spans = [slice((frame + j) * rows, (frame + j + 1) * rows) for j in range(3)]
            key_frames = [k_ref[:, span].astype(jnp.float32) for span in spans]
            probs = temporal_probs_of(live_ref, query_frame, key_frames, frame, scale)
            mixed = sum(
                prob * v_ref[:, span].astype(jnp.float32) for prob, span in zip(probs, spans)
            )
            out_ref[:, frame * rows : (frame + 1) * rows] = mixed.astype(jnp.bfloat16)

    return call(
        body,
        (HEADS,),
        [
            pl.BlockSpec(memory_space=pltpu.SMEM),
            pl.BlockSpec((head_size, total_rows), lambda h: (h, 0)),
            pl.BlockSpec((head_size, extended_rows), lambda h: (h, 0)),
            pl.BlockSpec((head_size, extended_rows), lambda h: (HEADS + h, 0)),
        ],
        pl.BlockSpec((head_size, total_rows), lambda h: (h, 0)),
        jax.ShapeDtypeStruct(query.shape, jnp.bfloat16),
        "temporal_forward",
    )(live, query, key_value, key_value)


def temporal_backward(live, query, key_value, upstream, frame_count):
    model_width, total_rows = query.shape
    head_size = model_width // HEADS
    rows = total_rows // frame_count
    extended_rows = key_value.shape[1]
    scale = 1.0 / math.sqrt(head_size)

    def body(live_ref, q_ref, k_ref, v_ref, up_ref, dq_ref, dkv_ref):
        key_sums = [None] * (frame_count + 2)
        value_sums = [None] * (frame_count + 2)
        for frame in range(frame_count):
            own = slice(frame * rows, (frame + 1) * rows)
            query_frame = q_ref[:, own].astype(jnp.float32)
            up_frame = up_ref[:, own]
            spans = [slice((frame + j) * rows, (frame + j + 1) * rows) for j in range(3)]
            key_frames = [k_ref[:, span].astype(jnp.float32) for span in spans]
            probs = temporal_probs_of(live_ref, query_frame, key_frames, frame, scale)
            prob_grads = [
                jnp.sum(up_frame * v_ref[:, span].astype(jnp.float32), axis=0, keepdims=True)
                for span in spans
            ]
            delta = sum(prob * grad for prob, grad in zip(probs, prob_grads))
            score_grads = [
                prob * (grad - delta) * scale for prob, grad in zip(probs, prob_grads)
            ]
            dq_ref[:, own] = sum(
                grad * key_frame for grad, key_frame in zip(score_grads, key_frames)
            ).astype(jnp.bfloat16)
            for j in range(3):
                key_part = score_grads[j] * query_frame
                value_part = probs[j] * up_frame
                at = frame + j
                key_sums[at] = key_part if key_sums[at] is None else key_sums[at] + key_part
                value_sums[at] = (
                    value_part if value_sums[at] is None else value_sums[at] + value_part
                )
        for at in range(frame_count + 2):
            dkv_ref[0, :, at * rows : (at + 1) * rows] = key_sums[at].astype(jnp.bfloat16)
            dkv_ref[1, :, at * rows : (at + 1) * rows] = value_sums[at].astype(jnp.bfloat16)

    query_grad, pair_grad = call(
        body,
        (HEADS,),
        [
            pl.BlockSpec(memory_space=pltpu.SMEM),
            pl.BlockSpec((head_size, total_rows), lambda h: (h, 0)),
            pl.BlockSpec((head_size, extended_rows), lambda h: (h, 0)),
            pl.BlockSpec((head_size, extended_rows), lambda h: (HEADS + h, 0)),
            pl.BlockSpec((head_size, total_rows), lambda h: (h, 0)),
        ],
        [
            pl.BlockSpec((head_size, total_rows), lambda h: (h, 0)),
            pl.BlockSpec((2, head_size, extended_rows), lambda h: (0, h, 0)),
        ],
        [
            jax.ShapeDtypeStruct(query.shape, jnp.bfloat16),
            jax.ShapeDtypeStruct((2, model_width, extended_rows), jnp.bfloat16),
        ],
        "temporal_backward",
    )(live, query, key_value, key_value, upstream)
    return (query_grad, pair_grad.reshape(key_value.shape))


def normalize(values):
    centred = values - jnp.mean(values, axis=-1, keepdims=True)
    reciprocal = lax.rsqrt(jnp.mean(centred * centred, axis=-1, keepdims=True) + epsilon)
    return (centred * reciprocal, reciprocal)


def normalize_back(upstream, normed, reciprocal):
    return reciprocal * (
        upstream
        - jnp.mean(upstream, axis=-1, keepdims=True)
        - normed * jnp.mean(upstream * normed, axis=-1, keepdims=True)
    )


def gelu_tanh(values):
    return jax.nn.gelu(values, approximate=True)


def gather_halves(is_first, lower, upper):
    return lax.all_gather(
        jnp.where(is_first, lower, upper), ("bucket", "frame", "seq"), axis=0, tiled=True
    )


def tree_bits():
    return [
        (axis, step)
        for axis in ("frame", "seq")
        for step in reversed(range(lax.axis_size(axis).bit_length() - 1))
    ]


def tree_order(turn):
    bits = tree_bits()
    last = bits[0]
    first = [bit for bit in bits[::-1] if bit != last]
    turn = turn % len(first)
    return first[turn:] + first[:turn] + [last]


def blank(shape):
    return pl.pallas_call(
        lambda out_ref: None,
        out_specs=pl.BlockSpec(memory_space=pl.ANY),
        out_shape=jax.ShapeDtypeStruct(shape, jnp.bfloat16),
        name="blank",
    )()


def stack_halves(lower, upper):
    depth = lower[0].shape[0]
    stacked = blank((2 * depth, sum(part.shape[1] for part in lower)))
    for index, parts in enumerate((lower, upper)):
        column = 0
        for part in parts:
            stacked = lax.dynamic_update_slice(stacked, low(part), (index * depth, column))
            column += part.shape[1]
    return stacked


def scatter_halves(stacked):
    return lax.psum_scatter(stacked, ("bucket", "frame", "seq"), scatter_dimension=0, tiled=True)


def whole_halves(is_first, own):
    other = swapped(own)
    return (
        jnp.where(is_first, own, other).astype(jnp.float32),
        jnp.where(is_first, other, own).astype(jnp.float32),
    )


def my_bit(bit):
    return (lax.axis_index(bit[0]) >> bit[1]) & 1


def across(value, bit):
    axis, step = bit
    return lax.ppermute(
        value, axis, [(i, i ^ (1 << step)) for i in range(lax.axis_size(axis))]
    )


def gather_tree(value):
    for bit in tree_bits()[::-1]:
        other = across(value, bit)
        mine = my_bit(bit) == 0
        value = jnp.concatenate(
            [jnp.where(mine, value, other), jnp.where(mine, other, value)], axis=0
        )
    return value


class Chain:
    def __init__(self, is_first, pair, turn):
        self.order = tree_order(turn)
        self.dims = tree_bits()
        self.is_first = is_first
        self.received = None
        if len(pair) == 2:
            lower, upper = pair
            self.kept = jnp.where(is_first, lower, upper)
            self.received = swapped(jnp.where(is_first, upper, lower))
        else:
            self.kept = pair[0]

    def advance(self):
        value = self.kept
        if self.received is not None:
            value = (
                value.astype(jnp.float32) + self.received.astype(jnp.float32)
            ).astype(value.dtype)
        if self.dims and value.ndim == 2:
            count = 1 << len(self.dims)
            value = value.reshape(
                (2,) * len(self.dims) + (value.shape[0] // count, value.shape[1])
            )
        if self.order:
            bit = self.order.pop(0)
            dim = self.dims.index(bit)
            self.dims.remove(bit)
            index = my_bit(bit)
            self.received = across(
                lax.dynamic_index_in_dim(value, 1 - index, dim, keepdims=False), bit
            )
            self.kept = lax.dynamic_index_in_dim(value, index, dim, keepdims=False)
        else:
            self.kept = value
            self.received = None

    def finish(self):
        while self.received is not None or self.order:
            self.advance()
        return self.kept


def merged(chains):
    parts = [
        low(chain.kept.astype(jnp.float32) + chain.received.astype(jnp.float32))
        for chain in chains
    ]
    last = Chain(chains[0].is_first, (None,), 0)
    last.order = []
    last.dims = []
    bit = chains[0].order[0]
    index = my_bit(bit)
    last.kept = jnp.concatenate(
        [lax.dynamic_index_in_dim(part, index, 0, keepdims=False) for part in parts], axis=1
    )
    sent = [lax.dynamic_index_in_dim(part, 1 - index, 0, keepdims=False) for part in parts]
    last.received = across(jnp.concatenate(sent, axis=1), bit)
    return last


def together(main, chains):
    main, received = lax.optimization_barrier((main, [chain.received for chain in chains]))
    for chain, value in zip(chains, received):
        chain.received = value
    return main


def tick(main, chains):
    main, received = lax.optimization_barrier((main, [chain.received for chain in chains]))
    for chain, value in zip(chains, received):
        chain.received = value
        chain.advance()
    return main


def low(value):
    return value.astype(jnp.bfloat16)


def swapped(value):
    return lax.ppermute(value, "bucket", [(0, 1), (1, 0)])


def per_device(
    latent,
    condition,
    text,
    text_len,
    clip_ids,
    video_flag,
    ada_weight,
    text_kv_weight,
    qkv_weight,
    proj_weight,
    cross_q_weight,
    cross_proj_weight,
    up_weight,
    down_weight,
    temporal_qkv_weight,
    temporal_proj_weight,
    cotangent,
):
    frame_count, row_count, width = (latent.shape[1], latent.shape[2], latent.shape[3])
    total_rows = frame_count * row_count
    seq_size = lax.axis_size("seq")
    frame_size = lax.axis_size("frame")
    shards = seq_size * frame_size
    is_first = lax.axis_index("bucket") == 0
    ff_width = up_weight.shape[1]
    shard_rows = up_weight.shape[0]
    ff_blocks = ff_width // width
    half_ff = ff_width // 2

    shifts = [
        [((i + s) % seq_size, i) for i in range(seq_size)] for s in range(1, seq_size)
    ]
    latent_rest = [lax.ppermute(latent[0], "seq", shift) for shift in shifts]

    gathered_a = gather_halves(
        is_first,
        qkv_weight,
        jnp.concatenate([proj_weight, cross_q_weight, cross_proj_weight], axis=1),
    )
    up_mixed = (
        up_weight.reshape(shard_rows, shards, ff_blocks, shard_rows)
        .transpose(0, 2, 1, 3)
        .reshape(shard_rows, ff_width)
    )
    down_wide = (
        down_weight.reshape(ff_blocks, shard_rows, width)
        .transpose(1, 0, 2)
        .reshape(shard_rows, ff_width)
    )
    gathered_b = gather_halves(
        is_first,
        jnp.concatenate([up_mixed[:, :half_ff], down_wide[:, :half_ff]], axis=1),
        jnp.concatenate([up_mixed[:, half_ff:], down_wide[:, half_ff:]], axis=1),
    )

    silu_cond = jax.nn.silu(condition.astype(jnp.float32))
    mod_part = jnp.dot(silu_cond, ada_weight.astype(jnp.float32), precision=highest)
    modulation = gather_tree(mod_part).reshape(9, width)
    text_part = contract(text_kv_weight, text[0], 0, 1).astype(jnp.bfloat16)
    text_pair = gather_tree(text_part)

    inputs = latent[0].reshape(total_rows, width).astype(jnp.float32)
    normed_a, recip_a = normalize(inputs)
    hidden_a = (normed_a * (1.0 + modulation[1]) + modulation[0]).astype(jnp.bfloat16)
    normed_rest = [
        normalize(rest.reshape(total_rows, width).astype(jnp.float32))[0] for rest in latent_rest
    ]
    hidden_rest = [
        (normed * (1.0 + modulation[1]) + modulation[0]).astype(jnp.bfloat16)
        for normed in normed_rest
    ]
    hidden_all = jnp.concatenate(
        [part.reshape(frame_count, row_count, width) for part in [hidden_a] + hidden_rest], axis=1
    ).reshape(frame_count * seq_size * row_count, width)
    hidden_a, hidden_all, text_pair, gathered_a = lax.optimization_barrier(
        (hidden_a, hidden_all, text_pair, gathered_a)
    )
    query_full = gathered_a[:width, :width]
    pair_full = gathered_a[:width, width:]
    proj_full = gathered_a[width:, :width]
    cross_q_full = gathered_a[width:, width : 2 * width]
    cross_proj_full = gathered_a[width:, 2 * width :]
    query = contract(query_full, hidden_a, 0, 1).astype(jnp.bfloat16)
    key_value = contract(pair_full, hidden_all, 0, 1).astype(jnp.bfloat16)
    attended, log_total = spatial_forward(query, key_value, frame_count)
    branch_a = contract(attended, proj_full, 0, 0)
    after_a = inputs + modulation[2] * branch_a
    after_low = after_a.astype(jnp.bfloat16)
    cross_query = contract(cross_q_full, after_low, 0, 1).astype(jnp.bfloat16)
    cross_out = cross_forward(text_len, cross_query, text_pair)
    after_c = after_a + contract(cross_out, cross_proj_full, 0, 0)
    normed_m, recip_m = normalize(after_c)
    hidden_m = (normed_m * (1.0 + modulation[4]) + modulation[3]).astype(jnp.bfloat16)

    temporal_lower, temporal_upper = lax.optimization_barrier(
        (
            jnp.concatenate([temporal_qkv_weight[:, :width], temporal_proj_weight], axis=1),
            temporal_qkv_weight[:, width:],
            query,
        )
    )[:2]
    gathered_c = gather_halves(is_first, temporal_lower, temporal_upper)
    up_halves = (gathered_b[:width, :half_ff], gathered_b[width:, :half_ff])
    per_half = ff_blocks // 2
    down_halves = (gathered_b[:width, half_ff:ff_width], gathered_b[width:, half_ff:ff_width])
    down_parts = [
        down_halves[index // per_half][
            :, width * (index % per_half) : width * (index % per_half + 1)
        ]
        for index in range(ff_blocks)
    ]
    tquery_full = gathered_c[:width, :width]
    tproj_full = gathered_c[:width, width:]
    tpair_full = gathered_c[width:]

    upward_halves = [product(hidden_m, part) for part in up_halves]
    activated_halves = [gelu_tanh(part).astype(jnp.bfloat16) for part in upward_halves]
    activated_parts = [
        activated_halves[index // per_half][
            :, width * (index % per_half) : width * (index % per_half + 1)
        ]
        for index in range(ff_blocks)
    ]
    branch_m = sum(product(left, right) for left, right in zip(activated_parts, down_parts))
    after_m = after_c + modulation[5] * branch_m
    normed_t, recip_t = normalize(after_m)
    hidden_t = (normed_t * (1.0 + modulation[7]) + modulation[6]).astype(jnp.bfloat16)
    ahead = [(i, i + 1) for i in range(frame_size - 1)]
    back = [(i + 1, i) for i in range(frame_size - 1)]
    hidden_prev = lax.ppermute(hidden_t[total_rows - row_count :], "frame", ahead)
    hidden_next = lax.ppermute(hidden_t[:row_count], "frame", back)
    hidden_ext = jnp.concatenate([hidden_prev, hidden_t, hidden_next], axis=0)
    tquery = contract(tquery_full, hidden_t, 0, 1).astype(jnp.bfloat16)
    tpair = low(contract(tpair_full, hidden_ext, 0, 1))
    first_frame = lax.axis_index("frame") * frame_count
    clips_ext = jnp.concatenate(
        [jnp.full((1,), -1, jnp.int32), clip_ids[0], jnp.full((1,), -1, jnp.int32)]
    )
    clips_local = lax.dynamic_slice_in_dim(clips_ext, first_frame, frame_count + 2)
    live = jnp.stack(
        [clips_local[:-2] == clips_local[1:-1], clips_local[2:] == clips_local[1:-1]], axis=1
    ).astype(jnp.int32)
    flag_local = lax.dynamic_slice_in_dim(video_flag[0], first_frame, frame_count).astype(
        jnp.float32
    )
    mixed = temporal_forward(live, tquery, tpair, frame_count)
    branch_t = contract(mixed, tproj_full, 0, 0)
    flag_rows = jnp.repeat(flag_local, row_count)[:, None]
    result_rows = after_m + flag_rows * modulation[8] * branch_t
    result = result_rows.astype(jnp.bfloat16).reshape(latent.shape)

    result_grad = cotangent[0].reshape(total_rows, width).astype(jnp.float32)
    gate_t_grad = jnp.sum(flag_rows * branch_t * result_grad, axis=0)
    branch_t_grad = (flag_rows * modulation[8] * result_grad).astype(jnp.bfloat16)
    mixed_grad = contract(tproj_full, branch_t_grad, 1, 1)
    tquery_grad, tpair_grad = temporal_backward(live, tquery, tpair, mixed_grad, frame_count)
    halo_prev, halo_next, tpair_grad = lax.optimization_barrier(
        (
            low(contract(tpair_grad[:, :row_count], tpair_full, 0, 1)),
            low(contract(tpair_grad[:, -row_count:], tpair_full, 0, 1)),
            tpair_grad,
        )
    )
    to_prev = lax.ppermute(halo_prev, "frame", back)
    to_next = lax.ppermute(halo_next, "frame", ahead)
    stacked_c = stack_halves(
        [contract(hidden_t, tquery_grad, 0, 1), contract(mixed, branch_t_grad, 1, 0)],
        [contract(hidden_ext, tpair_grad, 0, 1)],
    )
    hidden_t_grad = contract(tpair_grad[:, row_count:-row_count], tpair_full, 0, 1) + contract(
        tquery_grad, tquery_full, 0, 1
    )
    hidden_t_grad, stacked_c = lax.optimization_barrier((hidden_t_grad, stacked_c))
    scattered_c = scatter_halves(stacked_c)
    hidden_t_grad = jnp.concatenate(
        [
            hidden_t_grad[:row_count] + to_next.astype(jnp.float32),
            hidden_t_grad[row_count : total_rows - row_count],
            hidden_t_grad[total_rows - row_count :] + to_prev.astype(jnp.float32),
        ],
        axis=0,
    )
    grad_m = result_grad + normalize_back(hidden_t_grad * (1.0 + modulation[7]), normed_t, recip_t)
    gate_m_grad = jnp.sum(branch_m * grad_m, axis=0)
    branch_m_grad = low(modulation[5] * grad_m)
    upward_grads = []
    for index in range(2):
        activated_grad = jnp.concatenate(
            [
                contract(branch_m_grad, part, 1, 1)
                for part in down_parts[index * per_half : (index + 1) * per_half]
            ],
            axis=1,
        )
        gelu_back = jax.vjp(gelu_tanh, upward_halves[index])[1]
        upward_grads.append(low(gelu_back(activated_grad)[0]))
    hidden_m_grad = contract(upward_grads[0], up_halves[0], 1, 1) + contract(
        upward_grads[1], up_halves[1], 1, 1
    )
    up_grads = [contract(hidden_m, part, 0, 0) for part in upward_grads]
    down_grads = [contract(part, branch_m_grad, 0, 0) for part in activated_parts]
    stacked_b = stack_halves(
        [up_grads[0]] + down_grads[:per_half], [up_grads[1]] + down_grads[per_half:]
    )
    hidden_m_grad, stacked_b = lax.optimization_barrier((hidden_m_grad, stacked_b))
    grad_c = grad_m + normalize_back(hidden_m_grad * (1.0 + modulation[4]), normed_m, recip_m)
    cross_branch_grad = low(grad_c)
    cross_out_grad = low(contract(cross_proj_full, cross_branch_grad, 1, 1))
    cross_query_grad, text_grad = cross_backward(text_len, cross_query, text_pair, cross_out_grad)
    chain_text = Chain(is_first, (low(text_grad),), 1)
    chain_text.advance()
    grad_a = grad_c + contract(cross_query_grad, cross_q_full, 0, 1)
    gate_a_grad = jnp.sum(branch_a * grad_a, axis=0)
    branch_a_grad = low(modulation[2] * grad_a)
    attended_grad = low(contract(proj_full, branch_a_grad, 1, 1))
    attended_grad, scattered_c, stacked_b = lax.optimization_barrier(
        (attended_grad, scattered_c, stacked_b)
    )
    scattered_b = scatter_halves(stacked_b)
    attended_grad = tick(attended_grad, [chain_text])
    proj_grad = low(contract(attended, branch_a_grad, 1, 0))
    cross_q_grad = low(contract(after_low, cross_query_grad, 0, 1))
    cross_proj_grad = low(contract(cross_out, cross_branch_grad, 1, 0))
    attended_grad, proj_grad, cross_q_grad, cross_proj_grad = lax.optimization_barrier(
        (attended_grad, proj_grad, cross_q_grad, cross_proj_grad)
    )
    query_grads, pair_grads, rest_grads, rest_received = ([], [], [], [])
    for frame in range(frame_count):
        query_grad, pair_grad = spatial_backward(
            query, key_value, log_total, attended_grad, frame_count, frame
        )
        rest_sent = contract(pair_grad[:, row_count:], pair_full, 0, 1)
        rest_low = low(rest_sent)
        pair_grad, rest_low, attended_grad = lax.optimization_barrier(
            (pair_grad, rest_low, attended_grad)
        )
        query_grads.append(query_grad)
        pair_grads.append(pair_grad)
        rest_grads.append(rest_sent)
        rest_received.append(
            [
                lax.ppermute(
                    rest_low[s * row_count : (s + 1) * row_count],
                    "seq",
                    [(j, i) for i, j in shifts[s]],
                )
                for s in range(seq_size - 1)
            ]
        )
        if frame == 0:
            attended_grad = tick(attended_grad, [chain_text])
        else:
            query_grads, pair_grads, rest_received[frame - 1] = lax.optimization_barrier(
                (query_grads, pair_grads, rest_received[frame - 1])
            )
    query_grad = jnp.concatenate(query_grads, axis=1)
    pair_grad = jnp.concatenate(pair_grads, axis=1)
    query_weight_grad = low(contract(hidden_a, query_grad, 0, 1))
    pair_weight_grad = low(contract(hidden_all, pair_grad, 0, 1))
    query_grad, pair_grads, query_weight_grad, pair_weight_grad = lax.optimization_barrier(
        (query_grad, pair_grads, query_weight_grad, pair_weight_grad)
    )
    chains_a = [
        Chain(is_first, pair, turn)
        for turn, pair in enumerate(
            (
                (pair_weight_grad[:, width:], cross_proj_grad),
                (query_weight_grad, proj_grad),
                (pair_weight_grad[:, :width], cross_q_grad),
            )
        )
    ]
    pair_own = jnp.concatenate(
        [contract(part[:, :row_count], pair_full, 0, 1) for part in pair_grads], axis=0
    )
    pair_own = tick(pair_own, chains_a + [chain_text])
    own_grad = pair_own + contract(query_grad, query_full, 0, 1)
    shift_a_grad = jnp.sum(own_grad, axis=0)
    scale_a_grad = jnp.sum(own_grad * normed_a, axis=0)
    for frame in range(frame_count):
        for s in range(seq_size - 1):
            rest_rows = rest_grads[frame][s * row_count : (s + 1) * row_count]
            rest_normed = normed_rest[s][frame * row_count : (frame + 1) * row_count]
            shift_a_grad = shift_a_grad + jnp.sum(rest_rows, axis=0)
            scale_a_grad = scale_a_grad + jnp.sum(rest_rows * rest_normed, axis=0)
    mod_grad = jnp.stack(
        [
            shift_a_grad,
            scale_a_grad,
            gate_a_grad,
            jnp.sum(hidden_m_grad, axis=0),
            jnp.sum(hidden_m_grad * normed_m, axis=0),
            gate_m_grad,
            jnp.sum(hidden_t_grad, axis=0),
            jnp.sum(hidden_t_grad * normed_t, axis=0),
            gate_t_grad,
        ]
    ).reshape(shards, 9 * width // shards)
    own_grad, mod_grad, rest_received = together(
        (own_grad, mod_grad, rest_received), chains_a + [chain_text]
    )
    for chain in chains_a + [chain_text]:
        chain.advance()
    chain_mod = Chain(is_first, (mod_grad,), 0)
    chain_mod.advance()
    hidden_a_grad = own_grad + jnp.concatenate(
        [sum(part.astype(jnp.float32) for part in parts) for parts in rest_received], axis=0
    )
    input_grad = grad_a + normalize_back(hidden_a_grad * (1.0 + modulation[1]), normed_a, recip_a)
    latent_grad = input_grad.reshape(latent.shape)
    latent_grad = together(latent_grad, chains_a + [chain_mod])
    while len(chains_a[0].order) > 1:
        for chain in chains_a + [chain_mod]:
            chain.advance()
        latent_grad = together(latent_grad, chains_a + [chain_mod])
    chain_last = merged(chains_a)
    chain_mod.advance()
    lower_b, upper_b = whole_halves(is_first, scattered_b)
    lower_c, upper_c = whole_halves(is_first, scattered_c)
    up_shard = (
        jnp.concatenate([lower_b[:, :half_ff], upper_b[:, :half_ff]], axis=1)
        .reshape(shard_rows, ff_blocks, shards, shard_rows)
        .transpose(0, 2, 1, 3)
        .reshape(shard_rows, ff_width)
    )
    down_shard = jnp.concatenate(
        [
            half[:, half_ff + width * index : half_ff + width * (index + 1)]
            for half in (lower_b, upper_b)
            for index in range(per_half)
        ],
        axis=0,
    )
    latent_grad = together(latent_grad, [chain_last, chain_mod])
    mod_slice = chain_mod.finish()
    own_a = chain_last.finish()
    other_a, up_shard, down_shard = lax.optimization_barrier(
        (swapped(own_a), up_shard, down_shard)
    )
    lower_a = jnp.where(is_first, own_a, other_a).astype(jnp.float32)
    upper_a = jnp.where(is_first, other_a, own_a).astype(jnp.float32)
    text_low = chain_text.finish()
    silu_pair = jnp.concatenate([silu_cond, swapped(silu_cond)], axis=0)
    mod_pair = jnp.concatenate([mod_slice, swapped(mod_slice)], axis=0)
    ada_grad = lax.dot_general(
        silu_pair, mod_pair, (((0,), (0,)), ((), ())), precision=highest
    )
    text_both = jnp.concatenate([text[0], swapped(text[0])], axis=0)
    slice_both = jnp.concatenate([text_low, swapped(text_low)], axis=1)
    text_kv_grad = contract(text_both, slice_both, 0, 1)
    return (
        result,
        latent_grad,
        ada_grad,
        text_kv_grad,
        jnp.concatenate([lower_a[:, width : 2 * width], lower_a[:, 2 * width :], lower_a[:, :width]], axis=1),
        upper_a[:, width : 2 * width],
        upper_a[:, 2 * width :],
        upper_a[:, :width],
        up_shard,
        down_shard,
        jnp.concatenate([lower_c[:, :width], upper_c], axis=1),
        lower_c[:, width:],
    )


def solution(mesh):
    return jax.shard_map(
        per_device,
        mesh=mesh,
        in_specs=(
            P("bucket", "frame", "seq", None),
            P("bucket", None),
            P("bucket", None, None),
            P("bucket"),
            P("bucket", None),
            P("bucket", None),
            P(None, ("frame", "seq")),
            P(None, ("frame", "seq")),
            P(("frame", "seq"), None),
            P(("frame", "seq"), None),
            P(("frame", "seq"), None),
            P(("frame", "seq"), None),
            P(("frame", "seq"), None),
            P(("frame", "seq"), None),
            P(("frame", "seq"), None),
            P(("frame", "seq"), None),
            P("bucket", "frame", "seq", None),
        ),
        out_specs=(
            P("bucket", "frame", "seq", None),
            P("bucket", "frame", "seq", None),
            P(None, ("frame", "seq")),
            P(None, ("frame", "seq")),
            P(("frame", "seq"), None),
            P(("frame", "seq"), None),
            P(("frame", "seq"), None),
            P(("frame", "seq"), None),
            P(("frame", "seq"), None),
            P(("frame", "seq"), None),
            P(("frame", "seq"), None),
            P(("frame", "seq"), None),
        ),
        check_vma=False,
    )
```

```python
import math

import jax
import jax.numpy as jnp
from jax import lax
from jax.experimental import pallas as pl
from jax.experimental.pallas import tpu as pltpu
from jax.sharding import PartitionSpec as P

HEADS = 16


epsilon = 1e-06
highest = lax.Precision.HIGHEST
masked_fill = -1e30
vmem_limit = 48 * 1024 * 1024


def product(left, right):
    return jnp.dot(left, right, preferred_element_type=jnp.float32)


def contract(left, right, left_dim, right_dim):
    return lax.dot_general(
        left, right, (((left_dim,), (right_dim,)), ((), ())), preferred_element_type=jnp.float32
    )


def call(body, grid, in_specs, out_specs, out_shape, name):
    return pl.pallas_call(
        body,
        grid=grid,
        in_specs=in_specs,
        out_specs=out_specs,
        out_shape=out_shape,
        name=name,
        compiler_params=pltpu.CompilerParams(vmem_limit_bytes=vmem_limit),
    )


def spatial_forward(query, key_value, frame_count):
    model_width, total_rows = query.shape
    head_size = model_width // HEADS
    rows = total_rows // frame_count
    keys = key_value.shape[1] // frame_count
    scale = math.log2(math.e) / math.sqrt(head_size)

    def body(q_ref, k_ref, v_ref, out_ref, exact_ref, lse_ref):
        scores = contract(k_ref[...], q_ref[...], 0, 0)
        top = jnp.max(scores, axis=0, keepdims=True) * scale
        weights = jnp.exp2(scores * scale - top)
        total = jnp.sum(weights, axis=0, keepdims=True)
        out = product(v_ref[...], weights.astype(jnp.bfloat16)) / total
        out_ref[...] = out.astype(jnp.bfloat16)
        exact_ref[...] = out
        lse_ref[0] = top + jnp.log2(total)

    return call(
        body,
        (frame_count, HEADS),
        [
            pl.BlockSpec((head_size, rows), lambda f, h: (h, f)),
            pl.BlockSpec((head_size, keys), lambda f, h: (h, f)),
            pl.BlockSpec((head_size, keys), lambda f, h: (HEADS + h, f)),
        ],
        [
            pl.BlockSpec((head_size, rows), lambda f, h: (h, f)),
            pl.BlockSpec((head_size, rows), lambda f, h: (h, f)),
            pl.BlockSpec((1, 1, rows), lambda f, h: (f * HEADS + h, 0, 0)),
        ],
        [
            jax.ShapeDtypeStruct(query.shape, jnp.bfloat16),
            jax.ShapeDtypeStruct(query.shape, jnp.float32),
            jax.ShapeDtypeStruct((frame_count * HEADS, 1, rows), jnp.float32),
        ],
        "spatial_forward",
    )(query, key_value, key_value)


def spatial_backward(query, key_value, log_total, exact, upstream, frame_count, frame):
    model_width, total_rows = query.shape
    head_size = model_width // HEADS
    rows = total_rows // frame_count
    keys = key_value.shape[1] // frame_count
    scale = 1.0 / math.sqrt(head_size)
    scale_two = math.log2(math.e) * scale

    def body(q_ref, k_ref, v_ref, lse_ref, exact_ref, up_ref, dq_ref, dkv_ref):
        query_head, key_head, up_head = (q_ref[...], k_ref[...], up_ref[...])
        probs = jnp.exp2(contract(key_head, query_head, 0, 0) * scale_two - lse_ref[0])
        dkv_ref[1] = contract(up_head, probs.astype(jnp.bfloat16), 1, 1).astype(jnp.bfloat16)
        prob_grad = contract(v_ref[...], up_head, 0, 0)
        delta = jnp.sum(up_head.astype(jnp.float32) * exact_ref[...], axis=0, keepdims=True)
        score_grad = (probs * (prob_grad - delta)).astype(jnp.bfloat16)
        dq_ref[...] = (product(key_head, score_grad) * scale).astype(jnp.bfloat16)
        dkv_ref[0] = (contract(query_head, score_grad, 1, 1) * scale).astype(jnp.bfloat16)

    query_grad, pair_grad = call(
        body,
        (HEADS,),
        [
            pl.BlockSpec((head_size, rows), lambda h: (h, frame)),
            pl.BlockSpec((head_size, keys), lambda h: (h, frame)),
            pl.BlockSpec((head_size, keys), lambda h: (HEADS + h, frame)),
            pl.BlockSpec((1, 1, rows), lambda h: (frame * HEADS + h, 0, 0)),
            pl.BlockSpec((head_size, rows), lambda h: (h, frame)),
            pl.BlockSpec((head_size, rows), lambda h: (h, frame)),
        ],
        [
            pl.BlockSpec((head_size, rows), lambda h: (h, 0)),
            pl.BlockSpec((2, head_size, keys), lambda h: (0, h, 0)),
        ],
        [
            jax.ShapeDtypeStruct((model_width, rows), jnp.bfloat16),
            jax.ShapeDtypeStruct((2, model_width, keys), jnp.bfloat16),
        ],
        "spatial_backward",
    )(query, key_value, key_value, log_total, exact, upstream)
    return (query_grad, pair_grad.reshape(2 * model_width, keys))


def cross_probs_of(length_ref, q_ref, k_ref, scale):
    scores = contract(k_ref[...], q_ref[...], 0, 0) * scale
    live = lax.broadcasted_iota(jnp.int32, scores.shape, 0) < length_ref[0]
    scores = jnp.where(live, scores, masked_fill)
    weights = jnp.exp(scores - jnp.max(scores, axis=0, keepdims=True))
    return weights / jnp.sum(weights, axis=0, keepdims=True)


def cross_forward(length, query, text_pair):
    model_width, total_rows = query.shape
    head_size = model_width // HEADS
    keys = text_pair.shape[1]
    scale = 1.0 / math.sqrt(head_size)

    def body(length_ref, q_ref, k_ref, v_ref, out_ref):
        probs = cross_probs_of(length_ref, q_ref, k_ref, scale)
        out_ref[...] = product(v_ref[...], probs.astype(jnp.bfloat16)).astype(jnp.bfloat16)

    return call(
        body,
        (HEADS,),
        [
            pl.BlockSpec(memory_space=pltpu.SMEM),
            pl.BlockSpec((head_size, total_rows), lambda h: (h, 0)),
            pl.BlockSpec((head_size, keys), lambda h: (h, 0)),
            pl.BlockSpec((head_size, keys), lambda h: (HEADS + h, 0)),
        ],
        pl.BlockSpec((head_size, total_rows), lambda h: (h, 0)),
        jax.ShapeDtypeStruct(query.shape, jnp.bfloat16),
        "cross_forward",
    )(length, query, text_pair, text_pair)


def cross_backward(length, query, text_pair, upstream):
    model_width, total_rows = query.shape
    head_size = model_width // HEADS
    keys = text_pair.shape[1]
    scale = 1.0 / math.sqrt(head_size)

    def body(length_ref, q_ref, k_ref, v_ref, up_ref, dq_ref, dkv_ref):
        up_head = up_ref[...]
        probs = cross_probs_of(length_ref, q_ref, k_ref, scale)
        prob_grad = contract(v_ref[...], up_head, 0, 0)
        delta = jnp.sum(probs * prob_grad, axis=0, keepdims=True)
        score_grad = (probs * (prob_grad - delta)).astype(jnp.bfloat16)
        dq_ref[...] = (product(k_ref[...], score_grad) * scale).astype(jnp.bfloat16)
        dkv_ref[0] = contract(q_ref[...], score_grad, 1, 1) * scale
        dkv_ref[1] = contract(up_head, probs.astype(jnp.bfloat16), 1, 1)

    query_grad, pair_grad = call(
        body,
        (HEADS,),
        [
            pl.BlockSpec(memory_space=pltpu.SMEM),
            pl.BlockSpec((head_size, total_rows), lambda h: (h, 0)),
            pl.BlockSpec((head_size, keys), lambda h: (h, 0)),
            pl.BlockSpec((head_size, keys), lambda h: (HEADS + h, 0)),
            pl.BlockSpec((head_size, total_rows), lambda h: (h, 0)),
        ],
        [
            pl.BlockSpec((head_size, total_rows), lambda h: (h, 0)),
            pl.BlockSpec((2, head_size, keys), lambda h: (0, h, 0)),
        ],
        [
            jax.ShapeDtypeStruct(query.shape, jnp.bfloat16),
            jax.ShapeDtypeStruct((2, model_width, keys), jnp.float32),
        ],
        "cross_backward",
    )(length, query, text_pair, text_pair, upstream)
    return (query_grad, pair_grad.reshape(text_pair.shape))


def temporal_probs_of(live_ref, query_frame, key_frames, frame, scale):
    scores = []
    for index in range(3):
        score = jnp.sum(query_frame * key_frames[index], axis=0, keepdims=True) * scale
        if index != 1:
            score = jnp.where(live_ref[frame, index // 2] != 0, score, masked_fill)
        scores.append(score)
    top = jnp.maximum(jnp.maximum(scores[0], scores[1]), scores[2])
    weights = [jnp.exp(score - top) for score in scores]
    inverse = 1.0 / (weights[0] + weights[1] + weights[2])
    return [weight * inverse for weight in weights]


def temporal_forward(live, query, key_value, frame_count):
    model_width, total_rows = query.shape
    head_size = model_width // HEADS
    rows = total_rows // frame_count
    extended_rows = key_value.shape[1]
    scale = 1.0 / math.sqrt(head_size)

    def body(live_ref, q_ref, k_ref, v_ref, out_ref):
        for frame in range(frame_count):
            query_frame = q_ref[:, frame * rows : (frame + 1) * rows].astype(jnp.float32)
            spans = [slice((frame + j) * rows, (frame + j + 1) * rows) for j in range(3)]
            key_frames = [k_ref[:, span].astype(jnp.float32) for span in spans]
            probs = temporal_probs_of(live_ref, query_frame, key_frames, frame, scale)
            mixed = sum(
                prob * v_ref[:, span].astype(jnp.float32) for prob, span in zip(probs, spans)
            )
            out_ref[:, frame * rows : (frame + 1) * rows] = mixed.astype(jnp.bfloat16)

    return call(
        body,
        (HEADS,),
        [
            pl.BlockSpec(memory_space=pltpu.SMEM),
            pl.BlockSpec((head_size, total_rows), lambda h: (h, 0)),
            pl.BlockSpec((head_size, extended_rows), lambda h: (h, 0)),
            pl.BlockSpec((head_size, extended_rows), lambda h: (HEADS + h, 0)),
        ],
        pl.BlockSpec((head_size, total_rows), lambda h: (h, 0)),
        jax.ShapeDtypeStruct(query.shape, jnp.bfloat16),
        "temporal_forward",
    )(live, query, key_value, key_value)


def temporal_backward(live, query, key_value, upstream, frame_count):
    model_width, total_rows = query.shape
    head_size = model_width // HEADS
    rows = total_rows // frame_count
    extended_rows = key_value.shape[1]
    scale = 1.0 / math.sqrt(head_size)

    def body(live_ref, q_ref, k_ref, v_ref, up_ref, dq_ref, dkv_ref):
        key_sums = [None] * (frame_count + 2)
        value_sums = [None] * (frame_count + 2)
        for frame in range(frame_count):
            own = slice(frame * rows, (frame + 1) * rows)
            query_frame = q_ref[:, own].astype(jnp.float32)
            up_frame = up_ref[:, own]
            spans = [slice((frame + j) * rows, (frame + j + 1) * rows) for j in range(3)]
            key_frames = [k_ref[:, span].astype(jnp.float32) for span in spans]
            probs = temporal_probs_of(live_ref, query_frame, key_frames, frame, scale)
            prob_grads = [
                jnp.sum(up_frame * v_ref[:, span].astype(jnp.float32), axis=0, keepdims=True)
                for span in spans
            ]
            delta = sum(prob * grad for prob, grad in zip(probs, prob_grads))
            score_grads = [
                prob * (grad - delta) * scale for prob, grad in zip(probs, prob_grads)
            ]
            dq_ref[:, own] = sum(
                grad * key_frame for grad, key_frame in zip(score_grads, key_frames)
            ).astype(jnp.bfloat16)
            for j in range(3):
                key_part = score_grads[j] * query_frame
                value_part = probs[j] * up_frame
                at = frame + j
                key_sums[at] = key_part if key_sums[at] is None else key_sums[at] + key_part
                value_sums[at] = (
                    value_part if value_sums[at] is None else value_sums[at] + value_part
                )
        for at in range(frame_count + 2):
            dkv_ref[0, :, at * rows : (at + 1) * rows] = key_sums[at].astype(jnp.bfloat16)
            dkv_ref[1, :, at * rows : (at + 1) * rows] = value_sums[at].astype(jnp.bfloat16)

    query_grad, pair_grad = call(
        body,
        (HEADS,),
        [
            pl.BlockSpec(memory_space=pltpu.SMEM),
            pl.BlockSpec((head_size, total_rows), lambda h: (h, 0)),
            pl.BlockSpec((head_size, extended_rows), lambda h: (h, 0)),
            pl.BlockSpec((head_size, extended_rows), lambda h: (HEADS + h, 0)),
            pl.BlockSpec((head_size, total_rows), lambda h: (h, 0)),
        ],
        [
            pl.BlockSpec((head_size, total_rows), lambda h: (h, 0)),
            pl.BlockSpec((2, head_size, extended_rows), lambda h: (0, h, 0)),
        ],
        [
            jax.ShapeDtypeStruct(query.shape, jnp.bfloat16),
            jax.ShapeDtypeStruct((2, model_width, extended_rows), jnp.bfloat16),
        ],
        "temporal_backward",
    )(live, query, key_value, key_value, upstream)
    return (query_grad, pair_grad.reshape(key_value.shape))


def normalize(values):
    centred = values - jnp.mean(values, axis=-1, keepdims=True)
    reciprocal = lax.rsqrt(jnp.mean(centred * centred, axis=-1, keepdims=True) + epsilon)
    return (centred * reciprocal, reciprocal)


def normalize_back(upstream, normed, reciprocal):
    return reciprocal * (
        upstream
        - jnp.mean(upstream, axis=-1, keepdims=True)
        - normed * jnp.mean(upstream * normed, axis=-1, keepdims=True)
    )


def gelu_tanh(values):
    return jax.nn.gelu(values, approximate=True)


def gather_halves(is_first, lower, upper):
    return lax.all_gather(
        jnp.where(is_first, lower, upper), ("bucket", "frame", "seq"), axis=0, tiled=True
    )


def tree_bits():
    return [
        (axis, step)
        for axis in ("frame", "seq")
        for step in reversed(range(lax.axis_size(axis).bit_length() - 1))
    ]


def tree_order(turn):
    bits = tree_bits()
    last = bits[0]
    first = [bit for bit in bits[::-1] if bit != last]
    turn = turn % len(first)
    return first[turn:] + first[:turn] + [last]


def blank(shape):
    return pl.pallas_call(
        lambda out_ref: None,
        out_specs=pl.BlockSpec(memory_space=pl.ANY),
        out_shape=jax.ShapeDtypeStruct(shape, jnp.bfloat16),
        name="blank",
    )()


def placed(stacked, parts):
    for part, row, column in parts:
        stacked = lax.dynamic_update_slice(stacked, low(part), (row, column))
    return stacked


def scatter_halves(stacked):
    return lax.psum_scatter(stacked, ("bucket", "frame", "seq"), scatter_dimension=0, tiled=True)


def whole_halves(is_first, own):
    other = swapped(own)
    return (
        jnp.where(is_first, own, other).astype(jnp.float32),
        jnp.where(is_first, other, own).astype(jnp.float32),
    )


def my_bit(bit):
    return (lax.axis_index(bit[0]) >> bit[1]) & 1


def across(value, bit):
    axis, step = bit
    return lax.ppermute(
        value, axis, [(i, i ^ (1 << step)) for i in range(lax.axis_size(axis))]
    )


def gather_tree(value):
    for bit in tree_bits()[::-1]:
        other = across(value, bit)
        mine = my_bit(bit) == 0
        value = jnp.concatenate(
            [jnp.where(mine, value, other), jnp.where(mine, other, value)], axis=0
        )
    return value


class Chain:
    def __init__(self, is_first, pair, turn):
        self.order = tree_order(turn)
        self.dims = tree_bits()
        self.is_first = is_first
        self.received = None
        if len(pair) == 2:
            lower, upper = pair
            self.kept = jnp.where(is_first, lower, upper)
            self.received = swapped(jnp.where(is_first, upper, lower))
        else:
            self.kept = pair[0]

    def advance(self):
        value = self.kept
        if self.received is not None:
            value = (
                value.astype(jnp.float32) + self.received.astype(jnp.float32)
            ).astype(value.dtype)
        if self.dims and value.ndim == 2:
            count = 1 << len(self.dims)
            value = value.reshape(
                (2,) * len(self.dims) + (value.shape[0] // count, value.shape[1])
            )
        if self.order:
            bit = self.order.pop(0)
            dim = self.dims.index(bit)
            self.dims.remove(bit)
            index = my_bit(bit)
            self.received = across(
                lax.dynamic_index_in_dim(value, 1 - index, dim, keepdims=False), bit
            )
            self.kept = lax.dynamic_index_in_dim(value, index, dim, keepdims=False)
        else:
            self.kept = value
            self.received = None

    def finish(self):
        while self.received is not None or self.order:
            self.advance()
        return self.kept


def merged(chains):
    parts = [
        low(chain.kept.astype(jnp.float32) + chain.received.astype(jnp.float32))
        for chain in chains
    ]
    last = Chain(chains[0].is_first, (None,), 0)
    last.order = []
    last.dims = []
    bit = chains[0].order[0]
    index = my_bit(bit)
    last.kept = jnp.concatenate(
        [lax.dynamic_index_in_dim(part, index, 0, keepdims=False) for part in parts], axis=1
    )
    sent = [lax.dynamic_index_in_dim(part, 1 - index, 0, keepdims=False) for part in parts]
    last.received = across(jnp.concatenate(sent, axis=1), bit)
    return last


def together(main, chains):
    main, received = lax.optimization_barrier((main, [chain.received for chain in chains]))
    for chain, value in zip(chains, received):
        chain.received = value
    return main


def tick(main, chains):
    main, received = lax.optimization_barrier((main, [chain.received for chain in chains]))
    for chain, value in zip(chains, received):
        chain.received = value
        chain.advance()
    return main


def low(value):
    return value.astype(jnp.bfloat16)


def swapped(value):
    return lax.ppermute(value, "bucket", [(0, 1), (1, 0)])


def per_device(
    latent,
    condition,
    text,
    text_len,
    clip_ids,
    video_flag,
    ada_weight,
    text_kv_weight,
    qkv_weight,
    proj_weight,
    cross_q_weight,
    cross_proj_weight,
    up_weight,
    down_weight,
    temporal_qkv_weight,
    temporal_proj_weight,
    cotangent,
):
    frame_count, row_count, width = (latent.shape[1], latent.shape[2], latent.shape[3])
    total_rows = frame_count * row_count
    seq_size = lax.axis_size("seq")
    frame_size = lax.axis_size("frame")
    shards = seq_size * frame_size
    is_first = lax.axis_index("bucket") == 0
    ff_width = up_weight.shape[1]
    shard_rows = up_weight.shape[0]
    ff_blocks = ff_width // width
    half_ff = ff_width // 2

    shifts = [
        [((i + s) % seq_size, i) for i in range(seq_size)] for s in range(1, seq_size)
    ]
    latent_rest = [lax.ppermute(latent[0], "seq", shift) for shift in shifts]

    gathered_a = gather_halves(
        is_first,
        qkv_weight,
        jnp.concatenate([proj_weight, cross_q_weight, cross_proj_weight], axis=1),
    )
    up_mixed = (
        up_weight.reshape(shard_rows, shards, ff_blocks, shard_rows)
        .transpose(0, 2, 1, 3)
        .reshape(shard_rows, ff_width)
    )
    down_wide = (
        down_weight.reshape(ff_blocks, shard_rows, width)
        .transpose(1, 0, 2)
        .reshape(shard_rows, ff_width)
    )
    gathered_b = gather_halves(
        is_first,
        jnp.concatenate([up_mixed[:, :half_ff], down_wide[:, :half_ff]], axis=1),
        jnp.concatenate([up_mixed[:, half_ff:], down_wide[:, half_ff:]], axis=1),
    )

    silu_cond = jax.nn.silu(condition.astype(jnp.float32))
    mod_part = jnp.dot(silu_cond, ada_weight.astype(jnp.float32), precision=highest)
    modulation = gather_tree(mod_part).reshape(9, width)
    text_part = contract(text_kv_weight, text[0], 0, 1).astype(jnp.bfloat16)
    text_pair = gather_tree(text_part)

    inputs = latent[0].reshape(total_rows, width).astype(jnp.float32)
    normed_a, recip_a = normalize(inputs)
    hidden_a = (normed_a * (1.0 + modulation[1]) + modulation[0]).astype(jnp.bfloat16)
    normed_rest = [
        normalize(rest.reshape(total_rows, width).astype(jnp.float32))[0] for rest in latent_rest
    ]
    hidden_rest = [
        (normed * (1.0 + modulation[1]) + modulation[0]).astype(jnp.bfloat16)
        for normed in normed_rest
    ]
    hidden_all = jnp.concatenate(
        [part.reshape(frame_count, row_count, width) for part in [hidden_a] + hidden_rest], axis=1
    ).reshape(frame_count * seq_size * row_count, width)
    hidden_a, hidden_all, text_pair, gathered_a = lax.optimization_barrier(
        (hidden_a, hidden_all, text_pair, gathered_a)
    )
    query_full = gathered_a[:width, :width]
    pair_full = gathered_a[:width, width:]
    proj_full = gathered_a[width:, :width]
    cross_q_full = gathered_a[width:, width : 2 * width]
    cross_proj_full = gathered_a[width:, 2 * width :]
    query = contract(query_full, hidden_a, 0, 1).astype(jnp.bfloat16)
    key_value = contract(pair_full, hidden_all, 0, 1).astype(jnp.bfloat16)
    attended, attended_exact, log_total = spatial_forward(query, key_value, frame_count)
    branch_a = contract(attended, proj_full, 0, 0)
    after_a = inputs + modulation[2] * branch_a
    after_low = after_a.astype(jnp.bfloat16)
    cross_query = contract(cross_q_full, after_low, 0, 1).astype(jnp.bfloat16)
    cross_out = cross_forward(text_len, cross_query, text_pair)
    after_c = after_a + contract(cross_out, cross_proj_full, 0, 0)
    normed_m, recip_m = normalize(after_c)
    hidden_m = (normed_m * (1.0 + modulation[4]) + modulation[3]).astype(jnp.bfloat16)

    temporal_lower, temporal_upper = lax.optimization_barrier(
        (
            jnp.concatenate([temporal_qkv_weight[:, :width], temporal_proj_weight], axis=1),
            temporal_qkv_weight[:, width:],
            query,
        )
    )[:2]
    gathered_c = gather_halves(is_first, temporal_lower, temporal_upper)
    up_halves = (gathered_b[:width, :half_ff], gathered_b[width:, :half_ff])
    per_half = ff_blocks // 2
    down_halves = (gathered_b[:width, half_ff:ff_width], gathered_b[width:, half_ff:ff_width])
    down_parts = [
        down_halves[index // per_half][
            :, width * (index % per_half) : width * (index % per_half + 1)
        ]
        for index in range(ff_blocks)
    ]
    tquery_full = gathered_c[:width, :width]
    tproj_full = gathered_c[:width, width:]
    tpair_full = gathered_c[width:]

    upward_halves = [product(hidden_m, part) for part in up_halves]
    activated_halves = [gelu_tanh(part).astype(jnp.bfloat16) for part in upward_halves]
    activated_parts = [
        activated_halves[index // per_half][
            :, width * (index % per_half) : width * (index % per_half + 1)
        ]
        for index in range(ff_blocks)
    ]
    branch_m = sum(product(left, right) for left, right in zip(activated_parts, down_parts))
    after_m = after_c + modulation[5] * branch_m
    normed_t, recip_t = normalize(after_m)
    hidden_t = (normed_t * (1.0 + modulation[7]) + modulation[6]).astype(jnp.bfloat16)
    ahead = [(i, i + 1) for i in range(frame_size - 1)]
    back = [(i + 1, i) for i in range(frame_size - 1)]
    hidden_prev = lax.ppermute(hidden_t[total_rows - row_count :], "frame", ahead)
    hidden_next = lax.ppermute(hidden_t[:row_count], "frame", back)
    hidden_ext = jnp.concatenate([hidden_prev, hidden_t, hidden_next], axis=0)
    tquery = contract(tquery_full, hidden_t, 0, 1).astype(jnp.bfloat16)
    tpair = low(contract(tpair_full, hidden_ext, 0, 1))
    first_frame = lax.axis_index("frame") * frame_count
    clips_ext = jnp.concatenate(
        [jnp.full((1,), -1, jnp.int32), clip_ids[0], jnp.full((1,), -1, jnp.int32)]
    )
    clips_local = lax.dynamic_slice_in_dim(clips_ext, first_frame, frame_count + 2)
    live = jnp.stack(
        [clips_local[:-2] == clips_local[1:-1], clips_local[2:] == clips_local[1:-1]], axis=1
    ).astype(jnp.int32)
    flag_local = lax.dynamic_slice_in_dim(video_flag[0], first_frame, frame_count).astype(
        jnp.float32
    )
    mixed = temporal_forward(live, tquery, tpair, frame_count)
    branch_t = contract(mixed, tproj_full, 0, 0)
    flag_rows = jnp.repeat(flag_local, row_count)[:, None]
    result_rows = after_m + flag_rows * modulation[8] * branch_t
    result = result_rows.astype(jnp.bfloat16).reshape(latent.shape)

    result_grad = cotangent[0].reshape(total_rows, width).astype(jnp.float32)
    gate_t_grad = jnp.sum(flag_rows * branch_t * result_grad, axis=0)
    branch_t_grad = (flag_rows * modulation[8] * result_grad).astype(jnp.bfloat16)
    mixed_grad = contract(tproj_full, branch_t_grad, 1, 1)
    tquery_grad, tpair_grad = temporal_backward(live, tquery, tpair, mixed_grad, frame_count)
    halo_prev, halo_next, tpair_grad = lax.optimization_barrier(
        (
            low(contract(tpair_grad[:, :row_count], tpair_full, 0, 1)),
            low(contract(tpair_grad[:, -row_count:], tpair_full, 0, 1)),
            tpair_grad,
        )
    )
    to_prev = lax.ppermute(halo_prev, "frame", back)
    to_next = lax.ppermute(halo_next, "frame", ahead)
    stacked = placed(
        blank((2 * width, ff_width + 2 * width)),
        [
            (contract(hidden_t, tquery_grad, 0, 1), 0, ff_width),
            (contract(mixed, branch_t_grad, 1, 0), 0, ff_width + width),
            (contract(hidden_ext, tpair_grad, 0, 1), width, ff_width),
        ],
    )
    hidden_t_grad = contract(tpair_grad[:, row_count:-row_count], tpair_full, 0, 1) + contract(
        tquery_grad, tquery_full, 0, 1
    )
    hidden_t_grad, stacked = lax.optimization_barrier((hidden_t_grad, stacked))
    hidden_t_grad = jnp.concatenate(
        [
            hidden_t_grad[:row_count] + to_next.astype(jnp.float32),
            hidden_t_grad[row_count : total_rows - row_count],
            hidden_t_grad[total_rows - row_count :] + to_prev.astype(jnp.float32),
        ],
        axis=0,
    )
    grad_m = result_grad + normalize_back(hidden_t_grad * (1.0 + modulation[7]), normed_t, recip_t)
    gate_m_grad = jnp.sum(branch_m * grad_m, axis=0)
    branch_m_grad = low(modulation[5] * grad_m)
    upward_grads = []
    for index in range(2):
        activated_grad = jnp.concatenate(
            [
                contract(branch_m_grad, part, 1, 1)
                for part in down_parts[index * per_half : (index + 1) * per_half]
            ],
            axis=1,
        )
        gelu_back = jax.vjp(gelu_tanh, upward_halves[index])[1]
        upward_grads.append(low(gelu_back(activated_grad)[0]))
    hidden_m_grad = contract(upward_grads[0], up_halves[0], 1, 1) + contract(
        upward_grads[1], up_halves[1], 1, 1
    )
    up_grads = [contract(hidden_m, part, 0, 0) for part in upward_grads]
    down_grads = [contract(part, branch_m_grad, 0, 0) for part in activated_parts]
    stacked = placed(
        stacked,
        [(up_grads[side], side * width, 0) for side in range(2)]
        + [
            (
                down_grads[index],
                index // per_half * width,
                half_ff + index % per_half * width,
            )
            for index in range(ff_blocks)
        ],
    )
    hidden_m_grad, stacked = lax.optimization_barrier((hidden_m_grad, stacked))
    scattered = scatter_halves(stacked)
    grad_c = grad_m + normalize_back(hidden_m_grad * (1.0 + modulation[4]), normed_m, recip_m)
    cross_branch_grad = low(grad_c)
    cross_out_grad = low(contract(cross_proj_full, cross_branch_grad, 1, 1))
    cross_query_grad, text_grad = cross_backward(text_len, cross_query, text_pair, cross_out_grad)
    chain_text = Chain(is_first, (low(text_grad),), 1)
    chain_text.advance()
    grad_a = grad_c + contract(cross_query_grad, cross_q_full, 0, 1)
    gate_a_grad = jnp.sum(branch_a * grad_a, axis=0)
    branch_a_grad = low(modulation[2] * grad_a)
    attended_grad = low(contract(proj_full, branch_a_grad, 1, 1))
    attended_grad = tick(attended_grad, [chain_text])
    proj_grad = low(contract(attended, branch_a_grad, 1, 0))
    cross_q_grad = low(contract(after_low, cross_query_grad, 0, 1))
    cross_proj_grad = low(contract(cross_out, cross_branch_grad, 1, 0))
    attended_grad, proj_grad, cross_q_grad, cross_proj_grad = lax.optimization_barrier(
        (attended_grad, proj_grad, cross_q_grad, cross_proj_grad)
    )
    query_grads, pair_grads, rest_grads, rest_received = ([], [], [], [])
    for frame in range(frame_count):
        query_grad, pair_grad = spatial_backward(
            query, key_value, log_total, attended_exact, attended_grad, frame_count, frame
        )
        rest_sent = contract(pair_grad[:, row_count:], pair_full, 0, 1)
        rest_low = low(rest_sent)
        pair_grad, rest_low, attended_grad = lax.optimization_barrier(
            (pair_grad, rest_low, attended_grad)
        )
        query_grads.append(query_grad)
        pair_grads.append(pair_grad)
        rest_grads.append(rest_sent)
        rest_received.append(
            [
                lax.ppermute(
                    rest_low[s * row_count : (s + 1) * row_count],
                    "seq",
                    [(j, i) for i, j in shifts[s]],
                )
                for s in range(seq_size - 1)
            ]
        )
        if frame == 0:
            attended_grad = tick(attended_grad, [chain_text])
        else:
            query_grads, pair_grads, rest_received[frame - 1] = lax.optimization_barrier(
                (query_grads, pair_grads, rest_received[frame - 1])
            )
    query_grad = jnp.concatenate(query_grads, axis=1)
    pair_grad = jnp.concatenate(pair_grads, axis=1)
    query_weight_grad = low(contract(hidden_a, query_grad, 0, 1))
    pair_weight_grad = low(contract(hidden_all, pair_grad, 0, 1))
    query_grad, pair_grads, query_weight_grad, pair_weight_grad = lax.optimization_barrier(
        (query_grad, pair_grads, query_weight_grad, pair_weight_grad)
    )
    chains_a = [
        Chain(is_first, pair, turn)
        for turn, pair in enumerate(
            (
                (pair_weight_grad[:, width:], cross_proj_grad),
                (query_weight_grad, proj_grad),
                (pair_weight_grad[:, :width], cross_q_grad),
            )
        )
    ]
    pair_own = jnp.concatenate(
        [contract(part[:, :row_count], pair_full, 0, 1) for part in pair_grads], axis=0
    )
    pair_own = tick(pair_own, chains_a + [chain_text])
    own_grad = pair_own + contract(query_grad, query_full, 0, 1)
    shift_a_grad = jnp.sum(own_grad, axis=0)
    scale_a_grad = jnp.sum(own_grad * normed_a, axis=0)
    for frame in range(frame_count):
        for s in range(seq_size - 1):
            rest_rows = rest_grads[frame][s * row_count : (s + 1) * row_count]
            rest_normed = normed_rest[s][frame * row_count : (frame + 1) * row_count]
            shift_a_grad = shift_a_grad + jnp.sum(rest_rows, axis=0)
            scale_a_grad = scale_a_grad + jnp.sum(rest_rows * rest_normed, axis=0)
    mod_grad = jnp.stack(
        [
            shift_a_grad,
            scale_a_grad,
            gate_a_grad,
            jnp.sum(hidden_m_grad, axis=0),
            jnp.sum(hidden_m_grad * normed_m, axis=0),
            gate_m_grad,
            jnp.sum(hidden_t_grad, axis=0),
            jnp.sum(hidden_t_grad * normed_t, axis=0),
            gate_t_grad,
        ]
    ).reshape(shards, 9 * width // shards)
    own_grad, mod_grad, rest_received = together(
        (own_grad, mod_grad, rest_received), chains_a + [chain_text]
    )
    for chain in chains_a + [chain_text]:
        chain.advance()
    chain_mod = Chain(is_first, (mod_grad,), 0)
    chain_mod.advance()
    hidden_a_grad = own_grad + jnp.concatenate(
        [sum(part.astype(jnp.float32) for part in parts) for parts in rest_received], axis=0
    )
    input_grad = grad_a + normalize_back(hidden_a_grad * (1.0 + modulation[1]), normed_a, recip_a)
    latent_grad = input_grad.reshape(latent.shape)
    latent_grad = together(latent_grad, chains_a + [chain_mod])
    while len(chains_a[0].order) > 1:
        for chain in chains_a + [chain_mod]:
            chain.advance()
        latent_grad = together(latent_grad, chains_a + [chain_mod])
    chain_last = merged(chains_a)
    chain_mod.advance()
    lower_b, upper_b = whole_halves(is_first, scattered)
    up_shard = (
        jnp.concatenate([lower_b[:, :half_ff], upper_b[:, :half_ff]], axis=1)
        .reshape(shard_rows, ff_blocks, shards, shard_rows)
        .transpose(0, 2, 1, 3)
        .reshape(shard_rows, ff_width)
    )
    down_shard = jnp.concatenate(
        [
            half[:, half_ff + width * index : half_ff + width * (index + 1)]
            for half in (lower_b, upper_b)
            for index in range(per_half)
        ],
        axis=0,
    )
    latent_grad = together(latent_grad, [chain_last, chain_mod])
    mod_slice = chain_mod.finish()
    own_a = chain_last.finish()
    other_a, up_shard, down_shard = lax.optimization_barrier(
        (swapped(own_a), up_shard, down_shard)
    )
    lower_a = jnp.where(is_first, own_a, other_a).astype(jnp.float32)
    upper_a = jnp.where(is_first, other_a, own_a).astype(jnp.float32)
    text_low = chain_text.finish()
    silu_pair = jnp.concatenate([silu_cond, swapped(silu_cond)], axis=0)
    mod_pair = jnp.concatenate([mod_slice, swapped(mod_slice)], axis=0)
    ada_grad = lax.dot_general(
        silu_pair, mod_pair, (((0,), (0,)), ((), ())), precision=highest
    )
    text_both = jnp.concatenate([text[0], swapped(text[0])], axis=0)
    slice_both = jnp.concatenate([text_low, swapped(text_low)], axis=1)
    text_kv_grad = contract(text_both, slice_both, 0, 1)
    return (
        result,
        latent_grad,
        ada_grad,
        text_kv_grad,
        jnp.concatenate([lower_a[:, width : 2 * width], lower_a[:, 2 * width :], lower_a[:, :width]], axis=1),
        upper_a[:, width : 2 * width],
        upper_a[:, 2 * width :],
        upper_a[:, :width],
        up_shard,
        down_shard,
        jnp.concatenate(
            [lower_b[:, ff_width : ff_width + width], upper_b[:, ff_width:]], axis=1
        ),
        lower_b[:, ff_width + width :],
    )


def solution(mesh):
    return jax.shard_map(
        per_device,
        mesh=mesh,
        in_specs=(
            P("bucket", "frame", "seq", None),
            P("bucket", None),
            P("bucket", None, None),
            P("bucket"),
            P("bucket", None),
            P("bucket", None),
            P(None, ("frame", "seq")),
            P(None, ("frame", "seq")),
            P(("frame", "seq"), None),
            P(("frame", "seq"), None),
            P(("frame", "seq"), None),
            P(("frame", "seq"), None),
            P(("frame", "seq"), None),
            P(("frame", "seq"), None),
            P(("frame", "seq"), None),
            P(("frame", "seq"), None),
            P("bucket", "frame", "seq", None),
        ),
        out_specs=(
            P("bucket", "frame", "seq", None),
            P("bucket", "frame", "seq", None),
            P(None, ("frame", "seq")),
            P(None, ("frame", "seq")),
            P(("frame", "seq"), None),
            P(("frame", "seq"), None),
            P(("frame", "seq"), None),
            P(("frame", "seq"), None),
            P(("frame", "seq"), None),
            P(("frame", "seq"), None),
            P(("frame", "seq"), None),
            P(("frame", "seq"), None),
        ),
        check_vma=False,
    )
```

```python
import math

import jax
import jax.numpy as jnp
from jax import lax
from jax.experimental import pallas as pl
from jax.experimental.pallas import tpu as pltpu
from jax.sharding import PartitionSpec as P

HEADS = 16


epsilon = 1e-06
highest = lax.Precision.HIGHEST
masked_fill = -1e30
vmem_limit = 48 * 1024 * 1024


def product(left, right):
    return jnp.dot(left, right, preferred_element_type=jnp.float32)


def contract(left, right, left_dim, right_dim):
    return lax.dot_general(
        left, right, (((left_dim,), (right_dim,)), ((), ())), preferred_element_type=jnp.float32
    )


def call(body, grid, in_specs, out_specs, out_shape, name):
    return pl.pallas_call(
        body,
        grid=grid,
        in_specs=in_specs,
        out_specs=out_specs,
        out_shape=out_shape,
        name=name,
        compiler_params=pltpu.CompilerParams(vmem_limit_bytes=vmem_limit),
    )


def spatial_forward(query, key_value, frame_count):
    model_width, total_rows = query.shape
    head_size = model_width // HEADS
    rows = total_rows // frame_count
    keys = key_value.shape[1] // frame_count
    scale = math.log2(math.e) / math.sqrt(head_size)

    def body(q_ref, k_ref, v_ref, out_ref, exact_ref, lse_ref):
        scores = contract(k_ref[...], q_ref[...], 0, 0)
        top = jnp.max(scores, axis=0, keepdims=True) * scale
        weights = jnp.exp2(scores * scale - top)
        total = jnp.sum(weights, axis=0, keepdims=True)
        out = product(v_ref[...], weights.astype(jnp.bfloat16)) / total
        out_ref[...] = out.astype(jnp.bfloat16)
        exact_ref[...] = out
        lse_ref[0] = top + jnp.log2(total)

    return call(
        body,
        (frame_count, HEADS),
        [
            pl.BlockSpec((head_size, rows), lambda f, h: (h, f)),
            pl.BlockSpec((head_size, keys), lambda f, h: (h, f)),
            pl.BlockSpec((head_size, keys), lambda f, h: (HEADS + h, f)),
        ],
        [
            pl.BlockSpec((head_size, rows), lambda f, h: (h, f)),
            pl.BlockSpec((head_size, rows), lambda f, h: (h, f)),
            pl.BlockSpec((1, 1, rows), lambda f, h: (f * HEADS + h, 0, 0)),
        ],
        [
            jax.ShapeDtypeStruct(query.shape, jnp.bfloat16),
            jax.ShapeDtypeStruct(query.shape, jnp.float32),
            jax.ShapeDtypeStruct((frame_count * HEADS, 1, rows), jnp.float32),
        ],
        "spatial_forward",
    )(query, key_value, key_value)


def spatial_backward(query, key_value, log_total, exact, upstream, frame_count, frame):
    model_width, total_rows = query.shape
    head_size = model_width // HEADS
    rows = total_rows // frame_count
    keys = key_value.shape[1] // frame_count
    scale = 1.0 / math.sqrt(head_size)
    scale_two = math.log2(math.e) * scale

    def body(q_ref, k_ref, v_ref, lse_ref, exact_ref, up_ref, dq_ref, dkv_ref):
        query_head, key_head, up_head = (q_ref[...], k_ref[...], up_ref[...])
        probs = jnp.exp2(contract(key_head, query_head, 0, 0) * scale_two - lse_ref[0])
        dkv_ref[1] = contract(up_head, probs.astype(jnp.bfloat16), 1, 1).astype(jnp.bfloat16)
        prob_grad = contract(v_ref[...], up_head, 0, 0)
        delta = jnp.sum(up_head.astype(jnp.float32) * exact_ref[...], axis=0, keepdims=True)
        score_grad = (probs * (prob_grad - delta)).astype(jnp.bfloat16)
        dq_ref[...] = (product(key_head, score_grad) * scale).astype(jnp.bfloat16)
        dkv_ref[0] = (contract(query_head, score_grad, 1, 1) * scale).astype(jnp.bfloat16)

    query_grad, pair_grad = call(
        body,
        (HEADS,),
        [
            pl.BlockSpec((head_size, rows), lambda h: (h, frame)),
            pl.BlockSpec((head_size, keys), lambda h: (h, frame)),
            pl.BlockSpec((head_size, keys), lambda h: (HEADS + h, frame)),
            pl.BlockSpec((1, 1, rows), lambda h: (frame * HEADS + h, 0, 0)),
            pl.BlockSpec((head_size, rows), lambda h: (h, frame)),
            pl.BlockSpec((head_size, rows), lambda h: (h, frame)),
        ],
        [
            pl.BlockSpec((head_size, rows), lambda h: (h, 0)),
            pl.BlockSpec((2, head_size, keys), lambda h: (0, h, 0)),
        ],
        [
            jax.ShapeDtypeStruct((model_width, rows), jnp.bfloat16),
            jax.ShapeDtypeStruct((2, model_width, keys), jnp.bfloat16),
        ],
        "spatial_backward",
    )(query, key_value, key_value, log_total, exact, upstream)
    return (query_grad, pair_grad.reshape(2 * model_width, keys))


def cross_probs_of(length_ref, q_ref, k_ref, scale):
    scores = contract(k_ref[...], q_ref[...], 0, 0) * scale
    live = lax.broadcasted_iota(jnp.int32, scores.shape, 0) < length_ref[0]
    scores = jnp.where(live, scores, masked_fill)
    weights = jnp.exp(scores - jnp.max(scores, axis=0, keepdims=True))
    return weights / jnp.sum(weights, axis=0, keepdims=True)


def cross_forward(length, query, text_pair):
    model_width, total_rows = query.shape
    head_size = model_width // HEADS
    keys = text_pair.shape[1]
    scale = 1.0 / math.sqrt(head_size)

    def body(length_ref, q_ref, k_ref, v_ref, out_ref):
        probs = cross_probs_of(length_ref, q_ref, k_ref, scale)
        out_ref[...] = product(v_ref[...], probs.astype(jnp.bfloat16)).astype(jnp.bfloat16)

    return call(
        body,
        (HEADS,),
        [
            pl.BlockSpec(memory_space=pltpu.SMEM),
            pl.BlockSpec((head_size, total_rows), lambda h: (h, 0)),
            pl.BlockSpec((head_size, keys), lambda h: (h, 0)),
            pl.BlockSpec((head_size, keys), lambda h: (HEADS + h, 0)),
        ],
        pl.BlockSpec((head_size, total_rows), lambda h: (h, 0)),
        jax.ShapeDtypeStruct(query.shape, jnp.bfloat16),
        "cross_forward",
    )(length, query, text_pair, text_pair)


def cross_backward(length, query, text_pair, upstream):
    model_width, total_rows = query.shape
    head_size = model_width // HEADS
    keys = text_pair.shape[1]
    scale = 1.0 / math.sqrt(head_size)

    def body(length_ref, q_ref, k_ref, v_ref, up_ref, dq_ref, dkv_ref):
        up_head = up_ref[...]
        probs = cross_probs_of(length_ref, q_ref, k_ref, scale)
        prob_grad = contract(v_ref[...], up_head, 0, 0)
        delta = jnp.sum(probs * prob_grad, axis=0, keepdims=True)
        score_grad = (probs * (prob_grad - delta)).astype(jnp.bfloat16)
        dq_ref[...] = (product(k_ref[...], score_grad) * scale).astype(jnp.bfloat16)
        dkv_ref[0] = contract(q_ref[...], score_grad, 1, 1) * scale
        dkv_ref[1] = contract(up_head, probs.astype(jnp.bfloat16), 1, 1)

    query_grad, pair_grad = call(
        body,
        (HEADS,),
        [
            pl.BlockSpec(memory_space=pltpu.SMEM),
            pl.BlockSpec((head_size, total_rows), lambda h: (h, 0)),
            pl.BlockSpec((head_size, keys), lambda h: (h, 0)),
            pl.BlockSpec((head_size, keys), lambda h: (HEADS + h, 0)),
            pl.BlockSpec((head_size, total_rows), lambda h: (h, 0)),
        ],
        [
            pl.BlockSpec((head_size, total_rows), lambda h: (h, 0)),
            pl.BlockSpec((2, head_size, keys), lambda h: (0, h, 0)),
        ],
        [
            jax.ShapeDtypeStruct(query.shape, jnp.bfloat16),
            jax.ShapeDtypeStruct((2, model_width, keys), jnp.float32),
        ],
        "cross_backward",
    )(length, query, text_pair, text_pair, upstream)
    return (query_grad, pair_grad.reshape(text_pair.shape))


def temporal_probs_of(live_ref, query_frame, key_frames, frame, scale):
    scores = []
    for index in range(3):
        score = jnp.sum(query_frame * key_frames[index], axis=0, keepdims=True) * scale
        if index != 1:
            score = jnp.where(live_ref[frame, index // 2] != 0, score, masked_fill)
        scores.append(score)
    top = jnp.maximum(jnp.maximum(scores[0], scores[1]), scores[2])
    weights = [jnp.exp(score - top) for score in scores]
    inverse = 1.0 / (weights[0] + weights[1] + weights[2])
    return [weight * inverse for weight in weights]


def temporal_forward(live, query, key_value, frame_count):
    model_width, total_rows = query.shape
    head_size = model_width // HEADS
    rows = total_rows // frame_count
    extended_rows = key_value.shape[1]
    scale = 1.0 / math.sqrt(head_size)

    def body(live_ref, q_ref, k_ref, v_ref, out_ref):
        for frame in range(frame_count):
            query_frame = q_ref[:, frame * rows : (frame + 1) * rows].astype(jnp.float32)
            spans = [slice((frame + j) * rows, (frame + j + 1) * rows) for j in range(3)]
            key_frames = [k_ref[:, span].astype(jnp.float32) for span in spans]
            probs = temporal_probs_of(live_ref, query_frame, key_frames, frame, scale)
            mixed = sum(
                prob * v_ref[:, span].astype(jnp.float32) for prob, span in zip(probs, spans)
            )
            out_ref[:, frame * rows : (frame + 1) * rows] = mixed.astype(jnp.bfloat16)

    return call(
        body,
        (HEADS,),
        [
            pl.BlockSpec(memory_space=pltpu.SMEM),
            pl.BlockSpec((head_size, total_rows), lambda h: (h, 0)),
            pl.BlockSpec((head_size, extended_rows), lambda h: (h, 0)),
            pl.BlockSpec((head_size, extended_rows), lambda h: (HEADS + h, 0)),
        ],
        pl.BlockSpec((head_size, total_rows), lambda h: (h, 0)),
        jax.ShapeDtypeStruct(query.shape, jnp.bfloat16),
        "temporal_forward",
    )(live, query, key_value, key_value)


def temporal_backward(live, query, key_value, upstream, frame_count):
    model_width, total_rows = query.shape
    head_size = model_width // HEADS
    rows = total_rows // frame_count
    extended_rows = key_value.shape[1]
    scale = 1.0 / math.sqrt(head_size)

    def body(live_ref, q_ref, k_ref, v_ref, up_ref, dq_ref, dkv_ref):
        key_sums = [None] * (frame_count + 2)
        value_sums = [None] * (frame_count + 2)
        for frame in range(frame_count):
            own = slice(frame * rows, (frame + 1) * rows)
            query_frame = q_ref[:, own].astype(jnp.float32)
            up_frame = up_ref[:, own]
            spans = [slice((frame + j) * rows, (frame + j + 1) * rows) for j in range(3)]
            key_frames = [k_ref[:, span].astype(jnp.float32) for span in spans]
            probs = temporal_probs_of(live_ref, query_frame, key_frames, frame, scale)
            prob_grads = [
                jnp.sum(up_frame * v_ref[:, span].astype(jnp.float32), axis=0, keepdims=True)
                for span in spans
            ]
            delta = sum(prob * grad for prob, grad in zip(probs, prob_grads))
            score_grads = [
                prob * (grad - delta) * scale for prob, grad in zip(probs, prob_grads)
            ]
            dq_ref[:, own] = sum(
                grad * key_frame for grad, key_frame in zip(score_grads, key_frames)
            ).astype(jnp.bfloat16)
            for j in range(3):
                key_part = score_grads[j] * query_frame
                value_part = probs[j] * up_frame
                at = frame + j
                key_sums[at] = key_part if key_sums[at] is None else key_sums[at] + key_part
                value_sums[at] = (
                    value_part if value_sums[at] is None else value_sums[at] + value_part
                )
        for at in range(frame_count + 2):
            dkv_ref[0, :, at * rows : (at + 1) * rows] = key_sums[at].astype(jnp.bfloat16)
            dkv_ref[1, :, at * rows : (at + 1) * rows] = value_sums[at].astype(jnp.bfloat16)

    query_grad, pair_grad = call(
        body,
        (HEADS,),
        [
            pl.BlockSpec(memory_space=pltpu.SMEM),
            pl.BlockSpec((head_size, total_rows), lambda h: (h, 0)),
            pl.BlockSpec((head_size, extended_rows), lambda h: (h, 0)),
            pl.BlockSpec((head_size, extended_rows), lambda h: (HEADS + h, 0)),
            pl.BlockSpec((head_size, total_rows), lambda h: (h, 0)),
        ],
        [
            pl.BlockSpec((head_size, total_rows), lambda h: (h, 0)),
            pl.BlockSpec((2, head_size, extended_rows), lambda h: (0, h, 0)),
        ],
        [
            jax.ShapeDtypeStruct(query.shape, jnp.bfloat16),
            jax.ShapeDtypeStruct((2, model_width, extended_rows), jnp.bfloat16),
        ],
        "temporal_backward",
    )(live, query, key_value, key_value, upstream)
    return (query_grad, pair_grad.reshape(key_value.shape))


def normalize(values):
    centred = values - jnp.mean(values, axis=-1, keepdims=True)
    reciprocal = lax.rsqrt(jnp.mean(centred * centred, axis=-1, keepdims=True) + epsilon)
    return (centred * reciprocal, reciprocal)


def normalize_back(upstream, normed, reciprocal):
    return reciprocal * (
        upstream
        - jnp.mean(upstream, axis=-1, keepdims=True)
        - normed * jnp.mean(upstream * normed, axis=-1, keepdims=True)
    )


def gelu_tanh(values):
    return jax.nn.gelu(values, approximate=True)


def gather_halves(is_first, lower, upper):
    return lax.all_gather(
        jnp.where(is_first, lower, upper), ("bucket", "frame", "seq"), axis=0, tiled=True
    )


def tree_bits():
    return [
        (axis, step)
        for axis in ("frame", "seq")
        for step in reversed(range(lax.axis_size(axis).bit_length() - 1))
    ]


def tree_order(turn):
    bits = tree_bits()
    last = bits[0]
    first = [bit for bit in bits[::-1] if bit != last]
    turn = turn % len(first)
    return first[turn:] + first[:turn] + [last]


def blank(shape):
    return pl.pallas_call(
        lambda out_ref: None,
        out_specs=pl.BlockSpec(memory_space=pl.ANY),
        out_shape=jax.ShapeDtypeStruct(shape, jnp.bfloat16),
        name="blank",
    )()


def stack_halves(lower, upper):
    depth = lower[0].shape[0]
    stacked = blank((2 * depth, sum(part.shape[1] for part in lower)))
    for index, parts in enumerate((lower, upper)):
        column = 0
        for part in parts:
            stacked = lax.dynamic_update_slice(stacked, low(part), (index * depth, column))
            column += part.shape[1]
    return stacked


def scatter_halves(stacked):
    return lax.psum_scatter(stacked, ("bucket", "frame", "seq"), scatter_dimension=0, tiled=True)


def whole_halves(is_first, own):
    other = swapped(own)
    return (
        jnp.where(is_first, own, other).astype(jnp.float32),
        jnp.where(is_first, other, own).astype(jnp.float32),
    )


def my_bit(bit):
    return (lax.axis_index(bit[0]) >> bit[1]) & 1


def across(value, bit):
    axis, step = bit
    return lax.ppermute(
        value, axis, [(i, i ^ (1 << step)) for i in range(lax.axis_size(axis))]
    )


def gather_tree(value):
    for bit in tree_bits()[::-1]:
        other = across(value, bit)
        mine = my_bit(bit) == 0
        value = jnp.concatenate(
            [jnp.where(mine, value, other), jnp.where(mine, other, value)], axis=0
        )
    return value


class Chain:
    def __init__(self, is_first, pair, turn):
        self.order = tree_order(turn)
        self.dims = tree_bits()
        self.is_first = is_first
        self.received = None
        if len(pair) == 2:
            lower, upper = pair
            self.kept = jnp.where(is_first, lower, upper)
            self.received = swapped(jnp.where(is_first, upper, lower))
        else:
            self.kept = pair[0]

    def advance(self):
        value = self.kept
        if self.received is not None:
            value = (
                value.astype(jnp.float32) + self.received.astype(jnp.float32)
            ).astype(value.dtype)
        if self.dims and value.ndim == 2:
            count = 1 << len(self.dims)
            value = value.reshape(
                (2,) * len(self.dims) + (value.shape[0] // count, value.shape[1])
            )
        if self.order:
            bit = self.order.pop(0)
            dim = self.dims.index(bit)
            self.dims.remove(bit)
            index = my_bit(bit)
            self.received = across(
                lax.dynamic_index_in_dim(value, 1 - index, dim, keepdims=False), bit
            )
            self.kept = lax.dynamic_index_in_dim(value, index, dim, keepdims=False)
        else:
            self.kept = value
            self.received = None

    def finish(self):
        while self.received is not None or self.order:
            self.advance()
        return self.kept


def merged(chains):
    parts = [
        low(chain.kept.astype(jnp.float32) + chain.received.astype(jnp.float32))
        for chain in chains
    ]
    last = Chain(chains[0].is_first, (None,), 0)
    last.order = []
    last.dims = []
    bit = chains[0].order[0]
    index = my_bit(bit)
    last.kept = jnp.concatenate(
        [lax.dynamic_index_in_dim(part, index, 0, keepdims=False) for part in parts], axis=1
    )
    sent = [lax.dynamic_index_in_dim(part, 1 - index, 0, keepdims=False) for part in parts]
    last.received = across(jnp.concatenate(sent, axis=1), bit)
    return last


def together(main, chains):
    main, received = lax.optimization_barrier((main, [chain.received for chain in chains]))
    for chain, value in zip(chains, received):
        chain.received = value
    return main


def tick(main, chains):
    main, received = lax.optimization_barrier((main, [chain.received for chain in chains]))
    for chain, value in zip(chains, received):
        chain.received = value
        chain.advance()
    return main


def low(value):
    return value.astype(jnp.bfloat16)


def swapped(value):
    return lax.ppermute(value, "bucket", [(0, 1), (1, 0)])


def per_device(
    latent,
    condition,
    text,
    text_len,
    clip_ids,
    video_flag,
    ada_weight,
    text_kv_weight,
    qkv_weight,
    proj_weight,
    cross_q_weight,
    cross_proj_weight,
    up_weight,
    down_weight,
    temporal_qkv_weight,
    temporal_proj_weight,
    cotangent,
):
    frame_count, row_count, width = (latent.shape[1], latent.shape[2], latent.shape[3])
    total_rows = frame_count * row_count
    seq_size = lax.axis_size("seq")
    frame_size = lax.axis_size("frame")
    shards = seq_size * frame_size
    is_first = lax.axis_index("bucket") == 0
    ff_width = up_weight.shape[1]
    shard_rows = up_weight.shape[0]
    ff_blocks = ff_width // width
    half_ff = ff_width // 2

    shifts = [
        [((i + s) % seq_size, i) for i in range(seq_size)] for s in range(1, seq_size)
    ]
    latent_rest = [lax.ppermute(latent[0], "seq", shift) for shift in shifts]

    gathered_a = gather_halves(
        is_first,
        qkv_weight,
        jnp.concatenate([proj_weight, cross_q_weight, cross_proj_weight], axis=1),
    )
    up_mixed = (
        up_weight.reshape(shard_rows, shards, ff_blocks, shard_rows)
        .transpose(0, 2, 1, 3)
        .reshape(shard_rows, ff_width)
    )
    down_wide = (
        down_weight.reshape(ff_blocks, shard_rows, width)
        .transpose(1, 0, 2)
        .reshape(shard_rows, ff_width)
    )
    gathered_b = gather_halves(
        is_first,
        jnp.concatenate([up_mixed[:, :half_ff], down_wide[:, :half_ff]], axis=1),
        jnp.concatenate([up_mixed[:, half_ff:], down_wide[:, half_ff:]], axis=1),
    )

    silu_cond = jax.nn.silu(condition.astype(jnp.float32))
    mod_part = jnp.dot(silu_cond, ada_weight.astype(jnp.float32), precision=highest)
    modulation = gather_tree(mod_part).reshape(9, width)
    text_part = contract(text_kv_weight, text[0], 0, 1).astype(jnp.bfloat16)
    text_pair = gather_tree(text_part)

    inputs = latent[0].reshape(total_rows, width).astype(jnp.float32)
    normed_a, recip_a = normalize(inputs)
    hidden_a = (normed_a * (1.0 + modulation[1]) + modulation[0]).astype(jnp.bfloat16)
    normed_rest = [
        normalize(rest.reshape(total_rows, width).astype(jnp.float32))[0] for rest in latent_rest
    ]
    hidden_rest = [
        (normed * (1.0 + modulation[1]) + modulation[0]).astype(jnp.bfloat16)
        for normed in normed_rest
    ]
    hidden_all = jnp.concatenate(
        [part.reshape(frame_count, row_count, width) for part in [hidden_a] + hidden_rest], axis=1
    ).reshape(frame_count * seq_size * row_count, width)
    hidden_a, hidden_all, text_pair, gathered_a = lax.optimization_barrier(
        (hidden_a, hidden_all, text_pair, gathered_a)
    )
    query_full = gathered_a[:width, :width]
    pair_full = gathered_a[:width, width:]
    proj_full = gathered_a[width:, :width]
    cross_q_full = gathered_a[width:, width : 2 * width]
    cross_proj_full = gathered_a[width:, 2 * width :]
    query = contract(query_full, hidden_a, 0, 1).astype(jnp.bfloat16)
    key_value = contract(pair_full, hidden_all, 0, 1).astype(jnp.bfloat16)
    attended, attended_exact, log_total = spatial_forward(query, key_value, frame_count)
    branch_a = contract(attended, proj_full, 0, 0)
    after_a = inputs + modulation[2] * branch_a
    after_low = after_a.astype(jnp.bfloat16)
    cross_query = contract(cross_q_full, after_low, 0, 1).astype(jnp.bfloat16)
    cross_out = cross_forward(text_len, cross_query, text_pair)
    after_c = after_a + contract(cross_out, cross_proj_full, 0, 0)
    normed_m, recip_m = normalize(after_c)
    hidden_m = (normed_m * (1.0 + modulation[4]) + modulation[3]).astype(jnp.bfloat16)

    temporal_lower, temporal_upper = lax.optimization_barrier(
        (
            jnp.concatenate([temporal_qkv_weight[:, :width], temporal_proj_weight], axis=1),
            temporal_qkv_weight[:, width:],
            query,
        )
    )[:2]
    gathered_c = gather_halves(is_first, temporal_lower, temporal_upper)
    up_halves = (gathered_b[:width, :half_ff], gathered_b[width:, :half_ff])
    per_half = ff_blocks // 2
    down_halves = (gathered_b[:width, half_ff:ff_width], gathered_b[width:, half_ff:ff_width])
    down_parts = [
        down_halves[index // per_half][
            :, width * (index % per_half) : width * (index % per_half + 1)
        ]
        for index in range(ff_blocks)
    ]
    tquery_full = gathered_c[:width, :width]
    tproj_full = gathered_c[:width, width:]
    tpair_full = gathered_c[width:]

    upward_halves = [product(hidden_m, part) for part in up_halves]
    activated_halves = [gelu_tanh(part).astype(jnp.bfloat16) for part in upward_halves]
    activated_parts = [
        activated_halves[index // per_half][
            :, width * (index % per_half) : width * (index % per_half + 1)
        ]
        for index in range(ff_blocks)
    ]
    branch_m = sum(product(left, right) for left, right in zip(activated_parts, down_parts))
    after_m = after_c + modulation[5] * branch_m
    normed_t, recip_t = normalize(after_m)
    hidden_t = (normed_t * (1.0 + modulation[7]) + modulation[6]).astype(jnp.bfloat16)
    ahead = [(i, i + 1) for i in range(frame_size - 1)]
    back = [(i + 1, i) for i in range(frame_size - 1)]
    hidden_prev = lax.ppermute(hidden_t[total_rows - row_count :], "frame", ahead)
    hidden_next = lax.ppermute(hidden_t[:row_count], "frame", back)
    hidden_ext = jnp.concatenate([hidden_prev, hidden_t, hidden_next], axis=0)
    tquery = contract(tquery_full, hidden_t, 0, 1).astype(jnp.bfloat16)
    tpair = low(contract(tpair_full, hidden_ext, 0, 1))
    first_frame = lax.axis_index("frame") * frame_count
    clips_ext = jnp.concatenate(
        [jnp.full((1,), -1, jnp.int32), clip_ids[0], jnp.full((1,), -1, jnp.int32)]
    )
    clips_local = lax.dynamic_slice_in_dim(clips_ext, first_frame, frame_count + 2)
    live = jnp.stack(
        [clips_local[:-2] == clips_local[1:-1], clips_local[2:] == clips_local[1:-1]], axis=1
    ).astype(jnp.int32)
    flag_local = lax.dynamic_slice_in_dim(video_flag[0], first_frame, frame_count).astype(
        jnp.float32
    )
    mixed = temporal_forward(live, tquery, tpair, frame_count)
    branch_t = contract(mixed, tproj_full, 0, 0)
    flag_rows = jnp.repeat(flag_local, row_count)[:, None]
    result_rows = after_m + flag_rows * modulation[8] * branch_t
    result = result_rows.astype(jnp.bfloat16).reshape(latent.shape)

    result_grad = cotangent[0].reshape(total_rows, width).astype(jnp.float32)
    gate_t_grad = jnp.sum(flag_rows * branch_t * result_grad, axis=0)
    branch_t_grad = (flag_rows * modulation[8] * result_grad).astype(jnp.bfloat16)
    mixed_grad = contract(tproj_full, branch_t_grad, 1, 1)
    tquery_grad, tpair_grad = temporal_backward(live, tquery, tpair, mixed_grad, frame_count)
    halo_prev, halo_next, tpair_grad = lax.optimization_barrier(
        (
            low(contract(tpair_grad[:, :row_count], tpair_full, 0, 1)),
            low(contract(tpair_grad[:, -row_count:], tpair_full, 0, 1)),
            tpair_grad,
        )
    )
    to_prev = lax.ppermute(halo_prev, "frame", back)
    to_next = lax.ppermute(halo_next, "frame", ahead)
    stacked_c = stack_halves(
        [contract(hidden_t, tquery_grad, 0, 1), contract(mixed, branch_t_grad, 1, 0)],
        [contract(hidden_ext, tpair_grad, 0, 1)],
    )
    hidden_t_grad = contract(tpair_grad[:, row_count:-row_count], tpair_full, 0, 1) + contract(
        tquery_grad, tquery_full, 0, 1
    )
    hidden_t_grad, stacked_c = lax.optimization_barrier((hidden_t_grad, stacked_c))
    scattered_c = scatter_halves(stacked_c)
    hidden_t_grad = jnp.concatenate(
        [
            hidden_t_grad[:row_count] + to_next.astype(jnp.float32),
            hidden_t_grad[row_count : total_rows - row_count],
            hidden_t_grad[total_rows - row_count :] + to_prev.astype(jnp.float32),
        ],
        axis=0,
    )
    grad_m = result_grad + normalize_back(hidden_t_grad * (1.0 + modulation[7]), normed_t, recip_t)
    gate_m_grad = jnp.sum(branch_m * grad_m, axis=0)
    branch_m_grad = low(modulation[5] * grad_m)
    upward_grads = []
    for index in range(2):
        activated_grad = jnp.concatenate(
            [
                contract(branch_m_grad, part, 1, 1)
                for part in down_parts[index * per_half : (index + 1) * per_half]
            ],
            axis=1,
        )
        gelu_back = jax.vjp(gelu_tanh, upward_halves[index])[1]
        upward_grads.append(low(gelu_back(activated_grad)[0]))
    hidden_m_grad = contract(upward_grads[0], up_halves[0], 1, 1) + contract(
        upward_grads[1], up_halves[1], 1, 1
    )
    up_grads = [contract(hidden_m, part, 0, 0) for part in upward_grads]
    down_grads = [contract(part, branch_m_grad, 0, 0) for part in activated_parts]
    stacked_b = stack_halves(
        [up_grads[0]] + down_grads[:per_half], [up_grads[1]] + down_grads[per_half:]
    )
    hidden_m_grad, stacked_b = lax.optimization_barrier((hidden_m_grad, stacked_b))
    grad_c = grad_m + normalize_back(hidden_m_grad * (1.0 + modulation[4]), normed_m, recip_m)
    cross_branch_grad = low(grad_c)
    cross_out_grad = low(contract(cross_proj_full, cross_branch_grad, 1, 1))
    cross_query_grad, text_grad = cross_backward(text_len, cross_query, text_pair, cross_out_grad)
    chain_text = Chain(is_first, (low(text_grad),), 1)
    chain_text.advance()
    grad_a = grad_c + contract(cross_query_grad, cross_q_full, 0, 1)
    gate_a_grad = jnp.sum(branch_a * grad_a, axis=0)
    branch_a_grad = low(modulation[2] * grad_a)
    attended_grad = low(contract(proj_full, branch_a_grad, 1, 1))
    attended_grad, scattered_c, stacked_b = lax.optimization_barrier(
        (attended_grad, scattered_c, stacked_b)
    )
    scattered_b = scatter_halves(stacked_b)
    attended_grad = tick(attended_grad, [chain_text])
    proj_grad = low(contract(attended, branch_a_grad, 1, 0))
    cross_q_grad = low(contract(after_low, cross_query_grad, 0, 1))
    cross_proj_grad = low(contract(cross_out, cross_branch_grad, 1, 0))
    attended_grad, proj_grad, cross_q_grad, cross_proj_grad = lax.optimization_barrier(
        (attended_grad, proj_grad, cross_q_grad, cross_proj_grad)
    )
    query_grads, pair_grads, rest_grads, rest_received = ([], [], [], [])
    for frame in range(frame_count):
        query_grad, pair_grad = spatial_backward(
            query, key_value, log_total, attended_exact, attended_grad, frame_count, frame
        )
        rest_sent = contract(pair_grad[:, row_count:], pair_full, 0, 1)
        rest_low = low(rest_sent)
        pair_grad, rest_low, attended_grad = lax.optimization_barrier(
            (pair_grad, rest_low, attended_grad)
        )
        query_grads.append(query_grad)
        pair_grads.append(pair_grad)
        rest_grads.append(rest_sent)
        rest_received.append(
            [
                lax.ppermute(
                    rest_low[s * row_count : (s + 1) * row_count],
                    "seq",
                    [(j, i) for i, j in shifts[s]],
                )
                for s in range(seq_size - 1)
            ]
        )
        if frame == 0:
            attended_grad = tick(attended_grad, [chain_text])
        else:
            query_grads, pair_grads, rest_received[frame - 1] = lax.optimization_barrier(
                (query_grads, pair_grads, rest_received[frame - 1])
            )
    query_grad = jnp.concatenate(query_grads, axis=1)
    pair_grad = jnp.concatenate(pair_grads, axis=1)
    query_weight_grad = low(contract(hidden_a, query_grad, 0, 1))
    pair_weight_grad = low(contract(hidden_all, pair_grad, 0, 1))
    query_grad, pair_grads, query_weight_grad, pair_weight_grad = lax.optimization_barrier(
        (query_grad, pair_grads, query_weight_grad, pair_weight_grad)
    )
    chains_a = [
        Chain(is_first, pair, turn)
        for turn, pair in enumerate(
            (
                (pair_weight_grad[:, width:], cross_proj_grad),
                (query_weight_grad, proj_grad),
                (pair_weight_grad[:, :width], cross_q_grad),
            )
        )
    ]
    pair_own = contract(pair_grads[0][:, :row_count], pair_full, 0, 1)
    pair_own, query_grad, pair_grads = tick(
        (pair_own, query_grad, pair_grads), chains_a + [chain_text]
    )
    own_grad = jnp.concatenate(
        [pair_own]
        + [contract(part[:, :row_count], pair_full, 0, 1) for part in pair_grads[1:]],
        axis=0,
    ) + contract(query_grad, query_full, 0, 1)
    shift_a_grad = jnp.sum(own_grad, axis=0)
    scale_a_grad = jnp.sum(own_grad * normed_a, axis=0)
    for frame in range(frame_count):
        for s in range(seq_size - 1):
            rest_rows = rest_grads[frame][s * row_count : (s + 1) * row_count]
            rest_normed = normed_rest[s][frame * row_count : (frame + 1) * row_count]
            shift_a_grad = shift_a_grad + jnp.sum(rest_rows, axis=0)
            scale_a_grad = scale_a_grad + jnp.sum(rest_rows * rest_normed, axis=0)
    mod_grad = jnp.stack(
        [
            shift_a_grad,
            scale_a_grad,
            gate_a_grad,
            jnp.sum(hidden_m_grad, axis=0),
            jnp.sum(hidden_m_grad * normed_m, axis=0),
            gate_m_grad,
            jnp.sum(hidden_t_grad, axis=0),
            jnp.sum(hidden_t_grad * normed_t, axis=0),
            gate_t_grad,
        ]
    ).reshape(shards, 9 * width // shards)
    chain_mod = Chain(is_first, (mod_grad,), 0)
    chain_mod.advance()
    own_grad, rest_received = together(
        (own_grad, rest_received), chains_a + [chain_text, chain_mod]
    )
    for chain in chains_a + [chain_text, chain_mod]:
        chain.advance()
    hidden_a_grad = own_grad + jnp.concatenate(
        [sum(part.astype(jnp.float32) for part in parts) for parts in rest_received], axis=0
    )
    input_grad = grad_a + normalize_back(hidden_a_grad * (1.0 + modulation[1]), normed_a, recip_a)
    latent_grad = input_grad.reshape(latent.shape)
    latent_grad = together(latent_grad, chains_a + [chain_mod])
    while len(chains_a[0].order) > 1:
        for chain in chains_a + [chain_mod]:
            chain.advance()
        latent_grad = together(latent_grad, chains_a + [chain_mod])
    chain_last = merged(chains_a)
    chain_mod.advance()
    lower_b, upper_b = whole_halves(is_first, scattered_b)
    lower_c, upper_c = whole_halves(is_first, scattered_c)
    up_shard = (
        jnp.concatenate([lower_b[:, :half_ff], upper_b[:, :half_ff]], axis=1)
        .reshape(shard_rows, ff_blocks, shards, shard_rows)
        .transpose(0, 2, 1, 3)
        .reshape(shard_rows, ff_width)
    )
    down_shard = jnp.concatenate(
        [
            half[:, half_ff + width * index : half_ff + width * (index + 1)]
            for half in (lower_b, upper_b)
            for index in range(per_half)
        ],
        axis=0,
    )
    latent_grad = together(latent_grad, [chain_last, chain_mod])
    mod_slice = chain_mod.finish()
    own_a = chain_last.finish()
    other_a, up_shard, down_shard = lax.optimization_barrier(
        (swapped(own_a), up_shard, down_shard)
    )
    lower_a = jnp.where(is_first, own_a, other_a).astype(jnp.float32)
    upper_a = jnp.where(is_first, other_a, own_a).astype(jnp.float32)
    text_low = chain_text.finish()
    silu_pair = jnp.concatenate([silu_cond, swapped(silu_cond)], axis=0)
    mod_pair = jnp.concatenate([mod_slice, swapped(mod_slice)], axis=0)
    ada_grad = lax.dot_general(
        silu_pair, mod_pair, (((0,), (0,)), ((), ())), precision=highest
    )
    text_both = jnp.concatenate([text[0], swapped(text[0])], axis=0)
    slice_both = jnp.concatenate([text_low, swapped(text_low)], axis=1)
    text_kv_grad = contract(text_both, slice_both, 0, 1)
    return (
        result,
        latent_grad,
        ada_grad,
        text_kv_grad,
        jnp.concatenate([lower_a[:, width : 2 * width], lower_a[:, 2 * width :], lower_a[:, :width]], axis=1),
        upper_a[:, width : 2 * width],
        upper_a[:, 2 * width :],
        upper_a[:, :width],
        up_shard,
        down_shard,
        jnp.concatenate([lower_c[:, :width], upper_c], axis=1),
        lower_c[:, width:],
    )


def solution(mesh):
    return jax.shard_map(
        per_device,
        mesh=mesh,
        in_specs=(
            P("bucket", "frame", "seq", None),
            P("bucket", None),
            P("bucket", None, None),
            P("bucket"),
            P("bucket", None),
            P("bucket", None),
            P(None, ("frame", "seq")),
            P(None, ("frame", "seq")),
            P(("frame", "seq"), None),
            P(("frame", "seq"), None),
            P(("frame", "seq"), None),
            P(("frame", "seq"), None),
            P(("frame", "seq"), None),
            P(("frame", "seq"), None),
            P(("frame", "seq"), None),
            P(("frame", "seq"), None),
            P("bucket", "frame", "seq", None),
        ),
        out_specs=(
            P("bucket", "frame", "seq", None),
            P("bucket", "frame", "seq", None),
            P(None, ("frame", "seq")),
            P(None, ("frame", "seq")),
            P(("frame", "seq"), None),
            P(("frame", "seq"), None),
            P(("frame", "seq"), None),
            P(("frame", "seq"), None),
            P(("frame", "seq"), None),
            P(("frame", "seq"), None),
            P(("frame", "seq"), None),
            P(("frame", "seq"), None),
        ),
        check_vma=False,
    )
```

```python
import math

import jax
import jax.numpy as jnp
from jax import lax
from jax.experimental import pallas as pl
from jax.experimental.pallas import tpu as pltpu
from jax.sharding import PartitionSpec as P

HEADS = 16


epsilon = 1e-06
highest = lax.Precision.HIGHEST
masked_fill = -1e30
vmem_limit = 48 * 1024 * 1024


def product(left, right):
    return jnp.dot(left, right, preferred_element_type=jnp.float32)


def contract(left, right, left_dim, right_dim):
    return lax.dot_general(
        left, right, (((left_dim,), (right_dim,)), ((), ())), preferred_element_type=jnp.float32
    )


def call(body, grid, in_specs, out_specs, out_shape, name):
    return pl.pallas_call(
        body,
        grid=grid,
        in_specs=in_specs,
        out_specs=out_specs,
        out_shape=out_shape,
        name=name,
        compiler_params=pltpu.CompilerParams(vmem_limit_bytes=vmem_limit),
    )


def spatial_forward(query, key_value, frame_count):
    model_width, total_rows = query.shape
    head_size = model_width // HEADS
    rows = total_rows // frame_count
    keys = key_value.shape[1] // frame_count
    scale = math.log2(math.e) / math.sqrt(head_size)

    def body(q_ref, k_ref, v_ref, out_ref, exact_ref, lse_ref):
        scores = contract(k_ref[...], q_ref[...], 0, 0)
        top = jnp.max(scores, axis=0, keepdims=True) * scale
        weights = jnp.exp2(scores * scale - top)
        total = jnp.sum(weights, axis=0, keepdims=True)
        out = product(v_ref[...], weights.astype(jnp.bfloat16)) / total
        out_ref[...] = out.astype(jnp.bfloat16)
        exact_ref[...] = out
        lse_ref[0] = top + jnp.log2(total)

    return call(
        body,
        (frame_count, HEADS),
        [
            pl.BlockSpec((head_size, rows), lambda f, h: (h, f)),
            pl.BlockSpec((head_size, keys), lambda f, h: (h, f)),
            pl.BlockSpec((head_size, keys), lambda f, h: (HEADS + h, f)),
        ],
        [
            pl.BlockSpec((head_size, rows), lambda f, h: (h, f)),
            pl.BlockSpec((head_size, rows), lambda f, h: (h, f)),
            pl.BlockSpec((1, 1, rows), lambda f, h: (f * HEADS + h, 0, 0)),
        ],
        [
            jax.ShapeDtypeStruct(query.shape, jnp.bfloat16),
            jax.ShapeDtypeStruct(query.shape, jnp.float32),
            jax.ShapeDtypeStruct((frame_count * HEADS, 1, rows), jnp.float32),
        ],
        "spatial_forward",
    )(query, key_value, key_value)


def spatial_backward(query, key_value, log_total, exact, upstream, frame_count, frame):
    model_width, total_rows = query.shape
    head_size = model_width // HEADS
    rows = total_rows // frame_count
    keys = key_value.shape[1] // frame_count
    scale = 1.0 / math.sqrt(head_size)
    scale_two = math.log2(math.e) * scale

    def body(q_ref, k_ref, v_ref, lse_ref, exact_ref, up_ref, dq_ref, dkv_ref):
        query_head, key_head, up_head = (q_ref[...], k_ref[...], up_ref[...])
        probs = jnp.exp2(contract(key_head, query_head, 0, 0) * scale_two - lse_ref[0])
        dkv_ref[1] = contract(up_head, probs.astype(jnp.bfloat16), 1, 1).astype(jnp.bfloat16)
        prob_grad = contract(v_ref[...], up_head, 0, 0)
        delta = jnp.sum(up_head.astype(jnp.float32) * exact_ref[...], axis=0, keepdims=True)
        score_grad = (probs * (prob_grad - delta)).astype(jnp.bfloat16)
        dq_ref[...] = (product(key_head, score_grad) * scale).astype(jnp.bfloat16)
        dkv_ref[0] = (contract(query_head, score_grad, 1, 1) * scale).astype(jnp.bfloat16)

    query_grad, pair_grad = call(
        body,
        (HEADS,),
        [
            pl.BlockSpec((head_size, rows), lambda h: (h, frame)),
            pl.BlockSpec((head_size, keys), lambda h: (h, frame)),
            pl.BlockSpec((head_size, keys), lambda h: (HEADS + h, frame)),
            pl.BlockSpec((1, 1, rows), lambda h: (frame * HEADS + h, 0, 0)),
            pl.BlockSpec((head_size, rows), lambda h: (h, frame)),
            pl.BlockSpec((head_size, rows), lambda h: (h, frame)),
        ],
        [
            pl.BlockSpec((head_size, rows), lambda h: (h, 0)),
            pl.BlockSpec((2, head_size, keys), lambda h: (0, h, 0)),
        ],
        [
            jax.ShapeDtypeStruct((model_width, rows), jnp.bfloat16),
            jax.ShapeDtypeStruct((2, model_width, keys), jnp.bfloat16),
        ],
        "spatial_backward",
    )(query, key_value, key_value, log_total, exact, upstream)
    return (query_grad, pair_grad.reshape(2 * model_width, keys))


def cross_probs_of(length_ref, q_ref, k_ref, scale):
    scores = contract(k_ref[...], q_ref[...], 0, 0) * scale
    live = lax.broadcasted_iota(jnp.int32, scores.shape, 0) < length_ref[0]
    scores = jnp.where(live, scores, masked_fill)
    weights = jnp.exp(scores - jnp.max(scores, axis=0, keepdims=True))
    return weights / jnp.sum(weights, axis=0, keepdims=True)


def cross_forward(length, query, text_pair):
    model_width, total_rows = query.shape
    head_size = model_width // HEADS
    keys = text_pair.shape[1]
    scale = 1.0 / math.sqrt(head_size)

    def body(length_ref, q_ref, k_ref, v_ref, out_ref):
        probs = cross_probs_of(length_ref, q_ref, k_ref, scale)
        out_ref[...] = product(v_ref[...], probs.astype(jnp.bfloat16)).astype(jnp.bfloat16)

    return call(
        body,
        (HEADS,),
        [
            pl.BlockSpec(memory_space=pltpu.SMEM),
            pl.BlockSpec((head_size, total_rows), lambda h: (h, 0)),
            pl.BlockSpec((head_size, keys), lambda h: (h, 0)),
            pl.BlockSpec((head_size, keys), lambda h: (HEADS + h, 0)),
        ],
        pl.BlockSpec((head_size, total_rows), lambda h: (h, 0)),
        jax.ShapeDtypeStruct(query.shape, jnp.bfloat16),
        "cross_forward",
    )(length, query, text_pair, text_pair)


def cross_backward(length, query, text_pair, upstream):
    model_width, total_rows = query.shape
    head_size = model_width // HEADS
    keys = text_pair.shape[1]
    scale = 1.0 / math.sqrt(head_size)

    def body(length_ref, q_ref, k_ref, v_ref, up_ref, dq_ref, dkv_ref):
        up_head = up_ref[...]
        probs = cross_probs_of(length_ref, q_ref, k_ref, scale)
        prob_grad = contract(v_ref[...], up_head, 0, 0)
        delta = jnp.sum(probs * prob_grad, axis=0, keepdims=True)
        score_grad = (probs * (prob_grad - delta)).astype(jnp.bfloat16)
        dq_ref[...] = (product(k_ref[...], score_grad) * scale).astype(jnp.bfloat16)
        dkv_ref[0] = contract(q_ref[...], score_grad, 1, 1) * scale
        dkv_ref[1] = contract(up_head, probs.astype(jnp.bfloat16), 1, 1)

    query_grad, pair_grad = call(
        body,
        (HEADS,),
        [
            pl.BlockSpec(memory_space=pltpu.SMEM),
            pl.BlockSpec((head_size, total_rows), lambda h: (h, 0)),
            pl.BlockSpec((head_size, keys), lambda h: (h, 0)),
            pl.BlockSpec((head_size, keys), lambda h: (HEADS + h, 0)),
            pl.BlockSpec((head_size, total_rows), lambda h: (h, 0)),
        ],
        [
            pl.BlockSpec((head_size, total_rows), lambda h: (h, 0)),
            pl.BlockSpec((2, head_size, keys), lambda h: (0, h, 0)),
        ],
        [
            jax.ShapeDtypeStruct(query.shape, jnp.bfloat16),
            jax.ShapeDtypeStruct((2, model_width, keys), jnp.float32),
        ],
        "cross_backward",
    )(length, query, text_pair, text_pair, upstream)
    return (query_grad, pair_grad.reshape(text_pair.shape))


def temporal_probs_of(live_ref, query_frame, key_frames, frame, scale):
    scores = []
    for index in range(3):
        score = jnp.sum(query_frame * key_frames[index], axis=0, keepdims=True) * scale
        if index != 1:
            score = jnp.where(live_ref[frame, index // 2] != 0, score, masked_fill)
        scores.append(score)
    top = jnp.maximum(jnp.maximum(scores[0], scores[1]), scores[2])
    weights = [jnp.exp(score - top) for score in scores]
    inverse = 1.0 / (weights[0] + weights[1] + weights[2])
    return [weight * inverse for weight in weights]


def temporal_forward(live, query, key_value, frame_count):
    model_width, total_rows = query.shape
    head_size = model_width // HEADS
    rows = total_rows // frame_count
    extended_rows = key_value.shape[1]
    scale = 1.0 / math.sqrt(head_size)

    def body(live_ref, q_ref, k_ref, v_ref, out_ref):
        for frame in range(frame_count):
            query_frame = q_ref[:, frame * rows : (frame + 1) * rows].astype(jnp.float32)
            spans = [slice((frame + j) * rows, (frame + j + 1) * rows) for j in range(3)]
            key_frames = [k_ref[:, span].astype(jnp.float32) for span in spans]
            probs = temporal_probs_of(live_ref, query_frame, key_frames, frame, scale)
            mixed = sum(
                prob * v_ref[:, span].astype(jnp.float32) for prob, span in zip(probs, spans)
            )
            out_ref[:, frame * rows : (frame + 1) * rows] = mixed.astype(jnp.bfloat16)

    return call(
        body,
        (HEADS,),
        [
            pl.BlockSpec(memory_space=pltpu.SMEM),
            pl.BlockSpec((head_size, total_rows), lambda h: (h, 0)),
            pl.BlockSpec((head_size, extended_rows), lambda h: (h, 0)),
            pl.BlockSpec((head_size, extended_rows), lambda h: (HEADS + h, 0)),
        ],
        pl.BlockSpec((head_size, total_rows), lambda h: (h, 0)),
        jax.ShapeDtypeStruct(query.shape, jnp.bfloat16),
        "temporal_forward",
    )(live, query, key_value, key_value)


def temporal_backward(live, query, key_value, upstream, frame_count):
    model_width, total_rows = query.shape
    head_size = model_width // HEADS
    rows = total_rows // frame_count
    extended_rows = key_value.shape[1]
    scale = 1.0 / math.sqrt(head_size)

    def body(live_ref, q_ref, k_ref, v_ref, up_ref, dq_ref, dkv_ref):
        key_sums = [None] * (frame_count + 2)
        value_sums = [None] * (frame_count + 2)
        for frame in range(frame_count):
            own = slice(frame * rows, (frame + 1) * rows)
            query_frame = q_ref[:, own].astype(jnp.float32)
            up_frame = up_ref[:, own]
            spans = [slice((frame + j) * rows, (frame + j + 1) * rows) for j in range(3)]
            key_frames = [k_ref[:, span].astype(jnp.float32) for span in spans]
            probs = temporal_probs_of(live_ref, query_frame, key_frames, frame, scale)
            prob_grads = [
                jnp.sum(up_frame * v_ref[:, span].astype(jnp.float32), axis=0, keepdims=True)
                for span in spans
            ]
            delta = sum(prob * grad for prob, grad in zip(probs, prob_grads))
            score_grads = [
                prob * (grad - delta) * scale for prob, grad in zip(probs, prob_grads)
            ]
            dq_ref[:, own] = sum(
                grad * key_frame for grad, key_frame in zip(score_grads, key_frames)
            ).astype(jnp.bfloat16)
            for j in range(3):
                key_part = score_grads[j] * query_frame
                value_part = probs[j] * up_frame
                at = frame + j
                key_sums[at] = key_part if key_sums[at] is None else key_sums[at] + key_part
                value_sums[at] = (
                    value_part if value_sums[at] is None else value_sums[at] + value_part
                )
        for at in range(frame_count + 2):
            dkv_ref[0, :, at * rows : (at + 1) * rows] = key_sums[at].astype(jnp.bfloat16)
            dkv_ref[1, :, at * rows : (at + 1) * rows] = value_sums[at].astype(jnp.bfloat16)

    query_grad, pair_grad = call(
        body,
        (HEADS,),
        [
            pl.BlockSpec(memory_space=pltpu.SMEM),
            pl.BlockSpec((head_size, total_rows), lambda h: (h, 0)),
            pl.BlockSpec((head_size, extended_rows), lambda h: (h, 0)),
            pl.BlockSpec((head_size, extended_rows), lambda h: (HEADS + h, 0)),
            pl.BlockSpec((head_size, total_rows), lambda h: (h, 0)),
        ],
        [
            pl.BlockSpec((head_size, total_rows), lambda h: (h, 0)),
            pl.BlockSpec((2, head_size, extended_rows), lambda h: (0, h, 0)),
        ],
        [
            jax.ShapeDtypeStruct(query.shape, jnp.bfloat16),
            jax.ShapeDtypeStruct((2, model_width, extended_rows), jnp.bfloat16),
        ],
        "temporal_backward",
    )(live, query, key_value, key_value, upstream)
    return (query_grad, pair_grad.reshape(key_value.shape))


def normalize(values):
    centred = values - jnp.mean(values, axis=-1, keepdims=True)
    reciprocal = lax.rsqrt(jnp.mean(centred * centred, axis=-1, keepdims=True) + epsilon)
    return (centred * reciprocal, reciprocal)


def normalize_back(upstream, normed, reciprocal):
    return reciprocal * (
        upstream
        - jnp.mean(upstream, axis=-1, keepdims=True)
        - normed * jnp.mean(upstream * normed, axis=-1, keepdims=True)
    )


def gelu_tanh(values):
    return jax.nn.gelu(values, approximate=True)


def gather_halves(is_first, lower, upper):
    return lax.all_gather(
        jnp.where(is_first, lower, upper), ("bucket", "frame", "seq"), axis=0, tiled=True
    )


def tree_bits():
    return [
        (axis, step)
        for axis in ("frame", "seq")
        for step in reversed(range(lax.axis_size(axis).bit_length() - 1))
    ]


def tree_order(turn):
    bits = tree_bits()
    last = bits[0]
    first = [bit for bit in bits[::-1] if bit != last]
    turn = turn % len(first)
    return first[turn:] + first[:turn] + [last]


def blank(shape):
    return pl.pallas_call(
        lambda out_ref: None,
        out_specs=pl.BlockSpec(memory_space=pl.ANY),
        out_shape=jax.ShapeDtypeStruct(shape, jnp.bfloat16),
        name="blank",
    )()


def placed(stacked, parts):
    for part, row, column in parts:
        stacked = lax.dynamic_update_slice(stacked, low(part), (row, column))
    return stacked


def scatter_halves(stacked):
    return lax.psum_scatter(stacked, ("bucket", "frame", "seq"), scatter_dimension=0, tiled=True)


def whole_halves(is_first, own):
    other = swapped(own)
    return (
        jnp.where(is_first, own, other).astype(jnp.float32),
        jnp.where(is_first, other, own).astype(jnp.float32),
    )


def my_bit(bit):
    return (lax.axis_index(bit[0]) >> bit[1]) & 1


def across(value, bit):
    axis, step = bit
    return lax.ppermute(
        value, axis, [(i, i ^ (1 << step)) for i in range(lax.axis_size(axis))]
    )


def gather_tree(value):
    for bit in tree_bits()[::-1]:
        other = across(value, bit)
        mine = my_bit(bit) == 0
        value = jnp.concatenate(
            [jnp.where(mine, value, other), jnp.where(mine, other, value)], axis=0
        )
    return value


class Chain:
    def __init__(self, is_first, pair, turn):
        self.order = tree_order(turn)
        self.dims = tree_bits()
        self.is_first = is_first
        self.received = None
        if len(pair) == 2:
            lower, upper = pair
            self.kept = jnp.where(is_first, lower, upper)
            self.received = swapped(jnp.where(is_first, upper, lower))
        else:
            self.kept = pair[0]

    def advance(self):
        value = self.kept
        if self.received is not None:
            value = (
                value.astype(jnp.float32) + self.received.astype(jnp.float32)
            ).astype(value.dtype)
        if self.dims and value.ndim == 2:
            count = 1 << len(self.dims)
            value = value.reshape(
                (2,) * len(self.dims) + (value.shape[0] // count, value.shape[1])
            )
        if self.order:
            bit = self.order.pop(0)
            dim = self.dims.index(bit)
            self.dims.remove(bit)
            index = my_bit(bit)
            self.received = across(
                lax.dynamic_index_in_dim(value, 1 - index, dim, keepdims=False), bit
            )
            self.kept = lax.dynamic_index_in_dim(value, index, dim, keepdims=False)
        else:
            self.kept = value
            self.received = None

    def finish(self):
        while self.received is not None or self.order:
            self.advance()
        return self.kept


def merged(chains):
    parts = [
        low(chain.kept.astype(jnp.float32) + chain.received.astype(jnp.float32))
        for chain in chains
    ]
    last = Chain(chains[0].is_first, (None,), 0)
    last.order = []
    last.dims = []
    bit = chains[0].order[0]
    index = my_bit(bit)
    last.kept = jnp.concatenate(
        [lax.dynamic_index_in_dim(part, index, 0, keepdims=False) for part in parts], axis=1
    )
    sent = [lax.dynamic_index_in_dim(part, 1 - index, 0, keepdims=False) for part in parts]
    last.received = across(jnp.concatenate(sent, axis=1), bit)
    return last


def together(main, chains):
    main, received = lax.optimization_barrier((main, [chain.received for chain in chains]))
    for chain, value in zip(chains, received):
        chain.received = value
    return main


def tick(main, chains):
    main, received = lax.optimization_barrier((main, [chain.received for chain in chains]))
    for chain, value in zip(chains, received):
        chain.received = value
        chain.advance()
    return main


def low(value):
    return value.astype(jnp.bfloat16)


def swapped(value):
    return lax.ppermute(value, "bucket", [(0, 1), (1, 0)])


def per_device(
    latent,
    condition,
    text,
    text_len,
    clip_ids,
    video_flag,
    ada_weight,
    text_kv_weight,
    qkv_weight,
    proj_weight,
    cross_q_weight,
    cross_proj_weight,
    up_weight,
    down_weight,
    temporal_qkv_weight,
    temporal_proj_weight,
    cotangent,
):
    frame_count, row_count, width = (latent.shape[1], latent.shape[2], latent.shape[3])
    total_rows = frame_count * row_count
    seq_size = lax.axis_size("seq")
    frame_size = lax.axis_size("frame")
    shards = seq_size * frame_size
    is_first = lax.axis_index("bucket") == 0
    ff_width = up_weight.shape[1]
    shard_rows = up_weight.shape[0]
    ff_blocks = ff_width // width
    half_ff = ff_width // 2

    shifts = [
        [((i + s) % seq_size, i) for i in range(seq_size)] for s in range(1, seq_size)
    ]
    latent_rest = [lax.ppermute(latent[0], "seq", shift) for shift in shifts]

    gathered_a = gather_halves(
        is_first,
        qkv_weight,
        jnp.concatenate([proj_weight, cross_q_weight, cross_proj_weight], axis=1),
    )
    up_mixed = (
        up_weight.reshape(shard_rows, shards, ff_blocks, shard_rows)
        .transpose(0, 2, 1, 3)
        .reshape(shard_rows, ff_width)
    )
    down_wide = (
        down_weight.reshape(ff_blocks, shard_rows, width)
        .transpose(1, 0, 2)
        .reshape(shard_rows, ff_width)
    )
    gathered_b = gather_halves(
        is_first,
        jnp.concatenate([up_mixed[:, :half_ff], down_wide[:, :half_ff]], axis=1),
        jnp.concatenate([up_mixed[:, half_ff:], down_wide[:, half_ff:]], axis=1),
    )

    silu_cond = jax.nn.silu(condition.astype(jnp.float32))
    mod_part = jnp.dot(silu_cond, ada_weight.astype(jnp.float32), precision=highest)
    modulation = gather_tree(mod_part).reshape(9, width)
    text_part = contract(text_kv_weight, text[0], 0, 1).astype(jnp.bfloat16)
    text_pair = gather_tree(text_part)

    inputs = latent[0].reshape(total_rows, width).astype(jnp.float32)
    normed_a, recip_a = normalize(inputs)
    hidden_a = (normed_a * (1.0 + modulation[1]) + modulation[0]).astype(jnp.bfloat16)
    normed_rest = [
        normalize(rest.reshape(total_rows, width).astype(jnp.float32))[0] for rest in latent_rest
    ]
    hidden_rest = [
        (normed * (1.0 + modulation[1]) + modulation[0]).astype(jnp.bfloat16)
        for normed in normed_rest
    ]
    hidden_all = jnp.concatenate(
        [part.reshape(frame_count, row_count, width) for part in [hidden_a] + hidden_rest], axis=1
    ).reshape(frame_count * seq_size * row_count, width)
    hidden_a, hidden_all, text_pair, gathered_a = lax.optimization_barrier(
        (hidden_a, hidden_all, text_pair, gathered_a)
    )
    query_full = gathered_a[:width, :width]
    pair_full = gathered_a[:width, width:]
    proj_full = gathered_a[width:, :width]
    cross_q_full = gathered_a[width:, width : 2 * width]
    cross_proj_full = gathered_a[width:, 2 * width :]
    query = contract(query_full, hidden_a, 0, 1).astype(jnp.bfloat16)
    key_value = contract(pair_full, hidden_all, 0, 1).astype(jnp.bfloat16)
    attended, attended_exact, log_total = spatial_forward(query, key_value, frame_count)
    branch_a = contract(attended, proj_full, 0, 0)
    after_a = inputs + modulation[2] * branch_a
    after_low = after_a.astype(jnp.bfloat16)
    cross_query = contract(cross_q_full, after_low, 0, 1).astype(jnp.bfloat16)
    cross_out = cross_forward(text_len, cross_query, text_pair)
    after_c = after_a + contract(cross_out, cross_proj_full, 0, 0)
    normed_m, recip_m = normalize(after_c)
    hidden_m = (normed_m * (1.0 + modulation[4]) + modulation[3]).astype(jnp.bfloat16)

    temporal_lower, temporal_upper = lax.optimization_barrier(
        (
            jnp.concatenate([temporal_qkv_weight[:, :width], temporal_proj_weight], axis=1),
            temporal_qkv_weight[:, width:],
            query,
        )
    )[:2]
    gathered_c = gather_halves(is_first, temporal_lower, temporal_upper)
    up_halves = (gathered_b[:width, :half_ff], gathered_b[width:, :half_ff])
    per_half = ff_blocks // 2
    down_halves = (gathered_b[:width, half_ff:ff_width], gathered_b[width:, half_ff:ff_width])
    down_parts = [
        down_halves[index // per_half][
            :, width * (index % per_half) : width * (index % per_half + 1)
        ]
        for index in range(ff_blocks)
    ]
    tquery_full = gathered_c[:width, :width]
    tproj_full = gathered_c[:width, width:]
    tpair_full = gathered_c[width:]

    upward_halves = [product(hidden_m, part) for part in up_halves]
    activated_halves = [gelu_tanh(part).astype(jnp.bfloat16) for part in upward_halves]
    activated_parts = [
        activated_halves[index // per_half][
            :, width * (index % per_half) : width * (index % per_half + 1)
        ]
        for index in range(ff_blocks)
    ]
    branch_m = sum(product(left, right) for left, right in zip(activated_parts, down_parts))
    after_m = after_c + modulation[5] * branch_m
    normed_t, recip_t = normalize(after_m)
    hidden_t = (normed_t * (1.0 + modulation[7]) + modulation[6]).astype(jnp.bfloat16)
    ahead = [(i, i + 1) for i in range(frame_size - 1)]
    back = [(i + 1, i) for i in range(frame_size - 1)]
    hidden_prev = lax.ppermute(hidden_t[total_rows - row_count :], "frame", ahead)
    hidden_next = lax.ppermute(hidden_t[:row_count], "frame", back)
    hidden_ext = jnp.concatenate([hidden_prev, hidden_t, hidden_next], axis=0)
    tquery = contract(tquery_full, hidden_t, 0, 1).astype(jnp.bfloat16)
    tpair = low(contract(tpair_full, hidden_ext, 0, 1))
    first_frame = lax.axis_index("frame") * frame_count
    clips_ext = jnp.concatenate(
        [jnp.full((1,), -1, jnp.int32), clip_ids[0], jnp.full((1,), -1, jnp.int32)]
    )
    clips_local = lax.dynamic_slice_in_dim(clips_ext, first_frame, frame_count + 2)
    live = jnp.stack(
        [clips_local[:-2] == clips_local[1:-1], clips_local[2:] == clips_local[1:-1]], axis=1
    ).astype(jnp.int32)
    flag_local = lax.dynamic_slice_in_dim(video_flag[0], first_frame, frame_count).astype(
        jnp.float32
    )
    mixed = temporal_forward(live, tquery, tpair, frame_count)
    branch_t = contract(mixed, tproj_full, 0, 0)
    flag_rows = jnp.repeat(flag_local, row_count)[:, None]
    result_rows = after_m + flag_rows * modulation[8] * branch_t
    result = result_rows.astype(jnp.bfloat16).reshape(latent.shape)

    result_grad = cotangent[0].reshape(total_rows, width).astype(jnp.float32)
    gate_t_grad = jnp.sum(flag_rows * branch_t * result_grad, axis=0)
    branch_t_grad = (flag_rows * modulation[8] * result_grad).astype(jnp.bfloat16)
    mixed_grad = contract(tproj_full, branch_t_grad, 1, 1)
    tquery_grad, tpair_grad = temporal_backward(live, tquery, tpair, mixed_grad, frame_count)
    halo_prev, halo_next, tpair_grad = lax.optimization_barrier(
        (
            low(contract(tpair_grad[:, :row_count], tpair_full, 0, 1)),
            low(contract(tpair_grad[:, -row_count:], tpair_full, 0, 1)),
            tpair_grad,
        )
    )
    to_prev = lax.ppermute(halo_prev, "frame", back)
    to_next = lax.ppermute(halo_next, "frame", ahead)
    stacked = placed(
        blank((2 * width, ff_width + 2 * width)),
        [
            (contract(hidden_t, tquery_grad, 0, 1), 0, ff_width),
            (contract(mixed, branch_t_grad, 1, 0), 0, ff_width + width),
            (contract(hidden_ext, tpair_grad, 0, 1), width, ff_width),
        ],
    )
    hidden_t_grad = contract(tpair_grad[:, row_count:-row_count], tpair_full, 0, 1) + contract(
        tquery_grad, tquery_full, 0, 1
    )
    hidden_t_grad, stacked = lax.optimization_barrier((hidden_t_grad, stacked))
    hidden_t_grad = jnp.concatenate(
        [
            hidden_t_grad[:row_count] + to_next.astype(jnp.float32),
            hidden_t_grad[row_count : total_rows - row_count],
            hidden_t_grad[total_rows - row_count :] + to_prev.astype(jnp.float32),
        ],
        axis=0,
    )
    grad_m = result_grad + normalize_back(hidden_t_grad * (1.0 + modulation[7]), normed_t, recip_t)
    gate_m_grad = jnp.sum(branch_m * grad_m, axis=0)
    branch_m_grad = low(modulation[5] * grad_m)
    upward_grads = []
    for index in range(2):
        activated_grad = jnp.concatenate(
            [
                contract(branch_m_grad, part, 1, 1)
                for part in down_parts[index * per_half : (index + 1) * per_half]
            ],
            axis=1,
        )
        gelu_back = jax.vjp(gelu_tanh, upward_halves[index])[1]
        upward_grads.append(low(gelu_back(activated_grad)[0]))
    hidden_m_grad = contract(upward_grads[0], up_halves[0], 1, 1) + contract(
        upward_grads[1], up_halves[1], 1, 1
    )
    up_grads = [contract(hidden_m, part, 0, 0) for part in upward_grads]
    down_grads = [contract(part, branch_m_grad, 0, 0) for part in activated_parts]
    stacked = placed(
        stacked,
        [(up_grads[side], side * width, 0) for side in range(2)]
        + [
            (
                down_grads[index],
                index // per_half * width,
                half_ff + index % per_half * width,
            )
            for index in range(ff_blocks)
        ],
    )
    hidden_m_grad, stacked = lax.optimization_barrier((hidden_m_grad, stacked))
    scattered = scatter_halves(stacked)
    grad_c = grad_m + normalize_back(hidden_m_grad * (1.0 + modulation[4]), normed_m, recip_m)
    cross_branch_grad = low(grad_c)
    cross_out_grad = low(contract(cross_proj_full, cross_branch_grad, 1, 1))
    cross_query_grad, text_grad = cross_backward(text_len, cross_query, text_pair, cross_out_grad)
    chain_text = Chain(is_first, (low(text_grad),), 1)
    chain_text.advance()
    grad_a = grad_c + contract(cross_query_grad, cross_q_full, 0, 1)
    gate_a_grad = jnp.sum(branch_a * grad_a, axis=0)
    branch_a_grad = low(modulation[2] * grad_a)
    attended_grad = low(contract(proj_full, branch_a_grad, 1, 1))
    attended_grad = tick(attended_grad, [chain_text])
    proj_grad = low(contract(attended, branch_a_grad, 1, 0))
    cross_q_grad = low(contract(after_low, cross_query_grad, 0, 1))
    cross_proj_grad = low(contract(cross_out, cross_branch_grad, 1, 0))
    attended_grad, proj_grad, cross_q_grad, cross_proj_grad = lax.optimization_barrier(
        (attended_grad, proj_grad, cross_q_grad, cross_proj_grad)
    )
    query_grads, pair_grads, rest_grads, rest_received = ([], [], [], [])
    for frame in range(frame_count):
        query_grad, pair_grad = spatial_backward(
            query, key_value, log_total, attended_exact, attended_grad, frame_count, frame
        )
        rest_sent = contract(pair_grad[:, row_count:], pair_full, 0, 1)
        rest_low = low(rest_sent)
        pair_grad, rest_low, attended_grad = lax.optimization_barrier(
            (pair_grad, rest_low, attended_grad)
        )
        query_grads.append(query_grad)
        pair_grads.append(pair_grad)
        rest_grads.append(rest_sent)
        rest_received.append(
            [
                lax.ppermute(
                    rest_low[s * row_count : (s + 1) * row_count],
                    "seq",
                    [(j, i) for i, j in shifts[s]],
                )
                for s in range(seq_size - 1)
            ]
        )
        if frame == 0:
            attended_grad = tick(attended_grad, [chain_text])
        else:
            query_grads, pair_grads, rest_received[frame - 1] = lax.optimization_barrier(
                (query_grads, pair_grads, rest_received[frame - 1])
            )
    query_grad = jnp.concatenate(query_grads, axis=1)
    pair_grad = jnp.concatenate(pair_grads, axis=1)
    query_weight_grad = low(contract(hidden_a, query_grad, 0, 1))
    pair_weight_grad = low(contract(hidden_all, pair_grad, 0, 1))
    query_grad, pair_grads, query_weight_grad, pair_weight_grad = lax.optimization_barrier(
        (query_grad, pair_grads, query_weight_grad, pair_weight_grad)
    )
    chains_a = [
        Chain(is_first, pair, turn)
        for turn, pair in enumerate(
            (
                (pair_weight_grad[:, width:], cross_proj_grad),
                (query_weight_grad, proj_grad),
                (pair_weight_grad[:, :width], cross_q_grad),
            )
        )
    ]
    pair_own = jnp.concatenate(
        [contract(part[:, :row_count], pair_full, 0, 1) for part in pair_grads], axis=0
    )
    pair_own = together(tick(pair_own, [chain_text]), chains_a)
    for chain in chains_a:
        chain.kept = low(
            chain.kept.astype(jnp.float32) + chain.received.astype(jnp.float32)
        )
        chain.received = None
    own_grad = pair_own + contract(query_grad, query_full, 0, 1)
    shift_a_grad = jnp.sum(own_grad, axis=0)
    scale_a_grad = jnp.sum(own_grad * normed_a, axis=0)
    for frame in range(frame_count):
        for s in range(seq_size - 1):
            rest_rows = rest_grads[frame][s * row_count : (s + 1) * row_count]
            rest_normed = normed_rest[s][frame * row_count : (frame + 1) * row_count]
            shift_a_grad = shift_a_grad + jnp.sum(rest_rows, axis=0)
            scale_a_grad = scale_a_grad + jnp.sum(rest_rows * rest_normed, axis=0)
    mod_grad = jnp.stack(
        [
            shift_a_grad,
            scale_a_grad,
            gate_a_grad,
            jnp.sum(hidden_m_grad, axis=0),
            jnp.sum(hidden_m_grad * normed_m, axis=0),
            gate_m_grad,
            jnp.sum(hidden_t_grad, axis=0),
            jnp.sum(hidden_t_grad * normed_t, axis=0),
            gate_t_grad,
        ]
    ).reshape(shards, 9 * width // shards)
    chain_mod = Chain(is_first, (mod_grad,), 0)
    chain_mod.advance()
    own_grad, rest_received = together((own_grad, rest_received), [chain_text, chain_mod])
    chain_text.advance()
    chain_mod.advance()
    hidden_a_grad = own_grad + jnp.concatenate(
        [sum(part.astype(jnp.float32) for part in parts) for parts in rest_received], axis=0
    )
    input_grad = grad_a + normalize_back(hidden_a_grad * (1.0 + modulation[1]), normed_a, recip_a)
    latent_grad = input_grad.reshape(latent.shape)
    latent_grad, scattered, kept = together(
        (latent_grad, scattered, [chain.kept for chain in chains_a]), [chain_mod]
    )
    for chain, value in zip(chains_a, kept):
        chain.kept = value
    while len(chains_a[0].order) > 1:
        for chain in chains_a:
            chain.advance()
        if chain_mod.received is not None:
            chain_mod.advance()
        latent_grad = together(
            latent_grad,
            chains_a + ([chain_mod] if chain_mod.received is not None else []),
        )
    chain_last = merged(chains_a)
    mod_slice = chain_mod.finish()
    lower_b, upper_b = whole_halves(is_first, scattered)
    up_shard = (
        jnp.concatenate([lower_b[:, :half_ff], upper_b[:, :half_ff]], axis=1)
        .reshape(shard_rows, ff_blocks, shards, shard_rows)
        .transpose(0, 2, 1, 3)
        .reshape(shard_rows, ff_width)
    )
    down_shard = jnp.concatenate(
        [
            half[:, half_ff + width * index : half_ff + width * (index + 1)]
            for half in (lower_b, upper_b)
            for index in range(per_half)
        ],
        axis=0,
    )
    latent_grad = together(latent_grad, [chain_last])
    own_a = chain_last.finish()
    other_a, up_shard, down_shard = lax.optimization_barrier(
        (swapped(own_a), up_shard, down_shard)
    )
    lower_a = jnp.where(is_first, own_a, other_a).astype(jnp.float32)
    upper_a = jnp.where(is_first, other_a, own_a).astype(jnp.float32)
    text_low = chain_text.finish()
    silu_pair = jnp.concatenate([silu_cond, swapped(silu_cond)], axis=0)
    mod_pair = jnp.concatenate([mod_slice, swapped(mod_slice)], axis=0)
    ada_grad = lax.dot_general(
        silu_pair, mod_pair, (((0,), (0,)), ((), ())), precision=highest
    )
    text_both = jnp.concatenate([text[0], swapped(text[0])], axis=0)
    slice_both = jnp.concatenate([text_low, swapped(text_low)], axis=1)
    text_kv_grad = contract(text_both, slice_both, 0, 1)
    return (
        result,
        latent_grad,
        ada_grad,
        text_kv_grad,
        jnp.concatenate([lower_a[:, width : 2 * width], lower_a[:, 2 * width :], lower_a[:, :width]], axis=1),
        upper_a[:, width : 2 * width],
        upper_a[:, 2 * width :],
        upper_a[:, :width],
        up_shard,
        down_shard,
        jnp.concatenate(
            [lower_b[:, ff_width : ff_width + width], upper_b[:, ff_width:]], axis=1
        ),
        lower_b[:, ff_width + width :],
    )


def solution(mesh):
    return jax.shard_map(
        per_device,
        mesh=mesh,
        in_specs=(
            P("bucket", "frame", "seq", None),
            P("bucket", None),
            P("bucket", None, None),
            P("bucket"),
            P("bucket", None),
            P("bucket", None),
            P(None, ("frame", "seq")),
            P(None, ("frame", "seq")),
            P(("frame", "seq"), None),
            P(("frame", "seq"), None),
            P(("frame", "seq"), None),
            P(("frame", "seq"), None),
            P(("frame", "seq"), None),
            P(("frame", "seq"), None),
            P(("frame", "seq"), None),
            P(("frame", "seq"), None),
            P("bucket", "frame", "seq", None),
        ),
        out_specs=(
            P("bucket", "frame", "seq", None),
            P("bucket", "frame", "seq", None),
            P(None, ("frame", "seq")),
            P(None, ("frame", "seq")),
            P(("frame", "seq"), None),
            P(("frame", "seq"), None),
            P(("frame", "seq"), None),
            P(("frame", "seq"), None),
            P(("frame", "seq"), None),
            P(("frame", "seq"), None),
            P(("frame", "seq"), None),
            P(("frame", "seq"), None),
        ),
        check_vma=False,
    )
```
